32 devices in a mesh: fsdp: 4 (over x, core), seq: 8 (over z, y).
Axes of the slice: x: 2, y: 2, z: 4, core: 2. Of those that a mesh axis runs over, the one named last changes fastest.
Arguments:
- residual: bfloat16 [4, 2048, 1024], P('fsdp', 'seq'), may hold values from -6 to 6
- out_cotangent: bfloat16 [4, 2048, 1024], P('fsdp', 'seq'), may hold values from -6 to 6
- doc_lengths: int32 [4, 8], P('fsdp'), may hold values from 1 to 1024, 2048 in all within a row
- norm_gain: bfloat16 [1024], P('fsdp'), may hold values from 0.5 to 1.5
- input_proj: bfloat16 [1024, 4096], P('fsdp'), may hold values from -0.1875 to 0.1875
- conv_kernel: bfloat16 [4, 2048], P(None, 'fsdp'), may hold values from -3 to 3
- conv_bias: bfloat16 [2048], P('fsdp'), may hold values from -3 to 3
- select_proj: bfloat16 [2048, 96], P('fsdp'), may hold values from -0.125 to 0.125
- step_proj: bfloat16 [64, 2048], P(None, 'fsdp'), may hold values from -0.75 to 0.75
- step_bias: bfloat16 [2048], P('fsdp'), may hold values from -6 to -1
- log_decay: bfloat16 [16, 2048], P(None, 'fsdp'), may hold values from -2 to 2.5
- skip_gain: bfloat16 [2048], P('fsdp'), may hold values from 0.5 to 1.5
- output_proj: bfloat16 [2048, 1024], P('fsdp'), may hold values from -0.25 to 0.25
Outputs:
- layer_output: bfloat16 [4, 2048, 1024], P('fsdp', 'seq')
- residual_grad: float32 [4, 2048, 1024], P('fsdp', 'seq')
- norm_gain_grad: float32 [1024], P('fsdp')
- input_proj_grad: float32 [1024, 4096], P('fsdp')
- conv_kernel_grad: float32 [4, 2048], P(None, 'fsdp')
- conv_bias_grad: float32 [2048], P('fsdp')
- select_proj_grad: float32 [2048, 96], P('fsdp')
- step_proj_grad: float32 [64, 2048], P(None, 'fsdp')
- step_bias_grad: float32 [2048], P('fsdp')
- log_decay_grad: float32 [16, 2048], P(None, 'fsdp')
- skip_gain_grad: float32 [2048], P('fsdp')
- output_proj_grad: float32 [2048, 1024], P('fsdp')
The draws below stay inside these ranges and needn't reach their ends.
Inputs may be any that keep to these rules, and one draw needn't show every extreme that they name: `doc_lengths`: each row's 8 lengths sum to 2048, and its longest is exactly 1024.
All inputs are finite; a program needn't handle non-finite values.
Results may differ from the reference program's by a relative error of at most 0.012.
The reference program's roundings to bfloat16 on the way count: a program that leaves them out, or rounds other values in their place, can miss the bound.
Values may be sent and summed in bfloat16 or wider, within the bound.
A program may use at most 128 MiB of HBM per device.

```python
import math
import jax
import jax.numpy as jnp
import numpy as np
from jax import lax

D = 1024
INNER = 2048
STATE = 16
RANK = 64
KERNEL = 4
BLOCK = 32
DOCS = 8
ROWS = 4
SEQ_LEN = 2048


def steps_of(rng, extent, cuts, low, largest):
    factor_of, own = 1.0, jax.random.fold_in(rng, 6)
    for axis_at, blocks in cuts:
        draws = jnp.exp(jax.random.uniform(jax.random.fold_in(own, axis_at), (blocks,), jnp.float32, low / len(cuts), largest / len(cuts)))
        factor_of = factor_of * jnp.repeat(draws, extent[axis_at] // blocks).reshape([-1 if axis == axis_at else 1 for axis in range(len(extent))])
    return factor_of


def profile(amount, total, reach, skew):
    loads = [(1 << 20) // math.isqrt(rank ** skew) + 1 for rank in range(2, amount + 1)]
    rest, holding = total - reach - (amount - 1), [1] * (amount - 1)
    while rest > 0:
        movable = [i for i in range(amount - 1) if holding[i] < reach]
        mass, left = sum([loads[i] for i in movable]), rest
        for i in movable:
            extra = min(reach - holding[i], max(1, left * loads[i] // mass), rest)
            holding[i] = holding[i] + extra
            rest = rest - extra
    return np.array([reach] + holding)


def ragged_sizes(stream_key, count, total, most, slope):
    if count == 2:
        one = jax.random.randint(stream_key, (), max(1, total - most), min(most, total - 1) + 1)
        return jnp.stack([one, total - one])
    tallies = jnp.asarray(profile(count, total, most, slope), jnp.int32)
    twos = (count - 1) // 2
    giver, taker = tallies[1:1 + 2 * twos:2], tallies[2:2 + 2 * twos:2]
    room = jnp.minimum(giver - 1, most - taker)
    shifted = jax.random.randint(jax.random.fold_in(stream_key, 1), (twos,), 0, 1 << 20) % (room + 1)
    tallies = tallies.at[1:1 + 2 * twos:2].set(giver - shifted).at[2:2 + 2 * twos:2].set(taker + shifted)
    return tallies[jax.random.permutation(jax.random.fold_in(stream_key, 2), count)]


def noise(rng, extent, width, reach, cuts=(), kind=jnp.bfloat16):
    factor_of = steps_of(rng, extent, cuts, -0.22, 0.18) if cuts else 1.0
    values = jax.random.normal(rng, extent, jnp.float32) * width * factor_of
    return jnp.minimum(jnp.maximum(values, -reach), reach).astype(kind)


def setup_inputs(seed: int = 0) -> dict:
    key_of = jax.random.split(jax.random.key(seed), 14)
    residual = noise(key_of[0], (ROWS, SEQ_LEN, D), 1.0, 6.0, ((0, 4), (1, 8)))
    out_cotangent = noise(key_of[1], (ROWS, SEQ_LEN, D), 1.0, 6.0, ((0, 4), (1, 8)))
    doc_lengths = jax.vmap(lambda own: ragged_sizes(own, DOCS, SEQ_LEN, SEQ_LEN // 2, 2))(jax.random.split(key_of[2], ROWS)).reshape((ROWS, DOCS)).astype(jnp.int32)
    norm_gain = jnp.clip(1.0 + 0.1 * jax.random.normal(key_of[3], (D,), jnp.float32), 0.5, 1.5).astype(jnp.bfloat16)
    input_proj = noise(key_of[4], (D, 2 * INNER), D ** -0.5, 0.1875, ((0, 4),))
    conv_kernel = noise(key_of[5], (KERNEL, INNER), KERNEL ** -0.5, 3.0, ((1, 4),))
    conv_bias = noise(key_of[6], (INNER,), 0.5, 3.0, ((0, 4),))
    select_proj = noise(key_of[7], (INNER, RANK + 2 * STATE), INNER ** -0.5, 0.125, ((0, 4),))
    step_proj = noise(key_of[8], (RANK, INNER), RANK ** -0.5, 0.75, ((1, 4),))
    step_bias = jnp.clip(-6.0 + 5.0 * jax.random.uniform(key_of[9], (INNER,), jnp.float32) ** steps_of(key_of[9], (INNER,), ((0, 4),), -0.2, 0.2), -6.0, -1.0).astype(jnp.bfloat16)
    log_decay = jnp.clip(-2.0 + 4.5 * jax.random.uniform(key_of[10], (STATE, INNER), jnp.float32) ** steps_of(key_of[10], (STATE, INNER), ((1, 4),), -0.2, 0.2), -2.0, 2.5).astype(jnp.bfloat16)
    skip_gain = jnp.clip(0.5 + 1.0 * jax.random.uniform(key_of[11], (INNER,), jnp.float32) ** steps_of(key_of[11], (INNER,), ((0, 4),), -0.2, 0.2), 0.5, 1.5).astype(jnp.bfloat16)
    output_proj = noise(key_of[12], (INNER, D), (INNER // 4) ** -0.5, 0.25, ((0, 4),))
    return {"residual": residual, "out_cotangent": out_cotangent, "doc_lengths": doc_lengths, "norm_gain": norm_gain, "input_proj": input_proj, "conv_kernel": conv_kernel, "conv_bias": conv_bias, "select_proj": select_proj, "step_proj": step_proj, "step_bias": step_bias, "log_decay": log_decay, "skip_gain": skip_gain, "output_proj": output_proj}


EPS = 1e-05

@jax.custom_vjp
def low(v):
    return lax.optimization_barrier(v.astype(jnp.bfloat16)).astype(jnp.float32)

@jax.custom_vjp
def low_back(v):
    return v

def low_keep(v):
    return (low(v), None)

def low_pass(kept, grad):
    return (grad,)

def back_keep(v):
    return (v, None)

def back_low(kept, grad):
    return (low(grad),)
low.defvjp(low_keep, low_pass)
low_back.defvjp(back_keep, back_low)

def hi_dot(left, right):
    return jnp.dot(left, right, precision=lax.Precision.HIGHEST)

def combine_pairs(first, second):
    return (first[0] * second[0], second[0] * first[1] + second[1])

def doc_marks(lengths, first, count):
    starts = (jnp.cumsum(lengths) - lengths).astype(jnp.int32)
    place = first + jnp.arange(count, dtype=jnp.int32)
    ident = lax.optimization_barrier(jnp.sum((starts[None, :] <= place[:, None]).astype(jnp.int32), axis=1))
    begin = jnp.any(starts[None, :] == place[:, None], axis=1).astype(jnp.float32)
    return (ident, begin)

def block_step(state, item, rate):
    step_b, enter_b, read_b, mixed_b, keep_b = item
    decay = jnp.exp(step_b[:, None, :] * rate[None]) * keep_b[:, None, None]
    drive = step_b[:, None, :] * enter_b[:, :, None] * mixed_b[:, None, :]
    cum_a, cum_b = lax.associative_scan(combine_pairs, (decay, drive), axis=0)
    states = cum_a * state[None] + cum_b
    return (states[-1], lax.optimization_barrier(jnp.sum(read_b[:, :, None] * states, axis=1)))

def layer_row(row, ident, keep, params):
    gain, w_in, kernel, kbias, w_sel, w_step, sbias, logd, skip, w_out = params
    count = row.shape[0]
    scale = lax.rsqrt(lax.optimization_barrier(jnp.mean(row * row, axis=1, keepdims=True)) + EPS)
    normed = low(row * scale * gain[None, :])
    both = low_back(low(hi_dot(normed, w_in)))
    inner = both[:, :INNER]
    gate = both[:, INNER:]
    padded = jnp.concatenate([jnp.zeros((KERNEL - 1, INNER), jnp.float32), inner], axis=0)
    conv = jnp.zeros((count, INNER), jnp.float32) + kbias[None, :]
    for k in range(KERNEL):
        same = (ident[k:k + count] == ident[KERNEL - 1:]).astype(jnp.float32)
        conv = conv + kernel[k][None, :] * padded[k:k + count] * same[:, None]
    mixed = low(jax.nn.silu(conv))
    proj = low_back(hi_dot(mixed, w_sel))
    step_low = low(proj[:, :RANK])
    enter_coef = proj[:, RANK:RANK + STATE]
    read_coef = proj[:, RANK + STATE:]
    step = jax.nn.softplus(low_back(hi_dot(step_low, w_step)) + sbias[None, :])
    rate = -jnp.exp(logd)
    blocks = count // BLOCK

    def split(v):
        return v.reshape((blocks, BLOCK) + v.shape[1:])

    def run(state, item):
        return jax.checkpoint(block_step)(state, item, rate)
    final, outs = lax.scan(run, jnp.zeros((STATE, INNER), jnp.float32), (split(step), split(enter_coef), split(read_coef), split(mixed), split(keep)))
    y_full = outs.reshape(count, INNER) + skip[None, :] * mixed
    gated = low_back(low(y_full * jax.nn.silu(gate)))
    return row + hi_dot(gated, w_out)

def reference(residual, out_cotangent, doc_lengths, norm_gain, input_proj, conv_kernel, conv_bias, select_proj, step_proj, step_bias, log_decay, skip_gain, output_proj):
    count = residual.shape[1]
    ident, begin = jax.vmap(lambda lengths: doc_marks(lengths, -(KERNEL - 1), count + KERNEL - 1))(doc_lengths)
    keep = 1.0 - begin[:, KERNEL - 1:]
    params = (norm_gain.astype(jnp.float32), input_proj.astype(jnp.float32), conv_kernel.astype(jnp.float32), conv_bias.astype(jnp.float32), select_proj.astype(jnp.float32), step_proj.astype(jnp.float32), step_bias.astype(jnp.float32), log_decay.astype(jnp.float32), skip_gain.astype(jnp.float32), output_proj.astype(jnp.float32))

    def forward(rows_in, weights):
        return lax.map(lambda item: layer_row(item[0], item[1], item[2], weights), (rows_in, ident, keep))
    result, pull = jax.vjp(forward, residual.astype(jnp.float32), params)
    grad_rows, grads = pull(out_cotangent.astype(jnp.float32))
    g_gain, g_in, g_kernel, g_kbias, g_sel, g_step, g_sbias, g_logd, g_skip, g_out = grads
    return (result.astype(jnp.bfloat16), grad_rows, g_gain, g_in, g_kernel, g_kbias, g_sel, g_step, g_sbias, g_logd, g_skip, g_out)
```

```python
import functools
import math

import jax
import jax.numpy as jnp
from jax import lax
from jax.experimental import pallas as pl
from jax.experimental.pallas import tpu as pltpu
from jax.sharding import PartitionSpec as P

EPS = 1e-05
MESH = pl.DeviceIdType.MESH
LOG2E = math.log2(math.e)
LN2 = math.log(2.0)
BF16 = jnp.bfloat16
F32 = jnp.float32
ANY = pl.BlockSpec(memory_space=pl.ANY)
VMEM = pl.BlockSpec(memory_space=pltpu.VMEM)
RESET = 1e30
HALO = 16


def here():
    return lax.axis_index("fsdp"), lax.axis_index("seq")


def greet(peers):
    barrier = pltpu.get_barrier_semaphore()
    count = 0
    for ok, device in peers:
        if ok is None:
            pl.semaphore_signal(barrier, inc=1, device_id=device, device_id_type=MESH)
            count = count + 1
        else:

            @pl.when(ok)
            def _():
                pl.semaphore_signal(barrier, inc=1, device_id=device, device_id_type=MESH)

            count = count + ok.astype(jnp.int32)
    pl.semaphore_wait(barrier, count)


def remote(src, dst, send, recv, device):
    return pltpu.make_async_remote_copy(
        src_ref=src, dst_ref=dst, send_sem=send, recv_sem=recv, device_id=device, device_id_type=MESH
    )


def comm_params(cid, vmem=None):
    return pltpu.CompilerParams(collective_id=cid, has_side_effects=True, vmem_limit_bytes=vmem)


def enter_kernel(nf, ns, ch, inner, x, ct, w, sm, xg, cg, wi, wg, sg, hal, ssem, rsem, lsem):
    f, s = here()
    core = lax.bitwise_xor(f, 1)
    up, down = s + 1, s - 1
    has_up, has_down = up < ns, down >= 0
    peers = [(None, (lax.bitwise_xor(f, i), s)) for i in range(1, nf)]
    for i in range(nf):
        peers.append((has_up, (lax.bitwise_xor(f, i), up)))
        peers.append((has_down, (lax.bitwise_xor(f, i), down)))
    greet(peers)
    stretch = x.shape[1]
    tail = x.at[:, pl.ds(stretch - HALO, HALO), :]

    def cols(block, base):
        return w.at[:, pl.ds(pl.multiple_of(base + block * ch, 128), ch)]

    def make(kind, i, src, dst, device):
        return remote(src, dst, ssem.at[kind, i], rsem.at[kind, i], device)

    first, later, halos = [], [], []
    for i in range(1, nf):
        other = lax.bitwise_xor(f, i)
        device = (other, s)
        first.append(make(0, i, sm, sg.at[f], device))
        first.append(make(1, i, cols(other, 0), wi.at[f], device))
        later.append(make(2, i, cols(other, inner), wg.at[f], device))
    xcopies = [make(3, i, x, xg.at[f], (lax.bitwise_xor(f, i), s)) for i in [1] + list(range(2, nf, 2))]
    ccopies = [make(4, i, ct, cg.at[f], (lax.bitwise_xor(f, i), s)) for i in [1] + list(range(2, nf, 2))]
    for i in range(nf):
        halos.append(make(5, i, tail, hal.at[f], (lax.bitwise_xor(f, i), up)))
    for c in xcopies + first:
        c.start()

    @pl.when(has_up)
    def _():
        for c in halos:
            c.start()

    for c in ccopies + later:
        c.start()
    local = [
        pltpu.make_async_copy(x, xg.at[f], lsem.at[0]),
        pltpu.make_async_copy(ct, cg.at[f], lsem.at[1]),
        pltpu.make_async_copy(cols(f, 0), wi.at[f], lsem.at[2]),
        pltpu.make_async_copy(cols(f, inner), wg.at[f], lsem.at[3]),
        pltpu.make_async_copy(sm, sg.at[f], lsem.at[4]),
    ]
    for c in local:
        c.start()
    forwards = []
    for n, i in enumerate(range(2, nf, 2)):
        xcopies[1 + n].wait_recv()
        src = lax.bitwise_xor(f, i)
        c = make(3, i + 1, xg.at[src], xg.at[src], (core, s))
        c.start()
        forwards.append(c)
    for n, i in enumerate(range(2, nf, 2)):
        ccopies[1 + n].wait_recv()
        src = lax.bitwise_xor(f, i)
        c = make(4, i + 1, cg.at[src], cg.at[src], (core, s))
        c.start()
        forwards.append(c)
    xcopies[0].wait_recv()
    ccopies[0].wait_recv()
    for c in xcopies + ccopies:
        c.wait_send()
    for c in first + later + forwards + local:
        c.wait()

    @pl.when(has_up)
    def _():
        for c in halos:
            c.wait_send()

    @pl.when(has_down)
    def _():
        for c in halos:
            c.wait_recv()


def enter_all(nf, ns, x, ct, w, sm):
    rd, stretch, width = x.shape
    rows, both = w.shape
    inner = both // 2
    ch = inner // nf
    shape = jax.ShapeDtypeStruct
    return pl.pallas_call(
        functools.partial(enter_kernel, nf, ns, ch, inner),
        out_shape=(
            shape((nf, rd, stretch, width), BF16),
            shape((nf, rd, stretch, width), BF16),
            shape((nf, rows, ch), BF16),
            shape((nf, rows, ch), BF16),
            shape((nf, 8, 128), F32),
            shape((nf, rd, HALO, width), BF16),
        ),
        in_specs=[ANY] * 4,
        out_specs=[ANY] * 6,
        scratch_shapes=[
            pltpu.SemaphoreType.DMA((6, nf)),
            pltpu.SemaphoreType.DMA((6, nf)),
            pltpu.SemaphoreType.DMA((5,)),
        ],
        compiler_params=comm_params(0),
        name="enter_all",
    )(x, ct, w, sm)


def total_kernel(nf, part, out, got, mid, far, ssem, rsem):
    f, s = here()
    c = lax.rem(f, 2)
    half = part.shape[0] // 2
    core = (lax.bitwise_xor(f, 1), s)
    chips = list(range(2, nf, 2))
    greet([(None, core)] + [(None, (lax.bitwise_xor(f, i), s)) for i in chips])
    mine = pl.ds(pl.multiple_of(c * half, 8), half)
    other = pl.ds(pl.multiple_of((1 - c) * half, 8), half)
    one = remote(part.at[other], got, ssem.at[0], rsem.at[0], core)
    one.start()
    one.wait()
    mid[...] = part[mine, :] + got[...]
    two = []
    for n, i in enumerate(chips):
        cp = remote(mid, far.at[n], ssem.at[1 + n], rsem.at[1 + n], (lax.bitwise_xor(f, i), s))
        cp.start()
        two.append(cp)
    for cp in two:
        cp.wait()
    acc = mid[...]
    for n in range(len(chips)):
        acc = acc + far[n]
    out[mine, :] = acc
    last = len(chips) + 1
    three = remote(out.at[mine], out.at[mine], ssem.at[last], rsem.at[last], core)
    three.start()
    three.wait()


def total_over_fsdp(nf, cid, part):
    tokens, lanes = part.shape
    chips = nf // 2 - 1
    return pl.pallas_call(
        functools.partial(total_kernel, nf),
        out_shape=jax.ShapeDtypeStruct(part.shape, F32),
        in_specs=[VMEM],
        out_specs=VMEM,
        scratch_shapes=[
            pltpu.VMEM((tokens // 2, lanes), F32),
            pltpu.VMEM((tokens // 2, lanes), F32),
            pltpu.VMEM((chips, tokens // 2, lanes), F32),
            pltpu.SemaphoreType.DMA((chips + 2,)),
            pltpu.SemaphoreType.DMA((chips + 2,)),
        ],
        compiler_params=comm_params(cid, 40 << 20),
        name="total_over_fsdp",
    )(part)


def share_kernel(nf, part, out, got, mid, far, ssem, rsem):
    f, s = here()
    c = lax.rem(f, 2)
    core = (lax.bitwise_xor(f, 1), s)
    chips = list(range(2, nf, 2))
    greet([(None, core)] + [(None, (lax.bitwise_xor(f, i), s)) for i in chips])
    near = []
    for n, i in enumerate([0] + chips):
        dest = lax.bitwise_xor(lax.bitwise_xor(f, 1), i)
        cp = remote(part.at[dest], got.at[n], ssem.at[n], rsem.at[n], core)
        cp.start()
        near.append(cp)
    two = []
    for n, i in list(enumerate([0] + chips))[::-1]:
        near[n].wait()
        dest = lax.bitwise_xor(f, i)
        both = part[dest].astype(F32) + got[n].astype(F32)
        if i == 0:
            acc = both
        else:
            mid[n - 1] = both.astype(BF16)
            k = len(chips) + n
            cp = remote(mid.at[n - 1], far.at[n - 1], ssem.at[k], rsem.at[k], (dest, s))
            cp.start()
            two.append(cp)
    for cp in two:
        cp.wait()
    for n in range(len(chips)):
        acc = acc + far[n].astype(F32)
    out[...] = acc


def share_over_fsdp(nf, cid, part):
    block = part.shape[1:]
    chips = nf // 2 - 1
    return pl.pallas_call(
        functools.partial(share_kernel, nf),
        out_shape=jax.ShapeDtypeStruct(block, F32),
        in_specs=[VMEM],
        out_specs=VMEM,
        scratch_shapes=[
            pltpu.VMEM((chips + 1,) + block, BF16),
            pltpu.VMEM((chips,) + block, BF16),
            pltpu.VMEM((chips,) + block, BF16),
            pltpu.SemaphoreType.DMA((2 * chips + 1,)),
            pltpu.SemaphoreType.DMA((2 * chips + 1,)),
        ],
        compiler_params=comm_params(cid, 48 << 20),
        name="share_over_fsdp",
    )(part)


def swap_kernel(nf, part, out, ssem, rsem, lsem):
    f, s = here()
    greet([(None, (lax.bitwise_xor(f, i), s)) for i in range(1, nf)])
    copies = []
    for i in range(1, nf):
        other = lax.bitwise_xor(f, i)
        copies.append(remote(part.at[other], out.at[f], ssem.at[i], rsem.at[i], (other, s)))
    for cp in copies:
        cp.start()
    own = pltpu.make_async_copy(part.at[f], out.at[f], lsem)
    own.start()
    for cp in copies + [own]:
        cp.wait()


def swap_over_fsdp(nf, cid, part):
    return pl.pallas_call(
        functools.partial(swap_kernel, nf),
        out_shape=jax.ShapeDtypeStruct(part.shape, part.dtype),
        in_specs=[ANY],
        out_specs=ANY,
        scratch_shapes=[
            pltpu.SemaphoreType.DMA((nf,)),
            pltpu.SemaphoreType.DMA((nf,)),
            pltpu.SemaphoreType.DMA,
        ],
        compiler_params=comm_params(cid),
        name="swap_over_fsdp",
    )(part)


def carry_kernel(reach, ns, b, g, t, bf, gb, tf, tb, ssem, rsem):
    f, s = here()
    peers = []
    for j in range(1, reach + 1):
        peers.append((s + j < ns, (f, s + j)))
        peers.append((s - j >= 0, (f, s - j)))
    greet(peers)

    def copies(j):
        ahead, back = (f, s + j), (f, s - j)
        k = j - 1
        fwd = [
            remote(b, bf.at[k], ssem.at[0, k], rsem.at[0, k], ahead),
            remote(t, tf.at[k], ssem.at[1, k], rsem.at[1, k], ahead),
        ]
        bwd = [
            remote(g, gb.at[k], ssem.at[2, k], rsem.at[2, k], back),
            remote(t, tb.at[k], ssem.at[3, k], rsem.at[3, k], back),
        ]
        return fwd, bwd

    every = [copies(j) for j in range(1, reach + 1)]
    for j in range(1, reach + 1):
        fwd, bwd = every[j - 1]

        @pl.when(s + j < ns)
        def _():
            for cp in fwd:
                cp.start()

        @pl.when(s - j >= 0)
        def _():
            for cp in bwd:
                cp.start()

    for j in range(1, reach + 1):
        fwd, bwd = every[j - 1]

        @pl.when(s + j < ns)
        def _():
            for cp in fwd:
                cp.wait_send()
            for cp in bwd:
                cp.wait_recv()

        @pl.when(s - j >= 0)
        def _():
            for cp in bwd:
                cp.wait_send()
            for cp in fwd:
                cp.wait_recv()


def carry_over_seq(reach, ns, cid, b, g, t):
    shape = jax.ShapeDtypeStruct
    return pl.pallas_call(
        functools.partial(carry_kernel, reach, ns),
        out_shape=(
            shape((reach,) + b.shape, b.dtype),
            shape((reach,) + g.shape, g.dtype),
            shape((reach,) + t.shape, t.dtype),
            shape((reach,) + t.shape, t.dtype),
        ),
        in_specs=[VMEM] * 3,
        out_specs=[VMEM] * 4,
        scratch_shapes=[
            pltpu.SemaphoreType.DMA((4, reach)),
            pltpu.SemaphoreType.DMA((4, reach)),
        ],
        compiler_params=comm_params(cid, 32 << 20),
        name="carry_over_seq",
    )(b, g, t)


def back_kernel(ns, e, out, ssem, rsem):
    f, s = here()
    greet([(s + 1 < ns, (f, s + 1)), (s >= 1, (f, s - 1))])
    cp = remote(e, out, ssem, rsem, (f, s - 1))

    @pl.when(s >= 1)
    def _():
        cp.start()
        cp.wait_send()

    @pl.when(s + 1 < ns)
    def _():
        cp.wait_recv()


def back_over_seq(ns, cid, e):
    return pl.pallas_call(
        functools.partial(back_kernel, ns),
        out_shape=jax.ShapeDtypeStruct(e.shape, e.dtype),
        in_specs=[VMEM],
        out_specs=VMEM,
        scratch_shapes=[pltpu.SemaphoreType.DMA, pltpu.SemaphoreType.DMA],
        compiler_params=comm_params(cid),
        name="back_over_seq",
    )(e)


BLOCK_TOKENS = 1024


def at(t):
    return pl.ds(pl.multiple_of(t * 8, 8), 8)


def cut(d):
    return slice(d * 128, (d + 1) * 128)


def pieces(v, count):
    out = []
    for _ in range(count):
        top = v.astype(BF16)
        out.append(top)
        v = v - top.astype(F32)
    return out


def coef_pieces(proj, rank, nstate):
    parts = pieces(proj[:, rank : rank + 2 * nstate], 3)
    return jnp.pad(jnp.concatenate(parts, axis=1), ((0, 0), (0, 128 - 6 * nstate)))


def spread_coefs(packed, cscr, first, count, nstate):
    wide = 2 * count * 128
    source = lax.broadcasted_iota(jnp.int32, (128, wide), 0)
    block = lax.broadcasted_iota(jnp.int32, (128, wide), 1) // 128
    want = jnp.where(block < count, block, nstate - count + block) + first
    pick = jnp.where(
        jnp.logical_and(source % (2 * nstate) == want, source < 6 * nstate), 1.0, 0.0
    ).astype(BF16)
    cscr[...] = jnp.dot(packed[...], pick, preferred_element_type=F32)


ENDS_UNROLL = 4
SCAN_UNROLL = 4


def ends_kernel(count, groups, rank, nstate, step, u, dy, proj, rate, b, p, g, cscr):
    j = pl.program_id(2)
    steps = step.shape[0] // 8
    spread_coefs(proj, cscr, j * count, count, nstate)
    keys = [(d, i) for d in range(groups) for i in range(count)]
    rates = [jnp.broadcast_to(rate[0, i : i + 1, cut(d)], (8, 128)) for d, i in keys]

    def one(t, carry):
        bs, ps, gs = carry
        nb, np_, ng = [], [], []
        enter = [cscr[at(t), cut(i)] for i in range(count)]
        read = [cscr[at(t), cut(count + i)] for i in range(count)]
        for d in range(groups):
            st, ut, dt = step[at(t), cut(d)], u[at(t), cut(d)], dy[at(t), cut(d)]
            for i in range(count):
                k = d * count + i
                a = jnp.exp2(st * rates[k])
                prod = ps[k] * a
                nb.append(bs[k] * a + enter[i] * ut)
                np_.append(prod)
                ng.append(gs[k] + prod * (read[i] * dt))
        return tuple(nb), tuple(np_), tuple(ng)

    size = count * groups
    zero = jnp.zeros((8, 128), F32)
    init = ((zero,) * size, (zero + 1.0,) * size, (zero,) * size)
    bs, ps, gs = lax.fori_loop(0, steps, one, init, unroll=ENDS_UNROLL)
    for k, (d, i) in enumerate(keys):
        b[0, i, :, cut(d)] = bs[k]
        p[0, i, :, cut(d)] = ps[k]
        g[0, i, :, cut(d)] = gs[k]


def scan_ends(step, u, dy, proj, rate, rank, count):
    tokens, ch = step.shape
    nstate = rate.shape[0]
    blocks = tokens // BLOCK_TOKENS
    width = min(ch, 512)
    groups = width // 128
    tok = pl.BlockSpec((BLOCK_TOKENS, width), lambda n, c, j: (n, c))
    state = pl.BlockSpec((1, count, 8, width), lambda n, c, j: (n, j, 0, c))
    shape = jax.ShapeDtypeStruct((blocks, nstate, 8, ch), F32)
    return pl.pallas_call(
        functools.partial(ends_kernel, count, groups, rank, nstate),
        out_shape=(shape,) * 3,
        grid=(blocks, ch // width, nstate // count),
        in_specs=[
            tok,
            tok,
            tok,
            pl.BlockSpec((BLOCK_TOKENS, 128), lambda n, c, j: (n, 0)),
            pl.BlockSpec((1, count, width), lambda n, c, j: (j, 0, c)),
        ],
        out_specs=[state] * 3,
        scratch_shapes=[pltpu.VMEM((BLOCK_TOKENS, 2 * count * 128), F32)],
        compiler_params=pltpu.CompilerParams(vmem_limit_bytes=32 << 20),
        cost_estimate=pl.CostEstimate(
            flops=8 * tokens * nstate * ch, bytes_accessed=12 * tokens * ch, transcendentals=tokens * nstate * ch
        ),
        name="scan_ends",
    )(step, u, dy, proj, rate.reshape(nstate // count, count, ch))


def scan_kernel(
    count, groups, rank, nstate, step, u, dy, proj, rate, hin, lin, y, pulled, gs, coef, tot, ascr, hscr, cscr, seen_scr
):
    c, j = pl.program_id(1), pl.program_id(2)
    steps = step.shape[0] // 8
    size = count * groups
    keys = [(d, i) for d in range(groups) for i in range(count)]
    rates = [jnp.broadcast_to(rate[0, i : i + 1, cut(d)], (8, 128)) for d, i in keys]
    spread_coefs(proj, cscr, j * count, count, nstate)

    @pl.when(j == 0)
    def _():
        y[...] = jnp.zeros_like(y)
        pulled[...] = jnp.zeros_like(pulled)
        gs[...] = jnp.zeros_like(gs)

    @pl.when(jnp.logical_and(j == 0, c == 0))
    def _():
        coef[...] = jnp.zeros_like(coef)

    def forward(t, state):
        enter = [cscr[at(t), cut(i)] for i in range(count)]
        read = [cscr[at(t), cut(count + i)] for i in range(count)]
        new = []
        seen = [None] * count
        for d in range(groups):
            st, ut, dt = step[at(t), cut(d)], u[at(t), cut(d)], dy[at(t), cut(d)]
            out = None
            for i in range(count):
                k = d * count + i
                a = jnp.exp2(st * rates[k])
                ascr[t, k] = a
                hscr[t, k] = state[k]
                h = state[k] * a + enter[i] * ut
                new.append(h)
                out = read[i] * h if out is None else out + read[i] * h
                term = h * dt
                seen[i] = term if seen[i] is None else seen[i] + term
            y[at(t), cut(d)] += out
        for i in range(count):
            seen_scr[at(t), cut(count + i)] = seen[i]
        return tuple(new)

    lax.fori_loop(0, steps, forward, tuple(hin[0, i, :, cut(d)] for d, i in keys), unroll=SCAN_UNROLL)

    def backward(k0, carry):
        t = steps - 1 - k0
        passed, sums = carry
        enter = [cscr[at(t), cut(i)] for i in range(count)]
        read = [cscr[at(t), cut(count + i)] for i in range(count)]
        new, news = [], []
        seen = [None] * count
        for d in range(groups):
            st, ut, dt = step[at(t), cut(d)], u[at(t), cut(d)], dy[at(t), cut(d)]
            pull, slope_sum = None, None
            for i in range(count):
                k = d * count + i
                adj = passed[k] + read[i] * dt
                pull = adj * enter[i] if pull is None else pull + adj * enter[i]
                back = adj * ascr[t, k]
                slope = back * hscr[t, k]
                slope_sum = slope * rates[k] if slope_sum is None else slope_sum + slope * rates[k]
                new.append(back)
                news.append(sums[k] + slope * st)
                term = adj * ut
                seen[i] = term if seen[i] is None else seen[i] + term
            pulled[at(t), cut(d)] += pull
            gs[at(t), cut(d)] += slope_sum
        for i in range(count):
            seen_scr[at(t), cut(i)] = seen[i]
        return tuple(new), tuple(news)

    zero = jnp.zeros((8, 128), F32)
    init = (tuple(lin[0, i, :, cut(d)] for d, i in keys), (zero,) * size)
    passed, sums = lax.fori_loop(0, steps, backward, init, unroll=SCAN_UNROLL)
    for n, (d, i) in enumerate(keys):
        tot[0, i, :, cut(d)] = sums[n]

    wide = 2 * count * 128
    block = lax.broadcasted_iota(jnp.int32, (wide, 128), 0) // 128
    column = lax.broadcasted_iota(jnp.int32, (wide, 128), 1)
    want = jnp.where(block < count, block, nstate - count + block) + j * count + rank
    ones = jnp.where(column == want, 1.0, 0.0).astype(BF16)
    for part in pieces(seen_scr[...], 2):
        coef[...] += jnp.dot(part, ones, preferred_element_type=F32)


def scan_all(step, u, dy, proj, rate, hin, lin, rank, count):
    tokens, ch = step.shape
    nstate = rate.shape[0]
    blocks = tokens // BLOCK_TOKENS
    width = min(ch, 512)
    groups = width // 128
    steps = BLOCK_TOKENS // 8
    tok = pl.BlockSpec((BLOCK_TOKENS, width), lambda n, c, j: (n, c))
    narrow = pl.BlockSpec((BLOCK_TOKENS, 128), lambda n, c, j: (n, 0))
    state = pl.BlockSpec((1, count, 8, width), lambda n, c, j: (n, j, 0, c))
    shape = jax.ShapeDtypeStruct
    return pl.pallas_call(
        functools.partial(scan_kernel, count, groups, rank, nstate),
        out_shape=(
            shape((tokens, ch), F32),
            shape((tokens, ch), F32),
            shape((tokens, ch), F32),
            shape((tokens, 128), F32),
            shape((blocks, nstate, 8, ch), F32),
        ),
        grid=(blocks, ch // width, nstate // count),
        in_specs=[
            tok,
            tok,
            tok,
            narrow,
            pl.BlockSpec((1, count, width), lambda n, c, j: (j, 0, c)),
            state,
            state,
        ],
        out_specs=[tok, tok, tok, narrow, state],
        scratch_shapes=[
            pltpu.VMEM((steps, count * groups, 8, 128), F32),
            pltpu.VMEM((steps, count * groups, 8, 128), F32),
            pltpu.VMEM((BLOCK_TOKENS, 2 * count * 128), F32),
            pltpu.VMEM((BLOCK_TOKENS, 2 * count * 128), F32),
        ],
        compiler_params=pltpu.CompilerParams(vmem_limit_bytes=60 << 20),
        cost_estimate=pl.CostEstimate(
            flops=20 * tokens * nstate * ch, bytes_accessed=24 * tokens * ch, transcendentals=tokens * nstate * ch
        ),
        name="scan_all",
    )(step, u, dy, proj, rate.reshape(nstate // count, count, ch), hin, lin)


def rows_inner(left, right):
    return lax.dot_general(left, right, (((0,), (0,)), ((), ())), preferred_element_type=F32)


def times_transposed(left, right):
    return lax.dot_general(left, right, (((1,), (1,)), ((), ())), preferred_element_type=F32)


def silu_slope(value):
    sig = jax.nn.sigmoid(value)
    return sig * (1.0 + value * (1.0 - sig))


def shards(
    nf,
    ns,
    residual,
    out_cotangent,
    doc_lengths,
    norm_gain,
    input_proj,
    conv_kernel,
    conv_bias,
    select_proj,
    step_proj,
    step_bias,
    log_decay,
    skip_gain,
    output_proj,
):
    rd, stretch, width = residual.shape
    rows = nf * rd
    docs = doc_lengths.shape[1]
    ch = conv_bias.shape[0]
    rank = step_proj.shape[0]
    nstate = log_decay.shape[0]
    taps = conv_kernel.shape[0]
    edge = taps - 1
    tokens = rows * stretch
    half = stretch // 2
    blocks = rows // 4
    f, s = here()
    reach = -(-(stretch * ns // 2 - 1) // stretch)
    count = 4

    small = jnp.zeros((8, 128), F32)
    small = small.at[:rd, :docs].set(doc_lengths.astype(F32))
    grows = norm_gain.shape[0]
    gl = min(grows, 128)
    small = small.at[4 : 4 + grows // gl, :gl].set(norm_gain.astype(F32).reshape(-1, gl))
    xg, cg, wi, wg, sg, hal = enter_all(nf, ns, residual, out_cotangent, input_proj, small)
    lengths = sg[:, :rd, :docs].reshape(rows, docs).astype(jnp.int32)
    gain = sg[:, 4 : 4 + grows // gl, :gl].reshape(1, width)
    w_inner = wi.reshape(width, ch)
    w_gate = wg.reshape(width, ch)

    def to_tokens(v):
        v = v.reshape((blocks, 4, 2, half) + v.shape[2:])
        return jnp.moveaxis(v, 3, 1).reshape((tokens,) + v.shape[4:])

    def from_tokens(v):
        v = v.reshape((blocks, half, 4, 2) + v.shape[1:])
        return jnp.moveaxis(v, 1, 3).reshape((rows, stretch) + v.shape[4:])

    def stacked(v):
        return v.reshape((blocks, half, 8) + v.shape[1:])

    def norm(v):
        v = v.astype(F32)
        scale = lax.rsqrt(jnp.mean(v * v, axis=-1, keepdims=True) + EPS)
        return (v * scale * gain).astype(BF16)

    normed = norm(to_tokens(xg.reshape(rows, stretch, width)))
    cot = to_tokens(cg.reshape(rows, stretch, width))
    before = jnp.where(s > 0, hal.reshape(rows * HALO, width), 0)

    starts = jnp.cumsum(lengths, axis=1) - lengths
    place = s * stretch - edge + jnp.arange(stretch + edge, dtype=jnp.int32)
    ident = jnp.sum((starts[:, None, :] <= place[None, :, None]).astype(jnp.int32), axis=2)
    begin = jnp.any(starts[:, None, :] == place[None, edge:, None], axis=2)
    same = [to_tokens(ident[:, k : k + stretch] == ident[:, edge:])[:, None] for k in range(taps)]
    begin = to_tokens(begin)[:, None]

    inner = jnp.dot(normed, w_inner, preferred_element_type=F32).astype(BF16)
    inner_before = jnp.dot(norm(before), w_inner, preferred_element_type=F32).astype(BF16)
    gate = jnp.dot(normed, w_gate, preferred_element_type=F32).astype(BF16).astype(F32)
    kern = conv_kernel.astype(F32)
    inner_s = stacked(inner)
    lead = inner_before.reshape(blocks, 4, HALO, ch)[:, :, HALO - edge :, :]
    lead = jnp.moveaxis(lead, 2, 1)[:, :, :, None, :]
    own_lead = inner_s[:, half - edge :].reshape(blocks, edge, 4, 2, ch)[:, :, :, :1, :]
    lead = jnp.concatenate([lead, own_lead], axis=3).reshape(blocks, edge, 8, ch)
    extended = jnp.concatenate([lead, inner_s], axis=1)
    taps_in = [extended[:, k : k + half].reshape(tokens, ch).astype(F32) for k in range(taps)]
    conv = conv_bias.astype(F32)[None, :]
    for k in range(taps):
        conv = conv + kern[k][None, :] * jnp.where(same[k], taps_in[k], 0.0)
    mixed = jax.nn.silu(conv).astype(BF16)
    mixed_f = mixed.astype(F32)
    w_sel = jnp.pad(select_proj, ((0, 0), (0, 128 - select_proj.shape[1])))
    proj = total_over_fsdp(nf, 1, jnp.dot(mixed, w_sel, preferred_element_type=F32))
    step_low = proj[:, :rank].astype(BF16)
    step_pre = jnp.dot(step_low, step_proj, preferred_element_type=F32) + step_bias.astype(F32)[None, :]
    step = jax.nn.softplus(step_pre)
    u = step * mixed_f
    stepd = jnp.where(begin, RESET, step)
    rate = -jnp.exp(log_decay.astype(F32))
    rate2 = rate * LOG2E
    gate_act = jax.nn.silu(gate)
    d_gated = times_transposed(cot, output_proj).astype(BF16).astype(F32)
    d_y = d_gated * gate_act

    coefs = coef_pieces(proj, rank, nstate)
    b, p, g = scan_ends(stepd, u, d_y, coefs, rate2, rank, count)
    run = jnp.sum(stacked(stepd), axis=1)

    def halves(v):
        v = v.reshape(v.shape[:-2] + (4, 2, ch))
        return v[..., 0, :], v[..., 1, :]

    b0, b1 = halves(b)
    p0, p1 = halves(p)
    g0, g1 = halves(g)
    r0, r1 = halves(run)
    flat = (blocks * nstate * 4, ch)
    bf, gb, tf, tb = carry_over_seq(
        reach,
        ns,
        2,
        (p1 * b0 + b1).astype(BF16).reshape(flat),
        (g0 + p0 * g1).astype(BF16).reshape(flat),
        (r0 + r1).reshape(blocks * 4, ch),
    )
    state_shape = (blocks, nstate, 4, ch)

    def gathered(ends, sums, valid):
        state = jnp.zeros(state_shape, F32)
        for j in range(reach - 1, -1, -1):
            decay = jnp.exp2(rate2[None, :, None, :] * sums[j].reshape(blocks, 1, 4, ch))
            new = decay * state + ends[j].reshape(state_shape).astype(F32)
            state = jnp.where(valid(j + 1), new, 0.0)
        return state

    h_first = gathered(bf, tf, lambda j: s - j >= 0)
    l_last = gathered(gb, tb, lambda j: s + j < ns)
    hin = jnp.stack([h_first, p0 * h_first + b0], axis=3).reshape(blocks, nstate, 8, ch)
    lin = jnp.stack([g1 + p1 * l_last, l_last], axis=3).reshape(blocks, nstate, 8, ch)

    y, pulled, slopes, coef, tot = scan_all(stepd, u, d_y, coefs, rate2, hin, lin, rank, count)
    log_decay_grad = rate * jnp.sum(tot, axis=(0, 2))
    d_step = mixed_f * pulled + slopes * LN2
    d_pre = d_step * jax.nn.sigmoid(step_pre)
    step_bias_grad = jnp.sum(d_pre, axis=0)
    d_lin = d_pre.astype(BF16)
    wide = jnp.pad(step_proj, ((0, 128 - rank), (0, 0)))
    part = times_transposed(d_lin, wide) + coef
    d_proj = total_over_fsdp(nf, 3, part).astype(BF16)

    skip = skip_gain.astype(F32)[None, :]
    y_full = y + skip * mixed_f
    gated = (y_full * gate_act).astype(BF16)
    out_part = jnp.dot(from_tokens(gated).reshape(tokens, ch), output_proj, preferred_element_type=F32)
    out_sum = share_over_fsdp(nf, 4, out_part.astype(BF16).reshape(nf, rd * stretch, width))
    own = residual.reshape(rd * stretch, width).astype(F32)
    layer_output = (own + out_sum).astype(BF16).reshape(rd, stretch, width)
    output_grad = rows_inner(gated, cot)
    d_gate = (d_gated * y_full * silu_slope(gate)).astype(BF16)
    gate_grad = rows_inner(normed, d_gate).astype(BF16)
    gate_grad = swap_over_fsdp(nf, 5, gate_grad.reshape(nf, width // nf, ch))
    skip_grad = jnp.sum(d_y * mixed_f, axis=0)
    step_grad = rows_inner(step_low, d_lin)

    w_sel_t = w_sel
    select_grad = rows_inner(mixed, d_proj)[:, : select_proj.shape[1]]
    d_mixed = step * pulled + d_y * skip + times_transposed(d_proj, w_sel_t)
    d_conv = d_mixed * silu_slope(conv)
    conv_bias_grad = jnp.sum(d_conv, axis=0)
    masked = [jnp.where(same[k], d_conv, 0.0) for k in range(taps)]
    kernel_grad = jnp.stack([jnp.sum(masked[k] * jnp.where(same[k], taps_in[k], 0.0), axis=0) for k in range(taps)])
    tilted = [stacked(masked[k])[:, :edge] * kern[k][None, None, None, :] for k in range(taps)]
    over = []
    for j in range(edge):
        over.append(sum(tilted[k][:, j - k] for k in range(j + 1)))
    over = jnp.stack(over, axis=1)
    behind = back_over_seq(ns, 6, over.reshape(blocks * edge * 8, ch)).reshape(blocks, edge, 4, 2, ch)
    behind = jnp.where(s + 1 < ns, behind[:, :, :, :1], 0.0)
    back = jnp.concatenate([over.reshape(blocks, edge, 4, 2, ch)[:, :, :, 1:], behind], axis=3)
    back = back.reshape(blocks, edge, 8, ch)
    d_inner = jnp.zeros((blocks, half, 8, ch), F32)
    for k in range(taps):
        ahead = edge - k
        d_inner = d_inner + jnp.pad(
            stacked(masked[k])[:, ahead:] * kern[k][None, None, None, :], ((0, 0), (0, ahead), (0, 0), (0, 0))
        )
    d_inner = d_inner + jnp.pad(back, ((0, 0), (half - edge, 0), (0, 0), (0, 0)))
    d_inner = d_inner.reshape(tokens, ch).astype(BF16)
    inner_grad = rows_inner(normed, d_inner).astype(BF16)
    inner_grad = swap_over_fsdp(nf, 7, inner_grad.reshape(nf, width // nf, ch))
    d_norm_part = times_transposed(from_tokens(d_inner).reshape(tokens, ch), w_inner) + times_transposed(
        from_tokens(d_gate).reshape(tokens, ch), w_gate
    )
    d_normed = share_over_fsdp(nf, 8, d_norm_part.astype(BF16).reshape(nf, rd * stretch, width))
    scale = lax.rsqrt(jnp.mean(own * own, axis=1, keepdims=True) + EPS)
    hat = own * scale
    gain_grad = jnp.sum(d_normed * hat, axis=0)
    d_hat = d_normed * gain
    d_flat = scale * (d_hat - hat * jnp.mean(d_hat * hat, axis=1, keepdims=True))
    own_cot = out_cotangent.reshape(rd * stretch, width).astype(F32)
    residual_grad = (own_cot + d_flat).reshape(rd, stretch, width)

    def sides(v):
        return jnp.moveaxis(v, 0, 1).reshape(width // nf, nf * ch)

    early = lax.psum((output_grad.astype(BF16), sides(gate_grad)), "seq")
    late = lax.psum(sides(inner_grad), "seq")
    tiny = lax.psum((select_grad, step_grad, kernel_grad, conv_bias_grad, step_bias_grad, log_decay_grad, skip_grad), "seq")
    gains = lax.psum_scatter(lax.psum(gain_grad, "seq"), "fsdp", scatter_dimension=0, tiled=True)
    input_grad = jnp.concatenate([late, early[1]], axis=1).astype(F32)
    return (
        layer_output,
        residual_grad,
        gains,
        input_grad,
        tiny[2],
        tiny[3],
        tiny[0],
        tiny[1],
        tiny[4],
        tiny[5],
        tiny[6],
        early[0].astype(F32),
    )


def solution(mesh):
    nf, ns = mesh.shape["fsdp"], mesh.shape["seq"]
    in_specs = (
        P("fsdp", "seq", None),
        P("fsdp", "seq", None),
        P("fsdp", None),
        P("fsdp"),
        P("fsdp", None),
        P(None, "fsdp"),
        P("fsdp"),
        P("fsdp", None),
        P(None, "fsdp"),
        P("fsdp"),
        P(None, "fsdp"),
        P("fsdp"),
        P("fsdp", None),
    )
    out_specs = (
        P("fsdp", "seq", None),
        P("fsdp", "seq", None),
        P("fsdp"),
        P("fsdp", None),
        P(None, "fsdp"),
        P("fsdp"),
        P("fsdp", None),
        P(None, "fsdp"),
        P("fsdp"),
        P(None, "fsdp"),
        P("fsdp"),
        P("fsdp", None),
    )
    return jax.shard_map(
        functools.partial(shards, nf, ns), mesh=mesh, in_specs=in_specs, out_specs=out_specs, check_vma=False
    )
```

```python
import functools
import math

import jax
import jax.numpy as jnp
from jax import lax
from jax.experimental import pallas as pl
from jax.experimental.pallas import tpu as pltpu
from jax.sharding import PartitionSpec as P

EPS = 1e-05
MESH = pl.DeviceIdType.MESH
LOG2E = math.log2(math.e)
LN2 = math.log(2.0)
BF16 = jnp.bfloat16
F32 = jnp.float32
ANY = pl.BlockSpec(memory_space=pl.ANY)
VMEM = pl.BlockSpec(memory_space=pltpu.VMEM)
RESET = 1e30
HALO = 16
DOCS = 8


def here():
    return lax.axis_index("fsdp"), lax.axis_index("seq")


def greet(peers):
    barrier = pltpu.get_barrier_semaphore()
    count = 0
    for ok, device in peers:
        if ok is None:
            pl.semaphore_signal(barrier, inc=1, device_id=device, device_id_type=MESH)
            count = count + 1
        else:

            @pl.when(ok)
            def _():
                pl.semaphore_signal(barrier, inc=1, device_id=device, device_id_type=MESH)

            count = count + ok.astype(jnp.int32)
    pl.semaphore_wait(barrier, count)


def remote(src, dst, send, recv, device):
    return pltpu.make_async_remote_copy(
        src_ref=src, dst_ref=dst, send_sem=send, recv_sem=recv, device_id=device, device_id_type=MESH
    )


def comm_params(cid, vmem=None):
    return pltpu.CompilerParams(collective_id=cid, has_side_effects=True, vmem_limit_bytes=vmem)


class Wire:
    def __init__(self, ssem, rsem):
        self.ssem, self.rsem, self.copies, self.done = ssem, rsem, [], []

    def send(self, src, dst, device):
        k = len(self.copies)
        cp = remote(src, dst, self.ssem.at[k], self.rsem.at[k], device)
        self.copies.append(cp)
        cp.start()
        return cp

    def sent(self, cp):
        cp.wait_send()
        self.done.append(cp)

    def drain(self):
        for cp in self.copies:
            if all(cp is not other for other in self.done):
                cp.wait_send()


LEAD = 24


def rows_at(base, size, unit=8):
    return pl.ds(pl.multiple_of(base, unit), size)


def split_at(i, n):
    return lax.div(i, n), lax.rem(i, n)


def front_kernel(nf, ns, rd, rank, nstate, sems, *refs):
    (x, ct, w, sm, vecs, w_sel, w_step, w_out) = refs[:8]
    (normed_o, cg_o, ext_o, slope_o, mix_o, dy_o, ga_o, dgs_o, step_o, beg_o, proj_o, packed_o, wi_o, wg_o, gain_o) = refs[8:23]
    (xg, cg, wi, wg, sg, hal, hres, vbuf, gbuf, ext, slope, mix, mixb, dy, ga, dgs, step, beg, part, got, mid, far, proj, packed) = refs[
        23:47
    ]
    ssem, rsem, hsem, hrem, lsem, osem = refs[47:]
    f, s = here()
    core, b = lax.rem(f, 2), lax.rem(s, 2)
    stretch = x.shape[1]
    half = stretch // 2
    dmodel = xg.shape[1]
    ch = wi.shape[1]
    groups = ch // 128
    rows = nf * rd
    blocks = rows // 4
    tokens = rows * stretch
    drow = w.shape[0]
    inner_all = w.shape[1] // 2
    chips = list(range(2, nf, 2))
    peer = (lax.bitwise_xor(f, 1), s)
    beside = (f, lax.bitwise_xor(s, 1))
    up, down = s + 1, s - 1
    has_up, has_down = up < ns, down >= 0

    def fdev(i):
        return (lax.bitwise_xor(f, i), s)

    greeted = [(None, fdev(i)) for i in range(1, nf)] + [(None, beside)]
    for i in range(nf):
        greeted.append((has_up, (lax.bitwise_xor(f, i), up)))
        greeted.append((has_down, (lax.bitwise_xor(f, i), down)))
    greet(greeted)
    wire = Wire(ssem, rsem)

    def act_rows(who):
        return rows_at(who * (rd * stretch), rd * stretch, 16)

    def wcols(who, base, start, size):
        return w.at[pl.ds(start, size), pl.ds(pl.multiple_of(base + who * ch, 128), ch)]

    def wrows(who, start, size):
        return pl.ds(pl.multiple_of(who * drow + start, 16), size)

    half_rows = drow // 2
    mine = pl.multiple_of(b * half_rows, 16)

    locals_ = []

    def local(src, dst):
        cp = pltpu.make_async_copy(src, dst, lsem.at[len(locals_)])
        locals_.append(cp)
        cp.start()
        return cp

    x2 = [x.at[q] for q in range(rd)]
    smalls = [wire.send(sm, sg.at[f], fdev(i)) for i in range(1, nf)]
    own_x = [local(x2[q], xg.at[rows_at((f * rd + q) * stretch, stretch, 16)]) for q in range(rd)]
    own_s = local(sm, sg.at[f])

    def send_rows(src, dst):
        if rd == 1:
            return [wire.send(src.at[0], dst.at[act_rows(f)], fdev(i)) for i in [1] + chips]
        return [wire.send(src, dst.at[act_rows(f)], fdev(i)) for i in [1] + chips]

    def send_weight(base, dst):
        out = [wire.send(wcols(peer[0], base, 0, drow), dst.at[wrows(f, 0, drow)], peer)]
        for i in range(2, nf):
            out.append(
                wire.send(wcols(lax.bitwise_xor(f, i), base, mine, half_rows), dst.at[wrows(f, mine, half_rows)], fdev(i))
            )
        return out

    xs = send_rows(x, xg)
    wis = send_weight(0, wi)
    halos = [
        remote(
            x.at[:, pl.ds(stretch - HALO, HALO), :],
            hal.at[pl.ds(f * rd, rd)],
            hsem.at[i],
            hrem.at[i],
            (lax.bitwise_xor(f, i), up),
        )
        for i in range(nf)
    ]

    @pl.when(has_up)
    def _():
        for cp in halos:
            cp.start()

    own_wi = local(wcols(f, 0, 0, drow), wi.at[wrows(f, 0, drow)])
    cs = send_rows(ct, cg)
    wgs = send_weight(inner_all, wg)
    own_c = [local(ct.at[q], cg.at[rows_at((f * rd + q) * stretch, stretch, 16)]) for q in range(rd)]
    own_wg = local(wcols(f, inner_all, 0, drow), wg.at[wrows(f, 0, drow)])

    own_s.wait()
    for cp in smalls:
        cp.wait_recv()
    table = sg[0]
    for k in range(1, nf):
        table = table + sg[k]
    gain = jnp.concatenate([table[q : q + 1, :] for q in range(dmodel // 128)], axis=1)
    gain_o[...] = table
    sub = lax.broadcasted_iota(jnp.int32, (8, 128), 0)
    for n in range(blocks):
        lens = jnp.zeros((8, 128), F32)
        for q in range(4):
            r = n * 4 + q
            line = sg[r // rd, 8 + r % rd : 9 + r % rd, :]
            lens = jnp.where(sub // 2 == q, jnp.broadcast_to(line, (8, 128)), lens)
        starts = [jnp.zeros((8, 128), F32)]
        for j in range(DOCS - 1):
            starts.append(starts[-1] + jnp.broadcast_to(lens[:, j : j + 1], (8, 128)))
        first = (s * stretch + (sub % 2) * half).astype(F32)

        def mark(t, carry, n=n, starts=starts, first=first):
            place = first + (t - 2).astype(F32)
            hit = starts[0] == place
            for j in range(1, DOCS):
                hit = jnp.logical_or(hit, starts[j] == place)
            beg[rows_at(n * (half + 2) * 8 + t * 8, 8), :] = jnp.where(hit, RESET, 0.0)
            return carry

        lax.fori_loop(0, half + 2, mark, 0)

    def norm_rows(ref, start, size):
        def one(i, carry):
            at_ = rows_at(start + i * 32, 32, 16)
            v = ref[at_, :].astype(F32)
            scale = lax.rsqrt(jnp.sum(v * v, axis=1, keepdims=True) * (1.0 / dmodel) + EPS)
            ref[at_, :] = (v * scale * gain).astype(BF16)
            return carry

        lax.fori_loop(0, size // 32, one, 0)

    span = rd * stretch
    for cp in own_x:
        cp.wait()
    norm_rows(xg, f * span, span)
    xs[0].wait_recv()
    norm_rows(xg, peer[0] * span, span)
    xf = []
    for n, i in enumerate(chips):
        xs[1 + n].wait_recv()
        block = act_rows(lax.bitwise_xor(f, i))
        xf.append(wire.send(xg.at[block], xg.at[block], peer))
    for n, i in enumerate(chips):
        xf[n].wait_recv()
        norm_rows(xg, lax.bitwise_xor(f, i + 1) * span, span)
        wire.sent(xf[n])
        norm_rows(xg, lax.bitwise_xor(f, i) * span, span)
    wif = []
    for n, i in enumerate(range(2, nf)):
        wis[1 + n].wait_recv()
        block = wrows(lax.bitwise_xor(f, i), mine, half_rows)
        wif.append(wire.send(wi.at[block], wi.at[block], beside))

    @pl.when(has_down)
    def _():
        for cp in halos:
            cp.wait_recv()

    hal_rows = rows * HALO
    hflat = vbuf
    for r in range(rows):
        v = hal[r].astype(F32)
        scale = lax.rsqrt(jnp.sum(v * v, axis=1, keepdims=True) * (1.0 / dmodel) + EPS)
        hflat[r * HALO : (r + 1) * HALO, :] = jnp.where(s > 0, v * scale * gain, 0.0).astype(BF16)
    own_wi.wait()
    wis[0].wait_recv()
    for cp in wif:
        cp.wait_recv()
    out_copies = []

    def put(src, dst):
        cp = pltpu.make_async_copy(src, dst, osem.at[len(out_copies)])
        out_copies.append(cp)
        cp.start()

    put(xg, normed_o)
    put(beg, beg_o)
    put(wi, wi_o)

    def inner_row(r, carry):
        v = jnp.dot(xg[rows_at(r * stretch, stretch, 16), :], wi[...], preferred_element_type=F32)
        v = v.astype(BF16).astype(F32)
        n, q = split_at(r, 4)
        base = n * (half * 8 + LEAD) + LEAD + q * 2
        for g in range(2):
            for d in range(groups):
                ext[d, pl.ds(base + g, half, stride=8), :] = v[g * half : (g + 1) * half, cut(d)]
        return carry

    lax.fori_loop(0, rows, inner_row, 0)
    hv = jnp.dot(hflat[...], wi[...], preferred_element_type=F32).astype(BF16).astype(F32)
    for d in range(groups):
        hres[d] = hv[:, cut(d)]
    for n in range(blocks):
        base = n * (half * 8 + LEAD)
        for d in range(groups):
            for j in range(3):
                before = hres[d, pl.ds(n * 4 * HALO + HALO - 3 + j, 4, stride=HALO), :]
                ext[d, pl.ds(base + j * 8, 4, stride=2), :] = before
                own = ext[d, pl.ds(base + LEAD + (half - 3 + j) * 8, 4, stride=2), :]
                ext[d, pl.ds(base + j * 8 + 1, 4, stride=2), :] = own
    put(ext, ext_o)

    span_t = half * 8
    chunk = 64
    per = span_t // chunk

    def conv_chunk(idx, carry):
        nd, c = split_at(idx, per)
        n, d = split_at(nd, groups)
        base = n * (span_t + LEAD) + c * chunk
        bb = n * (span_t + 16) + c * chunk
        same2 = jnp.where(beg[rows_at(bb + 16, chunk), :] > 0.0, 0.0, 1.0)
        same1 = jnp.where(beg[rows_at(bb + 8, chunk), :] > 0.0, 0.0, same2)
        same0 = jnp.where(beg[rows_at(bb, chunk), :] > 0.0, 0.0, same1)
        tap = [ext[d, rows_at(base + k * 8, chunk), :] for k in range(4)]
        v = vecs[d, 4:5, :] + vecs[d, 0:1, :] * (tap[0] * same0)
        v = v + vecs[d, 1:2, :] * (tap[1] * same1) + vecs[d, 2:3, :] * (tap[2] * same2) + vecs[d, 3:4, :] * tap[3]
        sig = jax.nn.sigmoid(v)
        m = (v * sig).astype(BF16)
        at_ = rows_at(n * span_t + c * chunk, chunk)
        slope[d, at_, :] = sig * (1.0 + v * (1.0 - sig))
        mixb[d, rows_at(n * span_t + c * chunk, chunk, 16), :] = m
        mix[d, at_, :] = m.astype(F32)
        return carry

    lax.fori_loop(0, blocks * groups * per, conv_chunk, 0)
    put(slope, slope_o)
    put(mix, mix_o)

    hs = tokens // 2
    other = (1 - core) * hs
    keep = core * hs

    def project(start):
        total = None
        for d in range(groups):
            term = jnp.dot(mixb[d, rows_at(start, hs, 16), :], w_sel[d * 128 : (d + 1) * 128, :], preferred_element_type=F32)
            total = term if total is None else total + term
        part[rows_at(start, hs), :] = total

    project(other)
    one = wire.send(part.at[rows_at(other, hs)], got, peer)
    project(keep)
    one.wait_recv()
    mid[...] = part[rows_at(keep, hs), :] + got[...]
    two = [wire.send(mid, far.at[n], fdev(i)) for n, i in enumerate(chips)]

    cf = []
    for n, i in enumerate(chips):
        cs[1 + n].wait_recv()
        block = act_rows(lax.bitwise_xor(f, i))
        cf.append(wire.send(cg.at[block], cg.at[block], peer))
    wgf = []
    for n, i in enumerate(range(2, nf)):
        wgs[1 + n].wait_recv()
        block = wrows(lax.bitwise_xor(f, i), mine, half_rows)
        wgf.append(wire.send(wg.at[block], wg.at[block], beside))
    for cp in own_c + [own_wg]:
        cp.wait()
    for cp in [cs[0], wgs[0]] + cf + wgf:
        cp.wait_recv()
    put(cg, cg_o)
    put(wg, wg_o)

    def gate_row(r, carry):
        at_ = rows_at(r * stretch, stretch, 16)
        gbuf[0] = jnp.dot(xg[at_, :], wg[...], preferred_element_type=F32).astype(BF16).astype(F32)
        gbuf[1] = times_transposed(cg[at_, :], w_out[...]).astype(BF16).astype(F32)
        n, q = split_at(r, 4)
        base = n * span_t + q * 2
        for g in range(2):
            for d in range(groups):
                def some(i, carry2, g=g, d=d):
                    src = rows_at(g * half + i * 32, 32)
                    v, dg = gbuf[0, src, cut(d)], gbuf[1, src, cut(d)]
                    sig = jax.nn.sigmoid(v)
                    act = v * sig
                    dst = rows_at(r * stretch + g * half + i * 32, 32)
                    ga[dst, cut(d)] = act
                    dgs[dst, cut(d)] = dg * (sig * (1.0 + v * (1.0 - sig)))
                    dy[d, pl.ds(base + g + i * 256, 32, stride=8), :] = dg * act
                    return carry2

                lax.fori_loop(0, half // 32, some, 0)
        return carry

    lax.fori_loop(0, rows, gate_row, 0)
    put(dy, dy_o)
    put(ga, ga_o)
    put(dgs, dgs_o)

    for cp in two:
        cp.wait_recv()
    acc = mid[...]
    for n in range(len(chips)):
        acc = acc + far[n]
    proj[rows_at(keep, hs), :] = acc
    three = wire.send(proj.at[rows_at(keep, hs)], proj.at[rows_at(keep, hs)], peer)

    lane = lax.broadcasted_iota(jnp.int32, (256, 128), 1)

    def step_rows(i, carry):
        at_ = rows_at(carry + i * 256, 256)
        p = proj[at_, :]
        pre = jnp.dot(p[:, :rank].astype(BF16), w_step[...], preferred_element_type=F32)
        for d in range(groups):
            v = pre[:, cut(d)] + vecs[d, 5:6, :]
            step[d, at_, :] = jnp.maximum(v, 0.0) + jnp.log1p(jnp.exp(-jnp.abs(v)))
        top = p.astype(BF16)
        rest = p - top.astype(F32)
        second = rest.astype(BF16)
        third = (rest - second.astype(F32)).astype(BF16).astype(F32)
        width = 2 * nstate
        out = pltpu.roll(top.astype(F32), 128 - rank, 1)
        out = jnp.where(lane < width, out, pltpu.roll(second.astype(F32), (128 - rank + width) % 128, 1))
        out = jnp.where(lane < 2 * width, out, pltpu.roll(third, (128 - rank + 2 * width) % 128, 1))
        packed[rows_at(carry + i * 256, 256, 16), :] = jnp.where(lane < 3 * width, out, 0.0).astype(BF16)
        return carry

    lax.fori_loop(0, hs // 256, step_rows, keep)
    three.wait_recv()
    lax.fori_loop(0, hs // 256, step_rows, other)
    put(step, step_o)
    put(proj, proj_o)
    put(packed, packed_o)
    for cp in out_copies:
        cp.wait()
    wire.drain()

    @pl.when(has_up)
    def _():
        for cp in halos:
            cp.wait_send()

    assert len(wire.copies) == sems


def front(nf, ns, x, ct, w, sm, vecs, w_sel, w_step, w_out, rank, nstate):
    rd, stretch, width = x.shape
    drow = w.shape[0]
    ch = w_step.shape[1]
    groups = ch // 128
    rows = nf * rd
    blocks = rows // 4
    tokens = rows * stretch
    half = stretch // 2
    chips = nf // 2 - 1
    ext_rows = blocks * (half * 8 + LEAD)
    beg_rows = blocks * (half + 2) * 8
    sems = 0
    sems += nf - 1
    sems += 2 * (1 + chips)
    sems += 2 * (nf - 1)
    sems += 2 * chips + 2 * (nf - 2)
    sems += 2 + chips
    shape = jax.ShapeDtypeStruct
    wide = (groups, tokens, 128)
    out_shape = (
        shape((tokens, width), BF16),
        shape((tokens, width), BF16),
        shape((groups, ext_rows, 128), F32),
        shape(wide, F32),
        shape(wide, F32),
        shape(wide, F32),
        shape((tokens, ch), F32),
        shape((tokens, ch), F32),
        shape(wide, F32),
        shape((beg_rows, 128), F32),
        shape((tokens, 128), F32),
        shape((tokens, 128), BF16),
        shape((width, ch), BF16),
        shape((width, ch), BF16),
        shape((16, 128), F32),
    )
    v = pltpu.VMEM
    scratch = [
        v((tokens, width), BF16),
        v((tokens, width), BF16),
        v((width, ch), BF16),
        v((width, ch), BF16),
        v((nf, 16, 128), F32),
        v((rows, HALO, width), BF16),
        v((groups, rows * HALO, 128), F32),
        v((rows * HALO, width), BF16),
        v((2, stretch, ch), F32),
        v((groups, ext_rows, 128), F32),
        v(wide, F32),
        v(wide, F32),
        v(wide, BF16),
        v(wide, F32),
        v((tokens, ch), F32),
        v((tokens, ch), F32),
        v(wide, F32),
        v((beg_rows, 128), F32),
        v((tokens, 128), F32),
        v((tokens // 2, 128), F32),
        v((tokens // 2, 128), F32),
        v((chips, tokens // 2, 128), F32),
        v((tokens, 128), F32),
        v((tokens, 128), BF16),
        pltpu.SemaphoreType.DMA((sems,)),
        pltpu.SemaphoreType.DMA((sems,)),
        pltpu.SemaphoreType.DMA((nf,)),
        pltpu.SemaphoreType.DMA((nf,)),
        pltpu.SemaphoreType.DMA((2 * rd + 3,)),
        pltpu.SemaphoreType.DMA((14,)),
    ]
    return pl.pallas_call(
        functools.partial(front_kernel, nf, ns, rd, rank, nstate, sems),
        out_shape=out_shape,
        in_specs=[ANY] * 4 + [VMEM] * 4,
        out_specs=[ANY] * 14 + [VMEM],
        scratch_shapes=scratch,
        compiler_params=comm_params(0, 62 << 20),
        name="front",
    )(x, ct, w, sm, vecs, w_sel, w_step, w_out)


def carry_kernel(reach, ns, b, g, t, bf, gb, tf, tb, ssem, rsem):
    f, s = here()
    peers = []
    for j in range(1, reach + 1):
        peers.append((s + j < ns, (f, s + j)))
        peers.append((s - j >= 0, (f, s - j)))
    greet(peers)

    def copies(j):
        ahead, back = (f, s + j), (f, s - j)
        k = j - 1
        fwd = [
            remote(b, bf.at[k], ssem.at[0, k], rsem.at[0, k], ahead),
            remote(t, tf.at[k], ssem.at[1, k], rsem.at[1, k], ahead),
        ]
        bwd = [
            remote(g, gb.at[k], ssem.at[2, k], rsem.at[2, k], back),
            remote(t, tb.at[k], ssem.at[3, k], rsem.at[3, k], back),
        ]
        return fwd, bwd

    every = [copies(j) for j in range(1, reach + 1)]
    for j in range(1, reach + 1):
        fwd, bwd = every[j - 1]

        @pl.when(s + j < ns)
        def _():
            for cp in fwd:
                cp.start()

        @pl.when(s - j >= 0)
        def _():
            for cp in bwd:
                cp.start()

    for j in range(1, reach + 1):
        fwd, bwd = every[j - 1]

        @pl.when(s + j < ns)
        def _():
            for cp in fwd:
                cp.wait_send()
            for cp in bwd:
                cp.wait_recv()

        @pl.when(s - j >= 0)
        def _():
            for cp in bwd:
                cp.wait_send()
            for cp in fwd:
                cp.wait_recv()


def carry_over_seq(reach, ns, cid, b, g, t):
    shape = jax.ShapeDtypeStruct
    return pl.pallas_call(
        functools.partial(carry_kernel, reach, ns),
        out_shape=(
            shape((reach,) + b.shape, b.dtype),
            shape((reach,) + g.shape, g.dtype),
            shape((reach,) + t.shape, t.dtype),
            shape((reach,) + t.shape, t.dtype),
        ),
        in_specs=[VMEM] * 3,
        out_specs=[VMEM] * 4,
        scratch_shapes=[
            pltpu.SemaphoreType.DMA((4, reach)),
            pltpu.SemaphoreType.DMA((4, reach)),
        ],
        compiler_params=comm_params(cid, 32 << 20),
        name="carry_over_seq",
    )(b, g, t)


BLOCK_TOKENS = 1024


def at(t):
    return pl.ds(pl.multiple_of(t * 8, 8), 8)


def cut(d):
    return slice(d * 128, (d + 1) * 128)


def pieces(v, count):
    out = []
    for _ in range(count):
        top = v.astype(BF16)
        out.append(top)
        v = v - top.astype(F32)
    return out


def spread_coefs(packed, cscr, first, count, nstate):
    wide = 2 * count * 128
    source = lax.broadcasted_iota(jnp.int32, (128, wide), 0)
    block = lax.broadcasted_iota(jnp.int32, (128, wide), 1) // 128
    want = jnp.where(block < count, block, nstate - count + block) + first
    pick = jnp.where(
        jnp.logical_and(source % (2 * nstate) == want, source < 6 * nstate), 1.0, 0.0
    ).astype(BF16)
    cscr[...] = jnp.dot(packed[...], pick, preferred_element_type=F32)


ENDS_UNROLL = 4
SCAN_UNROLL = 4


def ends_kernel(count, groups, nstate, step, mix, dy, beg, packed, rate, b, p, g, cscr):
    j = pl.program_id(1)
    steps = step.shape[1] // 8
    spread_coefs(packed, cscr, j * count, count, nstate)
    keys = [(d, i) for d in range(groups) for i in range(count)]
    rates = [jnp.broadcast_to(rate[0, i : i + 1, cut(d)], (8, 128)) for d, i in keys]

    def one(t, carry):
        bs, ps, gs = carry
        nb, np_, ng = [], [], []
        reset = beg[rows_at(LEAD - 8 + t * 8, 8), :]
        enter = [cscr[at(t), cut(i)] for i in range(count)]
        read = [cscr[at(t), cut(count + i)] for i in range(count)]
        for d in range(groups):
            st, dt = step[d, at(t), :], dy[d, at(t), :]
            ut = st * mix[d, at(t), :]
            st = st + reset
            for i in range(count):
                k = d * count + i
                a = jnp.exp2(st * rates[k])
                prod = ps[k] * a
                nb.append(bs[k] * a + enter[i] * ut)
                np_.append(prod)
                ng.append(gs[k] + prod * (read[i] * dt))
        return tuple(nb), tuple(np_), tuple(ng)

    size = count * groups
    zero = jnp.zeros((8, 128), F32)
    init = ((zero,) * size, (zero + 1.0,) * size, (zero,) * size)
    bs, ps, gs = lax.fori_loop(0, steps, one, init, unroll=ENDS_UNROLL)
    for k, (d, i) in enumerate(keys):
        b[0, i, :, cut(d)] = bs[k]
        p[0, i, :, cut(d)] = ps[k]
        g[0, i, :, cut(d)] = gs[k]


def scan_specs(tokens, ch, nstate, count):
    blocks = tokens // BLOCK_TOKENS
    groups = ch // 128
    steps = BLOCK_TOKENS // 8
    tok = pl.BlockSpec((groups, BLOCK_TOKENS, 128), lambda n, j: (0, n, 0))
    narrow = pl.BlockSpec((BLOCK_TOKENS, 128), lambda n, j: (n, 0))
    marks = pl.BlockSpec((BLOCK_TOKENS + 16, 128), lambda n, j: (n, 0))
    rates = pl.BlockSpec((1, count, ch), lambda n, j: (j, 0, 0))
    state = pl.BlockSpec((1, count, 8, ch), lambda n, j: (n, j, 0, 0))
    flat = pl.BlockSpec((BLOCK_TOKENS, ch), lambda n, j: (n, 0))
    grid = (blocks, nstate // count)
    kept = pl.BlockSpec((1, steps, count * groups, 8, 128), lambda n, j: (n * grid[1] + j, 0, 0, 0, 0))
    kept_shape = jax.ShapeDtypeStruct((math.prod(grid), steps, count * groups, 8, 128), F32)
    return grid, groups, tok, narrow, marks, rates, state, flat, kept, kept_shape


def scan_ends(step, mix, dy, beg, packed, rate, count):
    groups, tokens, _ = step.shape
    nstate, ch = rate.shape
    grid, groups, tok, narrow, marks, rates, state, flat, kept, kept_shape = scan_specs(tokens, ch, nstate, count)
    shape = jax.ShapeDtypeStruct((grid[0], nstate, 8, ch), F32)
    work = tokens * nstate * ch
    return pl.pallas_call(
        functools.partial(ends_kernel, count, groups, nstate),
        out_shape=(shape,) * 3,
        grid=grid,
        in_specs=[tok, tok, tok, marks, narrow, rates],
        out_specs=[state] * 3,
        scratch_shapes=[pltpu.VMEM((BLOCK_TOKENS, 2 * count * 128), F32)],
        compiler_params=pltpu.CompilerParams(vmem_limit_bytes=40 << 20),
        cost_estimate=pl.CostEstimate(flops=8 * work, bytes_accessed=12 * tokens * ch, transcendentals=work),
        name="scan_ends",
    )(step, mix, dy, beg, packed, rate.reshape(nstate // count, count, ch))


def rates_of(rate, keys):
    return [jnp.broadcast_to(rate[0, i : i + 1, cut(d)], (8, 128)) for d, i in keys]


def lane_sums(seen, coef, count, first):
    wide = count * 128
    block = lax.broadcasted_iota(jnp.int32, (wide, 128), 0) // 128
    column = lax.broadcasted_iota(jnp.int32, (wide, 128), 1)
    ones = jnp.where(column == block + first, 1.0, 0.0).astype(BF16)
    for part in pieces(seen[...], 2):
        coef[...] += jnp.dot(part, ones, preferred_element_type=F32)


def forward_kernel(
    count, groups, rank, nstate, step, mix, dy, beg, packed, rate, hin, ga, dgs, vecs, gated, dgate, states, coef, cscr, seen_scr, y
):
    j = pl.program_id(1)
    steps = step.shape[1] // 8
    keys = [(d, i) for d in range(groups) for i in range(count)]
    rates = rates_of(rate, keys)
    spread_coefs(packed, cscr, j * count, count, nstate)

    @pl.when(j == 0)
    def _():
        coef[...] = jnp.zeros_like(coef)
        for d in range(groups):
            y[d] = mix[d] * vecs[d, 6:7, :]

    def forward(t, state):
        reset = beg[rows_at(16 + t * 8, 8), :]
        enter = [cscr[at(t), cut(i)] for i in range(count)]
        read = [cscr[at(t), cut(count + i)] for i in range(count)]
        new = []
        seen = [None] * count
        for d in range(groups):
            st, dt = step[d, at(t), :], dy[d, at(t), :]
            ut = st * mix[d, at(t), :]
            st = st + reset
            out = None
            for i in range(count):
                k = d * count + i
                a = jnp.exp2(st * rates[k])
                states[0, t, k] = state[k]
                h = state[k] * a + enter[i] * ut
                new.append(h)
                out = read[i] * h if out is None else out + read[i] * h
                term = h * dt
                seen[i] = term if seen[i] is None else seen[i] + term
            y[d, at(t), :] += out
        for i in range(count):
            seen_scr[at(t), cut(i)] = seen[i]
        return tuple(new)

    lax.fori_loop(0, steps, forward, tuple(hin[0, i, :, cut(d)] for d, i in keys), unroll=SCAN_UNROLL)
    lane_sums(seen_scr, coef, count, rank + nstate + j * count)

    @pl.when(j == pl.num_programs(1) - 1)
    def _():
        def some(idx, carry):
            where, i = split_at(idx, steps // 32)
            q, g = split_at(where, 2)
            for d in range(groups):
                v = y[d, pl.ds(q * 2 + g + i * 256, 32, stride=8), :]
                at_ = rows_at(where * steps + i * 32, 32, 16)
                gated[at_, cut(d)] = (v * ga[at_, cut(d)]).astype(BF16)
                dgate[at_, cut(d)] = (v * dgs[at_, cut(d)]).astype(BF16)
            return carry

        lax.fori_loop(0, 8 * (steps // 32), some, 0)


def backward_kernel(
    count, groups, rank, nstate, step, mix, dy, beg, packed, rate, lin, states, reads, pulled, gs, coef, tot, cscr, seen_scr
):
    j = pl.program_id(1)
    steps = step.shape[1] // 8
    size = count * groups
    keys = [(d, i) for d in range(groups) for i in range(count)]
    rates = rates_of(rate, keys)
    spread_coefs(packed, cscr, j * count, count, nstate)

    @pl.when(j == 0)
    def _():
        pulled[...] = jnp.zeros_like(pulled)
        gs[...] = jnp.zeros_like(gs)
        coef[...] = reads[...]

    def backward(k0, carry):
        t = steps - 1 - k0
        passed, sums = carry
        reset = beg[rows_at(16 + t * 8, 8), :]
        enter = [cscr[at(t), cut(i)] for i in range(count)]
        read = [cscr[at(t), cut(count + i)] for i in range(count)]
        new, news = [], []
        seen = [None] * count
        for d in range(groups):
            st, dt = step[d, at(t), :], dy[d, at(t), :]
            ut = st * mix[d, at(t), :]
            st = st + reset
            pull, slope_sum = None, None
            for i in range(count):
                k = d * count + i
                adj = passed[k] + read[i] * dt
                pull = adj * enter[i] if pull is None else pull + adj * enter[i]
                back = adj * jnp.exp2(st * rates[k])
                slope = back * states[0, t, k]
                slope_sum = slope * rates[k] if slope_sum is None else slope_sum + slope * rates[k]
                new.append(back)
                news.append(sums[k] + slope * st)
                term = adj * ut
                seen[i] = term if seen[i] is None else seen[i] + term
            pulled[d, at(t), :] += pull
            gs[d, at(t), :] += slope_sum
        for i in range(count):
            seen_scr[at(t), cut(i)] = seen[i]
        return tuple(new), tuple(news)

    zero = jnp.zeros((8, 128), F32)
    init = (tuple(lin[0, i, :, cut(d)] for d, i in keys), (zero,) * size)
    passed, sums = lax.fori_loop(0, steps, backward, init, unroll=SCAN_UNROLL)
    for n, (d, i) in enumerate(keys):
        line = jnp.sum(sums[n] * rates[n], axis=0, keepdims=True) * LN2
        at_ = pl.ds(j * count + i, 1)

        @pl.when(pl.program_id(0) == 0)
        def _():
            tot[d, at_, :] = line

        @pl.when(pl.program_id(0) > 0)
        def _():
            tot[d, at_, :] += line

    lane_sums(seen_scr, coef, count, rank + j * count)


def scan_forward(step, mix, dy, beg, packed, rate, hin, ga, dgs, vecs, rank, count):
    groups, tokens, _ = step.shape
    nstate, ch = rate.shape
    grid, groups, tok, narrow, marks, rates, state, flat, kept, kept_shape = scan_specs(tokens, ch, nstate, count)
    shape = jax.ShapeDtypeStruct
    work = tokens * nstate * ch
    vec = pl.BlockSpec(vecs.shape, lambda n, j: (0, 0, 0))
    return pl.pallas_call(
        functools.partial(forward_kernel, count, groups, rank, nstate),
        out_shape=(shape((tokens, ch), BF16), shape((tokens, ch), BF16), kept_shape, shape((tokens, 128), F32)),
        grid=grid,
        in_specs=[tok, tok, tok, marks, narrow, rates, state, flat, flat, vec],
        out_specs=[flat, flat, kept, narrow],
        scratch_shapes=[
            pltpu.VMEM((BLOCK_TOKENS, 2 * count * 128), F32),
            pltpu.VMEM((BLOCK_TOKENS, count * 128), F32),
            pltpu.VMEM((groups, BLOCK_TOKENS, 128), F32),
        ],
        compiler_params=pltpu.CompilerParams(vmem_limit_bytes=60 << 20),
        cost_estimate=pl.CostEstimate(flops=8 * work, bytes_accessed=4 * work, transcendentals=work),
        name="scan_forward",
    )(step, mix, dy, beg, packed, rate.reshape(nstate // count, count, ch), hin, ga, dgs, vecs)


def scan_backward(step, mix, dy, beg, packed, rate, lin, states, reads, rank, count):
    groups, tokens, _ = step.shape
    nstate, ch = rate.shape
    grid, groups, tok, narrow, marks, rates, state, flat, kept, kept_shape = scan_specs(tokens, ch, nstate, count)
    shape = jax.ShapeDtypeStruct
    work = tokens * nstate * ch
    return pl.pallas_call(
        functools.partial(backward_kernel, count, groups, rank, nstate),
        out_shape=(
            shape(step.shape, F32),
            shape(step.shape, F32),
            shape((tokens, 128), F32),
            shape((groups, nstate, 128), F32),
        ),
        grid=grid,
        in_specs=[tok, tok, tok, marks, narrow, rates, state, kept, narrow],
        out_specs=[tok, tok, narrow, pl.BlockSpec((groups, nstate, 128), lambda n, j: (0, 0, 0))],
        scratch_shapes=[
            pltpu.VMEM((BLOCK_TOKENS, 2 * count * 128), F32),
            pltpu.VMEM((BLOCK_TOKENS, count * 128), F32),
        ],
        compiler_params=pltpu.CompilerParams(vmem_limit_bytes=60 << 20),
        cost_estimate=pl.CostEstimate(flops=12 * work, bytes_accessed=4 * work, transcendentals=work),
        name="scan_backward",
    )(step, mix, dy, beg, packed, rate.reshape(nstate // count, count, ch), lin, states, reads)


class Stream:
    def __init__(self, wire, place, src, got_y, mid, got_z, red, fin, out):
        self.wire, self.place = wire, place
        self.src, self.got_y, self.mid, self.got_z = src, got_y, mid, got_z
        self.red, self.fin, self.out = red, fin, out

    def start(self):
        p = self.place
        self.y = self.wire.send(self.src.at[:, 1 - p.b], self.got_y, p.beside)

    def across(self):
        p = self.place
        self.y.wait_recv()
        self.mid[...] = (self.src[:, p.b].astype(F32) + self.got_y[...].astype(F32)).astype(self.mid.dtype)
        self.z = [
            self.wire.send(self.mid.at[:, lax.bitwise_xor(p.a, i)], self.got_z.at[i - 1], p.zdev(i))
            for i in range(1, p.na)
        ]

    def swap(self):
        p = self.place
        for cp in self.z:
            cp.wait_recv()
        acc = self.mid[:, p.a].astype(F32)
        for i in range(1, p.na):
            acc = acc + self.got_z[i - 1].astype(F32)
        self.red[...] = acc.astype(self.red.dtype)
        self.w = [
            self.wire.send(self.red.at[lax.bitwise_xor(p.f, i)], self.fin.at[p.f], p.fdev(i)) for i in range(1, p.nf)
        ]
        self.fin[p.f] = self.red[p.f]

    def spread(self):
        p = self.place
        for cp in self.w:
            cp.wait_recv()
        self.out[p.b, p.a] = self.fin[...]
        self.g = [(self.wire.send(self.fin, self.out.at[p.b, p.a], p.zdev(i)), i) for i in range(1, p.na)]
        self.h = [self.wire.send(self.fin, self.out.at[p.b, p.a], p.beside)]

    def forward(self):
        p = self.place
        for cp, i in self.g:
            cp.wait_recv()
            block = self.out.at[p.b, lax.bitwise_xor(p.a, i)]
            self.h.append(self.wire.send(block, block, p.beside))

    def finish(self):
        for cp in self.h:
            cp.wait_recv()


class Place:
    def __init__(self, nf, ns):
        self.f, self.s = here()
        self.nf, self.ns, self.na = nf, ns, ns // 2
        self.a, self.b = lax.div(self.s, 2), lax.rem(self.s, 2)
        self.core = lax.rem(self.f, 2)
        self.peer = (lax.bitwise_xor(self.f, 1), self.s)
        self.beside = (self.f, lax.bitwise_xor(self.s, 1))

    def fdev(self, i):
        return (lax.bitwise_xor(self.f, i), self.s)

    def zdev(self, i):
        return (self.f, lax.bitwise_xor(self.a, i) * 2 + self.b)


def small_layout(groups, rank, nstate, ns):
    select, step, decay, vectors = 0, 128, 128 + rank, 128 + rank + nstate
    group = vectors + 8
    piece = -(-group * groups // (8 * ns)) * 8
    return select, step, decay, vectors, group, piece


def post_kernel(nf, ns, nq, rd, rank, nstate, sems, *refs):
    (pulled_i, slopes_i, mix_i, step_i, dy_i, slope_i, ext_i, beg_i, normed_i, wi_i, wg_i, dgate_i) = refs[:12]
    (ce, proj, vecs, w_sel, w_step, table, x, ct, decay) = refs[12:21]
    gates = refs[21 : 21 + nq]
    refs = refs[21 + nq :]
    rout, gain_out, small_out = refs[:3]
    outs = refs[3 : 3 + 2 * nq]
    refs = refs[3 + 2 * nq :]
    (pulled, slopes, mix, step, dy, slope, ext, beg, normed, wi, wg, dgate) = refs[:12]
    (mixb, dlin, dproj, dib, part, got, mid, far, sums) = refs[12:21]
    dconv, dp = mix, normed
    (near_d, mid_d, far_d, gain_l, gain_f, gain_m, gain_y, gain_n, gain_z, small, small_y, small_m, small_z) = refs[21:34]
    (edge_o, edge_i) = refs[34:36]
    refs = refs[36:]
    inners = refs[:nq]
    refs = refs[nq:]
    bufs = [refs[n * 2 * nq : (n + 1) * 2 * nq] for n in range(5)]
    ssem, rsem, lsem, esem = refs[10 * nq :]

    place = Place(nf, ns)
    f, s, a, b, core = place.f, place.s, place.a, place.b, place.core
    na = place.na
    chips = list(range(2, nf, 2))
    groups, tokens, _ = pulled.shape
    ch = groups * 128
    stretch = tokens // (nf * rd)
    half = stretch // 2
    span_t = half * 8
    blocks = tokens // span_t
    width = normed.shape[1]
    off_select, off_step, off_decay, off_vec, group_rows, piece = small_layout(groups, rank, nstate, ns)
    has_up, has_down = s + 1 < ns, s >= 1
    greet(
        [(None, place.fdev(i)) for i in range(1, nf)]
        + [(None, place.beside)]
        + [(None, place.zdev(i)) for i in range(1, na)]
        + [(has_up, (f, s + 1)), (has_down, (f, s - 1))]
    )
    wire = Wire(ssem, rsem)
    streams = []
    for n in range(2 * nq):
        src = gates[n] if n < nq else inners[n - nq]
        streams.append(Stream(wire, place, src, *[v[n] for v in bufs], outs[n]))
    for n in range(nq):
        streams[n].start()

    loads = []

    def load(src, dst):
        cp = pltpu.make_async_copy(src, dst, lsem.at[len(loads)])
        loads.append(cp)
        cp.start()
        return cp

    hs = tokens // 2
    other, keep = (1 - core) * hs, core * hs
    first = [(pulled_i, pulled), (slopes_i, slopes), (mix_i, mix), (step_i, step), (dy_i, dy)]
    by_half = []
    for start in (other, keep):
        rows_ = rows_at(start, hs)
        by_half.append([load(src.at[:, rows_], dst.at[:, rows_]) for src, dst in first])
    conv_in = [load(slope_i, slope), load(ext_i, ext), load(beg_i, beg.at[pl.ds(0, beg_i.shape[0])])]
    late = [load(normed_i, normed), load(wi_i, wi), load(wg_i, wg), load(dgate_i, dgate)]
    for d in range(groups):
        small[d * group_rows + off_decay : d * group_rows + off_vec, :] = decay[d]
        small[d * group_rows + off_vec : (d + 1) * group_rows, :] = jnp.zeros((8, 128), F32)
    rest = small.shape[0] - groups * group_rows
    if rest:
        small[groups * group_rows :, :] = jnp.zeros((rest, 128), F32)
    beg[beg_i.shape[0] :, :] = jnp.zeros((24, 128), F32)

    chunk = 64

    def fold(v):
        out = v[0:8]
        for q in range(1, v.shape[0] // 8):
            out = out + v[q * 8 : (q + 1) * 8]
        return out

    def add_row(d, k, v):
        at_ = slice(d * group_rows + off_vec + k, d * group_rows + off_vec + k + 1)
        small[at_, :] += jnp.sum(v, axis=0, keepdims=True)

    zero = jnp.zeros((8, 128), F32)

    def step_half(start, cps):
        for cp in cps:
            cp.wait()
        for d in range(groups):

            def one(c, carry, d=d):
                at_ = rows_at(start + c * chunk, chunk)
                pu, m, st, dv = pulled[d, at_, :], mix[d, at_, :], step[d, at_, :], dy[d, at_, :]
                tiny = st * (1.0 - st * (0.5 - st * (1.0 / 6.0 - st * (1.0 / 24.0))))
                sig = jnp.where(st < 0.03, tiny, 1.0 - jnp.exp(-st))
                dpre = (m * pu + slopes[d, at_, :] * LN2) * sig
                low_at = rows_at(start + c * chunk, chunk, 16)
                dlin[d, low_at, :] = dpre.astype(BF16)
                mixb[d, low_at, :] = m.astype(BF16)
                pulled[d, at_, :] = st * pu + dv * vecs[d, 6:7, :]
                return carry[0] + fold(dpre), carry[1] + fold(dv * m)

            bias, skip = lax.fori_loop(0, hs // chunk, one, (zero, zero))
            add_row(d, 5, bias)
            add_row(d, 6, skip)
        at_ = rows_at(start, hs)
        total = None
        for d in range(groups):
            term = times_transposed(dlin[d, rows_at(start, hs, 16), :], w_step[:, cut(d)])
            total = term if total is None else total + term
        part[at_, :] = ce[at_, :]
        part[at_, :rank] += total

    step_half(other, by_half[0])
    one = wire.send(part.at[rows_at(other, hs)], got, place.peer)
    step_half(keep, by_half[1])
    one.wait_recv()
    mid[...] = part[rows_at(keep, hs), :] + got[...]
    two = [wire.send(mid, far.at[n], place.fdev(i)) for n, i in enumerate(chips)]

    for d in range(groups):
        low = proj[...][:, :rank].astype(BF16)
        small[d * group_rows + off_step : d * group_rows + off_decay, :] = rows_inner(low, dlin[d])
    for n in range(nq):
        streams[n].across()

    for cp in two:
        cp.wait_recv()
    acc = mid[...]
    for n in range(len(chips)):
        acc = acc + far[n]
    sums[rows_at(keep, hs), :] = acc
    three = wire.send(sums.at[rows_at(keep, hs)], sums.at[rows_at(keep, hs)], place.peer)
    for cp in conv_in:
        cp.wait()

    def mask_at(base, k):
        out = jnp.where(beg[rows_at(base + 16, chunk), :] > 0.0, 0.0, 1.0)
        if k <= 1:
            out = jnp.where(beg[rows_at(base + 8, chunk), :] > 0.0, 0.0, out)
        if k == 0:
            out = jnp.where(beg[rows_at(base, chunk), :] > 0.0, 0.0, out)
        return out

    def conv_half(start):
        at_all = rows_at(start, hs)
        low_all = rows_at(start, hs, 16)
        dproj[low_all, :] = sums[at_all, :].astype(BF16)
        for d in range(groups):
            slopes[d, at_all, :] = times_transposed(dproj[low_all, :], w_sel[d * 128 : (d + 1) * 128, :])

            def one(c, carry, d=d):
                row = start + c * chunk
                n, inside = split_at(row, span_t)
                at_ = rows_at(row, chunk)
                v = (pulled[d, at_, :] + slopes[d, at_, :]) * slope[d, at_, :]
                base = n * (span_t + LEAD)
                dconv[d, rows_at(base + inside, chunk), :] = v
                bb = n * (span_t + 16) + inside
                out = [carry[0] + fold(v)]
                for k in range(4):
                    tap = ext[d, rows_at(base + inside + k * 8, chunk), :]
                    w = v * tap if k == 3 else v * tap * mask_at(bb, k)
                    out.append(carry[1 + k] + fold(w))
                return tuple(out)

            totals = lax.fori_loop(0, hs // chunk, one, (zero,) * 5)
            add_row(d, 4, totals[0])
            for k in range(4):
                add_row(d, k, totals[1 + k])

    for n in range(blocks):
        for d in range(groups):
            dconv[d, n * (span_t + LEAD) + span_t : (n + 1) * (span_t + LEAD), :] = jnp.zeros((LEAD, 128), F32)
    conv_half(keep)
    three.wait_recv()
    conv_half(other)

    sub = lax.broadcasted_iota(jnp.int32, (8, 128), 0)
    for n in range(blocks):
        base = n * (span_t + LEAD)
        bb = n * (span_t + 16)
        hit = [jnp.where(beg[bb + q * 8 : bb + q * 8 + 8, :] > 0.0, 0.0, 1.0) for q in range(5)]
        for d in range(groups):
            tail = [zero] * 3
            for q in range(3):
                v = dconv[d, base + q * 8 : base + q * 8 + 8, :]
                keepers = [hit[q + 2] * hit[q + 1] * hit[q], hit[q + 2] * hit[q + 1], hit[q + 2]]
                for k in range(3 - q):
                    tail[q + k] = tail[q + k] + vecs[d, k : k + 1, :] * (v * keepers[k])
            for q in range(3):
                edge_o[d, n * 24 + q * 8 : n * 24 + q * 8 + 8, :] = tail[q]
    edge = remote(edge_o, edge_i, esem.at[0], esem.at[1], (f, s - 1))

    @pl.when(has_down)
    def _():
        edge.start()

    for n in range(nq):
        streams[n].swap()

    per = span_t // chunk

    def inner_chunk(idx, carry):
        nd, c = split_at(idx, per)
        n, d = split_at(nd, groups)
        base = n * (span_t + LEAD) + c * chunk
        bb = n * (span_t + 16) + c * chunk
        acc = vecs[d, 3:4, :] * dconv[d, rows_at(base, chunk), :]
        for k in range(3):
            ahead = (3 - k) * 8
            acc = acc + vecs[d, k : k + 1, :] * (dconv[d, rows_at(base + ahead, chunk), :] * mask_at(bb + ahead, k))
        pulled[d, rows_at(n * span_t + c * chunk, chunk), :] = acc
        return carry

    lax.fori_loop(0, blocks * groups * per, inner_chunk, 0)

    for d in range(groups):
        small[d * group_rows + off_select : d * group_rows + off_step, :] = rows_inner(mixb[d], dproj[...])
    small_half = na * piece
    small_ys = wire.send(small.at[rows_at((1 - b) * small_half, small_half)], small_y, place.beside)
    for n in range(nq):
        streams[n].spread()

    @pl.when(has_up)
    def _():
        edge.wait_recv()

    for n in range(blocks):
        for d in range(groups):
            for q in range(3):
                at_ = slice(n * 24 + q * 8, n * 24 + q * 8 + 8)
                inward = pltpu.roll(edge_o[d, at_, :], 7, 0)
                outer = jnp.where(has_up, pltpu.roll(edge_i[d, at_, :], 1, 0), 0.0)
                row = n * span_t + (half - 3 + q) * 8
                pulled[d, row : row + 8, :] += jnp.where(sub % 2 == 0, inward, outer)

    def to_rows(idx, carry):
        r_g, i = split_at(idx, half // 32)
        r, g = split_at(r_g, 2)
        n, q = split_at(r, 4)
        at_ = rows_at(r_g * half + i * 32, 32, 16)
        for d in range(groups):
            v = pulled[d, pl.ds(n * span_t + q * 2 + g + i * 256, 32, stride=8), :]
            dib[at_, cut(d)] = v.astype(BF16)
        return carry

    lax.fori_loop(0, 2 * nf * rd * (half // 32), to_rows, 0)

    for cp in late:
        cp.wait()
    drow = width // nf
    prow = drow // ns
    lanes = max(drow, 128)
    cq = ch // nq
    for q in range(nq):

        def grad_block(k, carry, q=q):
            v = rows_inner(normed[:, pl.ds(pl.multiple_of(k * lanes, 128), lanes)], dib[:, q * cq : (q + 1) * cq])
            for m in range(lanes // drow):
                for p in range(ns):
                    r = m * drow + p * prow
                    piece_v = v[r : r + prow].astype(inners[q].dtype)
                    inners[q][k * (lanes // drow) + m, p // na, p % na] = piece_v
            return carry

        lax.fori_loop(0, width // lanes, grad_block, 0)
        streams[nq + q].start()

    span = rd * stretch

    def dn_rows(flip):
        def one(n, carry):
            who = lax.bitwise_xor(lax.bitwise_xor(f, flip), 2 * n)
            for q in range(rd):
                at_ = rows_at(who * span + q * stretch, stretch, 16)
                v = times_transposed(dib[at_, :], wi[...]) + times_transposed(dgate[at_, :], wg[...])
                dp[at_, :] = v.astype(BF16)
            return carry

        lax.fori_loop(0, nf // 2, one, 0)

    def dp_rows(who):
        return rows_at(who * span, span, 16)

    dn_rows(1)
    near = [
        wire.send(dp.at[dp_rows(lax.bitwise_xor(lax.bitwise_xor(f, 1), i))], near_d.at[n], place.peer)
        for n, i in enumerate([0] + chips)
    ]
    dn_rows(0)
    fars = []
    for n, i in reversed(list(enumerate([0] + chips))):
        near[n].wait_recv()
        if i:
            dest = lax.bitwise_xor(f, i)
            mid_d[n - 1] = (dp[dp_rows(dest), :].astype(F32) + near_d[n].astype(F32)).astype(BF16)
            fars.append(wire.send(mid_d.at[n - 1], far_d.at[n - 1], place.fdev(i)))
    for n in range(nq):
        streams[n].forward()
    small_ys.wait_recv()
    small_m[...] = small[rows_at(b * small_half, small_half), :] + small_y[...]

    def owned(who):
        return rows_at(who * piece, piece)

    small_zs = [
        wire.send(small_m.at[owned(lax.bitwise_xor(a, i))], small_z.at[i - 1], place.zdev(i)) for i in range(1, na)
    ]
    for n in range(nq, 2 * nq):
        streams[n].across()

    gain = jnp.concatenate([table[q : q + 1, :] for q in range(width // 128)], axis=1)
    for cp in fars:
        cp.wait_recv()

    def own_rows(i, total):
        at_ = rows_at(i * 16, 16, 16)
        v = x[at_, :].astype(F32)
        scale = lax.rsqrt(jnp.sum(v * v, axis=1, keepdims=True) * (1.0 / width) + EPS)
        hat = v * scale
        dn = dp[rows_at(f * span + i * 16, 16, 16), :].astype(F32) + near_d[0, at_, :].astype(F32)
        for n in range(len(chips)):
            dn = dn + far_d[n, at_, :].astype(F32)
        dh = dn * gain
        inner = jnp.sum(dh * hat, axis=1, keepdims=True) * (1.0 / width)
        rout[at_, :] = ct[at_, :].astype(F32) + scale * (dh - hat * inner)
        return total + jnp.sum(dn * hat, axis=0, keepdims=True)

    gain_l[...] = lax.fori_loop(0, x.shape[0] // 16, own_rows, jnp.zeros((1, width), F32))
    gain_a = [wire.send(gain_l, gain_f.at[i - 1], place.fdev(i)) for i in range(1, nf)]
    for cp in small_zs:
        cp.wait_recv()
    acc = small_m[owned(a), :]
    for i in range(1, na):
        acc = acc + small_z[i - 1]
    mine = rows_at(b * small_half + a * piece, piece)
    small_out[mine, :] = acc
    small_g = [(wire.send(small_out.at[mine], small_out.at[mine], place.zdev(i)), i) for i in range(1, na)]
    small_h = [wire.send(small_out.at[mine], small_out.at[mine], place.beside)]
    for n in range(nq, 2 * nq):
        streams[n].swap()
    for cp in gain_a:
        cp.wait_recv()
    acc = gain_l[...]
    for i in range(1, nf):
        acc = acc + gain_f[i - 1]
    gain_m[...] = acc
    gain_b = wire.send(gain_m, gain_y, place.beside)
    for n in range(nq, 2 * nq):
        streams[n].spread()
    for cp, i in small_g:
        cp.wait_recv()
        theirs = rows_at(b * small_half + lax.bitwise_xor(a, i) * piece, piece)
        small_h.append(wire.send(small_out.at[theirs], small_out.at[theirs], place.beside))
    gain_b.wait_recv()
    gain_n[...] = gain_m[...] + gain_y[...]
    gain_c = [wire.send(gain_n, gain_z.at[i - 1], place.zdev(i)) for i in range(1, na)]
    for n in range(nq, 2 * nq):
        streams[n].forward()
    for cp in gain_c:
        cp.wait_recv()
    acc = gain_n[...]
    for i in range(1, na):
        acc = acc + gain_z[i - 1]
    gain_out[...] = acc
    for cp in small_h:
        cp.wait_recv()
    for st in streams:
        st.finish()
    wire.drain()

    @pl.when(has_down)
    def _():
        edge.wait_send()

    assert len(wire.copies) == sems


def post(nf, ns, nq, cid, rd, rank, nstate, big, little, gates):
    shape = jax.ShapeDtypeStruct
    v = pltpu.VMEM
    pulled, ext, beg, normed, wi = big[0], big[6], big[7], big[8], big[9]
    x = little[6]
    groups, tokens, _ = pulled.shape
    ch = groups * 128
    width = normed.shape[1]
    na = ns // 2
    chips = nf // 2 - 1
    block = x.shape
    piece_shape = gates[0].shape[3:]
    piece = small_layout(groups, rank, nstate, ns)[-1]
    total = piece * ns
    hs = tokens // 2
    blocks = tokens // BLOCK_TOKENS
    stream = 1 + (na - 1) + (nf - 1) + (na - 1) + 1 + (na - 1)
    sems = 2 * nq * stream
    sems += 2 + chips
    sems += 1 + 2 * chips
    sems += 1 + (na - 1) + (na - 1) + 1 + (na - 1)
    sems += (nf - 1) + 1 + (na - 1)
    outs = [shape(block, F32), shape((1, width), F32), shape((total, 128), F32)]
    kind = gates[0].dtype
    outs += [shape((2, na, nf) + piece_shape, kind)] * (2 * nq)
    scratch = [v(m.shape, m.dtype) for m in big]
    scratch[2] = v(ext.shape, F32)
    scratch[7] = v((beg.shape[0] + 24, 128), F32)
    scratch += [
        v(pulled.shape, BF16),
        v(pulled.shape, BF16),
        v((tokens, 128), BF16),
        v((tokens, ch), BF16),
        v((tokens, 128), F32),
        v((hs, 128), F32),
        v((hs, 128), F32),
        v((chips, hs, 128), F32),
        v((tokens, 128), F32),
        v((chips + 1,) + block, BF16),
        v((chips,) + block, BF16),
        v((chips,) + block, BF16),
        v((1, width), F32),
        v((nf - 1, 1, width), F32),
        v((1, width), F32),
        v((1, width), F32),
        v((1, width), F32),
        v((na - 1, 1, width), F32),
        v((total, 128), F32),
        v((na * piece, 128), F32),
        v((na * piece, 128), F32),
        v((na - 1, piece, 128), F32),
        v((groups, blocks * 24, 128), F32),
        v((groups, blocks * 24, 128), F32),
    ]
    scratch += [v(gates[0].shape, kind)] * nq
    scratch += [v((nf, na) + piece_shape, kind)] * (2 * nq)
    scratch += [v((nf, na) + piece_shape, kind)] * (2 * nq)
    scratch += [v((na - 1, nf) + piece_shape, kind)] * (2 * nq)
    scratch += [v((nf,) + piece_shape, kind)] * (2 * nq)
    scratch += [v((nf,) + piece_shape, kind)] * (2 * nq)
    scratch += [
        pltpu.SemaphoreType.DMA((sems,)),
        pltpu.SemaphoreType.DMA((sems,)),
        pltpu.SemaphoreType.DMA((17,)),
        pltpu.SemaphoreType.DMA((2,)),
    ]
    return pl.pallas_call(
        functools.partial(post_kernel, nf, ns, nq, rd, rank, nstate, sems),
        out_shape=outs,
        in_specs=[ANY] * 12 + [VMEM] * (9 + nq),
        out_specs=[VMEM] * len(outs),
        scratch_shapes=scratch,
        compiler_params=comm_params(cid, 63 << 20),
        name="post",
    )(*big, *little, *gates)


def rows_inner(left, right):
    return lax.dot_general(left, right, (((0,), (0,)), ((), ())), preferred_element_type=F32)


def times_transposed(left, right):
    return lax.dot_general(left, right, (((1,), (1,)), ((), ())), preferred_element_type=F32)


def silu_slope(value):
    sig = jax.nn.sigmoid(value)
    return sig * (1.0 + value * (1.0 - sig))


def shards(
    nf,
    ns,
    residual,
    out_cotangent,
    doc_lengths,
    norm_gain,
    input_proj,
    conv_kernel,
    conv_bias,
    select_proj,
    step_proj,
    step_bias,
    log_decay,
    skip_gain,
    output_proj,
):
    rd, stretch, width = residual.shape
    rows = nf * rd
    docs = doc_lengths.shape[1]
    ch = conv_bias.shape[0]
    rank = step_proj.shape[0]
    nstate = log_decay.shape[0]
    taps = conv_kernel.shape[0]
    edge = taps - 1
    tokens = rows * stretch
    half = stretch // 2
    blocks = rows // 4
    f, s = here()
    reach = -(-(stretch * ns // 2 - 1) // stretch)
    count = 4

    groups = ch // 128
    grows = norm_gain.shape[0]
    spot = lax.broadcasted_iota(jnp.int32, (width,), 0) // grows == f
    small = jnp.where(spot, jnp.tile(norm_gain.astype(F32), nf), 0.0).reshape(width // 128, 128)
    marks = jnp.pad(doc_lengths.astype(F32), ((0, 8 - rd), (0, 128 - docs)))
    small = jnp.concatenate([small, marks], axis=0)
    vecs = jnp.concatenate(
        [conv_kernel, conv_bias[None], step_bias[None], skip_gain[None], jnp.zeros((1, ch), BF16)], axis=0
    ).astype(F32)
    vecs = jnp.moveaxis(vecs.reshape(8, groups, 128), 1, 0)
    w_sel = jnp.pad(select_proj, ((0, 0), (0, 128 - select_proj.shape[1])))
    normed, cot, ext, slope, mix, dy, ga, dgs, step, beg, proj, packed, w_inner, w_gate, gain = front(
        nf, ns, residual, out_cotangent, input_proj, small, vecs, w_sel, step_proj, output_proj, rank, nstate
    )
    rate = -jnp.exp(log_decay.astype(F32))
    rate2 = rate * LOG2E

    def stacked(v):
        return v.reshape((blocks, half, 8) + v.shape[1:])

    b, p, g = scan_ends(step, mix, dy, beg, packed, rate2, count)
    resets = beg.reshape(blocks, half + 2, 8, 128)[:, 2:].max(axis=1)[:, :, :1]
    run = jnp.moveaxis(jnp.sum(step.reshape(groups, blocks, half, 8, 128), axis=2), 0, 2).reshape(blocks, 8, ch) + resets

    def halves(v):
        v = v.reshape(v.shape[:-2] + (4, 2, ch))
        return v[..., 0, :], v[..., 1, :]

    b0, b1 = halves(b)
    p0, p1 = halves(p)
    g0, g1 = halves(g)
    r0, r1 = halves(run)
    flat = (blocks * nstate * 4, ch)
    bf, gb, tf, tb = carry_over_seq(
        reach,
        ns,
        2,
        (p1 * b0 + b1).astype(BF16).reshape(flat),
        (g0 + p0 * g1).astype(BF16).reshape(flat),
        (r0 + r1).reshape(blocks * 4, ch),
    )
    state_shape = (blocks, nstate, 4, ch)

    def gathered(ends, sums, valid):
        state = jnp.zeros(state_shape, F32)
        for j in range(reach - 1, -1, -1):
            decay = jnp.exp2(rate2[None, :, None, :] * sums[j].reshape(blocks, 1, 4, ch))
            new = decay * state + ends[j].reshape(state_shape).astype(F32)
            state = jnp.where(valid(j + 1), new, 0.0)
        return state

    h_first = gathered(bf, tf, lambda j: s - j >= 0)
    l_last = gathered(gb, tb, lambda j: s + j < ns)
    hin = jnp.stack([h_first, p0 * h_first + b0], axis=3).reshape(blocks, nstate, 8, ch)
    lin = jnp.stack([g1 + p1 * l_last, l_last], axis=3).reshape(blocks, nstate, 8, ch)

    gated, d_gate, states, coef_read = scan_forward(step, mix, dy, beg, packed, rate2, hin, ga, dgs, vecs, rank, count)
    nq = 2 if ch % 256 == 0 else 1
    cq = ch // nq
    piece_rows = width // nf // ns
    kind = BF16
    output_grad = rows_inner(gated, cot).astype(BF16)
    out_part = jnp.dot(gated, output_proj, preferred_element_type=F32).astype(BF16)
    gate_grads = [
        rows_inner(normed, d_gate[:, q * cq : (q + 1) * cq]).astype(kind).reshape(nf, 2, ns // 2, piece_rows, cq)
        for q in range(nq)
    ]
    output_grad, out_part, lin, *gate_grads = lax.optimization_barrier((output_grad, out_part, lin, *gate_grads))
    output_grad = lax.psum(output_grad, "seq")
    out_sum = lax.psum_scatter(out_part, "fsdp", scatter_dimension=0, tiled=True)

    pulled, slopes, coefs, decay = scan_backward(step, mix, dy, beg, packed, rate2, lin, states, coef_read, rank, count)
    big = (pulled, slopes, mix, step, dy, slope, ext, beg, normed, w_inner, w_gate, d_gate)
    little = (
        coefs,
        proj,
        vecs,
        w_sel,
        step_proj,
        gain,
        residual.reshape(rd * stretch, width),
        out_cotangent.reshape(rd * stretch, width),
        decay,
    )
    residual_grad, gain_sum, small_sum, *sums = post(nf, ns, nq, 3, rd, rank, nstate, big, little, gate_grads)
    layer_output = (residual.reshape(rd * stretch, width).astype(F32) + out_sum.astype(F32)).astype(BF16)

    def side(parts):
        parts = [v.reshape(ns, nf, piece_rows, cq) for v in parts]
        return jnp.moveaxis(jnp.concatenate(parts, axis=3), 1, 2).reshape(width // nf, nf * ch)

    input_grad = jnp.concatenate([side(sums[nq:]), side(sums[:nq])], axis=1).astype(F32)
    off_select, off_step, off_decay, off_vec, group_rows, _ = small_layout(groups, rank, nstate, ns)
    small_sum = small_sum[: groups * group_rows].reshape(groups, group_rows, 128)

    def section(start, count_):
        return jnp.moveaxis(small_sum[:, start : start + count_], 0, 1).reshape(count_, ch)

    vectors = section(off_vec, 8)
    return (
        layer_output.reshape(rd, stretch, width),
        residual_grad.reshape(rd, stretch, width),
        lax.dynamic_slice(gain_sum[0], (f * grows,), (grows,)),
        input_grad,
        vectors[:4],
        vectors[4],
        small_sum[:, :off_step, : select_proj.shape[1]].reshape(ch, select_proj.shape[1]),
        section(off_step, rank),
        vectors[5],
        section(off_decay, nstate),
        vectors[6],
        output_grad.astype(F32),
    )


def solution(mesh):
    nf, ns = mesh.shape["fsdp"], mesh.shape["seq"]
    in_specs = (
        P("fsdp", "seq", None),
        P("fsdp", "seq", None),
        P("fsdp", None),
        P("fsdp"),
        P("fsdp", None),
        P(None, "fsdp"),
        P("fsdp"),
        P("fsdp", None),
        P(None, "fsdp"),
        P("fsdp"),
        P(None, "fsdp"),
        P("fsdp"),
        P("fsdp", None),
    )
    out_specs = (
        P("fsdp", "seq", None),
        P("fsdp", "seq", None),
        P("fsdp"),
        P("fsdp", None),
        P(None, "fsdp"),
        P("fsdp"),
        P("fsdp", None),
        P(None, "fsdp"),
        P("fsdp"),
        P(None, "fsdp"),
        P("fsdp"),
        P("fsdp", None),
    )
    return jax.shard_map(
        functools.partial(shards, nf, ns), mesh=mesh, in_specs=in_specs, out_specs=out_specs, check_vma=False
    )
```

```python
import functools
import math

import jax
import jax.numpy as jnp
from jax import lax
from jax.experimental import pallas as pl
from jax.experimental.pallas import tpu as pltpu
from jax.sharding import PartitionSpec as P

EPS = 1e-05
MESH = pl.DeviceIdType.MESH
LOG2E = math.log2(math.e)
LN2 = math.log(2.0)
BF16 = jnp.bfloat16
F32 = jnp.float32
ANY = pl.BlockSpec(memory_space=pl.ANY)
VMEM = pl.BlockSpec(memory_space=pltpu.VMEM)
RESET = 1e30
HALO = 16
DOCS = 8


def here():
    return lax.axis_index("fsdp"), lax.axis_index("seq")


def greet(peers):
    barrier = pltpu.get_barrier_semaphore()
    count = 0
    for ok, device in peers:
        if ok is None:
            pl.semaphore_signal(barrier, inc=1, device_id=device, device_id_type=MESH)
            count = count + 1
        else:

            @pl.when(ok)
            def _():
                pl.semaphore_signal(barrier, inc=1, device_id=device, device_id_type=MESH)

            count = count + ok.astype(jnp.int32)
    pl.semaphore_wait(barrier, count)


def remote(src, dst, send, recv, device):
    return pltpu.make_async_remote_copy(
        src_ref=src, dst_ref=dst, send_sem=send, recv_sem=recv, device_id=device, device_id_type=MESH
    )


def comm_params(cid, vmem=None):
    return pltpu.CompilerParams(collective_id=cid, has_side_effects=True, vmem_limit_bytes=vmem)


class Wire:
    def __init__(self, ssem, rsem):
        self.ssem, self.rsem, self.copies, self.done = ssem, rsem, [], []

    def send(self, src, dst, device):
        k = len(self.copies)
        cp = remote(src, dst, self.ssem.at[k], self.rsem.at[k], device)
        self.copies.append(cp)
        cp.start()
        return cp

    def sent(self, cp):
        cp.wait_send()
        self.done.append(cp)

    def drain(self):
        for cp in self.copies:
            if all(cp is not other for other in self.done):
                cp.wait_send()


LEAD = 24


def rows_at(base, size, unit=8):
    return pl.ds(pl.multiple_of(base, unit), size)


def split_at(i, n):
    return lax.div(i, n), lax.rem(i, n)


def front_kernel(nf, ns, rd, rank, nstate, sems, *refs):
    (x, ct, w, sm, vecs, w_sel, w_step, w_out) = refs[:8]
    (normed_o, cg_o, ext_o, slope_o, mix_o, dy_o, ga_o, dgs_o, step_o, beg_o, proj_o, packed_o, wi_o, wg_o, gain_o) = refs[8:23]
    (xg, cg, wi, wg, sg, hal, hres, vbuf, gbuf, ext, slope, mix, mixb, dy, ga, dgs, step, beg, part, got, mid, far, proj, packed) = refs[
        23:47
    ]
    ssem, rsem, hsem, hrem, lsem, osem = refs[47:]
    f, s = here()
    core, b = lax.rem(f, 2), lax.rem(s, 2)
    stretch = x.shape[1]
    half = stretch // 2
    dmodel = xg.shape[1]
    ch = wi.shape[1]
    groups = ch // 128
    rows = nf * rd
    blocks = rows // 4
    tokens = rows * stretch
    drow = w.shape[0]
    inner_all = w.shape[1] // 2
    chips = list(range(2, nf, 2))
    peer = (lax.bitwise_xor(f, 1), s)
    beside = (f, lax.bitwise_xor(s, 1))
    up, down = s + 1, s - 1
    has_up, has_down = up < ns, down >= 0

    def fdev(i):
        return (lax.bitwise_xor(f, i), s)

    greeted = [(None, fdev(i)) for i in range(1, nf)] + [(None, beside)]
    for i in range(nf):
        greeted.append((has_up, (lax.bitwise_xor(f, i), up)))
        greeted.append((has_down, (lax.bitwise_xor(f, i), down)))
    greet(greeted)
    wire = Wire(ssem, rsem)

    def act_rows(who):
        return rows_at(who * (rd * stretch), rd * stretch, 16)

    def wcols(who, base, start, size):
        return w.at[pl.ds(start, size), pl.ds(pl.multiple_of(base + who * ch, 128), ch)]

    def wrows(who, start, size):
        return pl.ds(pl.multiple_of(who * drow + start, 16), size)

    half_rows = drow // 2
    mine = pl.multiple_of(b * half_rows, 16)

    locals_ = []

    def local(src, dst):
        cp = pltpu.make_async_copy(src, dst, lsem.at[len(locals_)])
        locals_.append(cp)
        cp.start()
        return cp

    x2 = [x.at[q] for q in range(rd)]
    smalls = [wire.send(sm, sg.at[f], fdev(i)) for i in range(1, nf)]
    own_x = [local(x2[q], xg.at[rows_at((f * rd + q) * stretch, stretch, 16)]) for q in range(rd)]
    own_s = local(sm, sg.at[f])

    def send_rows(src, dst):
        if rd == 1:
            return [wire.send(src.at[0], dst.at[act_rows(f)], fdev(i)) for i in [1] + chips]
        return [wire.send(src, dst.at[act_rows(f)], fdev(i)) for i in [1] + chips]

    def send_weight(base, dst):
        out = [wire.send(wcols(peer[0], base, 0, drow), dst.at[wrows(f, 0, drow)], peer)]
        for i in range(2, nf):
            out.append(
                wire.send(wcols(lax.bitwise_xor(f, i), base, mine, half_rows), dst.at[wrows(f, mine, half_rows)], fdev(i))
            )
        return out

    xs = send_rows(x, xg)
    wis = send_weight(0, wi)
    halos = [
        remote(
            x.at[:, pl.ds(stretch - HALO, HALO), :],
            hal.at[pl.ds(f * rd, rd)],
            hsem.at[i],
            hrem.at[i],
            (lax.bitwise_xor(f, i), up),
        )
        for i in range(nf)
    ]

    @pl.when(has_up)
    def _():
        for cp in halos:
            cp.start()

    own_wi = local(wcols(f, 0, 0, drow), wi.at[wrows(f, 0, drow)])
    cs = send_rows(ct, cg)
    wgs = send_weight(inner_all, wg)
    own_c = [local(ct.at[q], cg.at[rows_at((f * rd + q) * stretch, stretch, 16)]) for q in range(rd)]
    own_wg = local(wcols(f, inner_all, 0, drow), wg.at[wrows(f, 0, drow)])

    own_s.wait()
    for cp in smalls:
        cp.wait_recv()
    table = sg[0]
    for k in range(1, nf):
        table = table + sg[k]
    gain = jnp.concatenate([table[q : q + 1, :] for q in range(dmodel // 128)], axis=1)
    gain_o[...] = table
    sub = lax.broadcasted_iota(jnp.int32, (8, 128), 0)
    for n in range(blocks):
        lens = jnp.zeros((8, 128), F32)
        for q in range(4):
            r = n * 4 + q
            line = sg[r // rd, 8 + r % rd : 9 + r % rd, :]
            lens = jnp.where(sub // 2 == q, jnp.broadcast_to(line, (8, 128)), lens)
        starts = [jnp.zeros((8, 128), F32)]
        for j in range(DOCS - 1):
            starts.append(starts[-1] + jnp.broadcast_to(lens[:, j : j + 1], (8, 128)))
        first = (s * stretch + (sub % 2) * half).astype(F32)

        def mark(t, carry, n=n, starts=starts, first=first):
            place = first + (t - 2).astype(F32)
            hit = starts[0] == place
            for j in range(1, DOCS):
                hit = jnp.logical_or(hit, starts[j] == place)
            beg[rows_at(n * (half + 2) * 8 + t * 8, 8), :] = jnp.where(hit, RESET, 0.0)
            return carry

        lax.fori_loop(0, half + 2, mark, 0)

    def norm_rows(ref, start, size):
        def one(i, carry):
            at_ = rows_at(start + i * 32, 32, 16)
            v = ref[at_, :].astype(F32)
            scale = lax.rsqrt(jnp.sum(v * v, axis=1, keepdims=True) * (1.0 / dmodel) + EPS)
            ref[at_, :] = (v * scale * gain).astype(BF16)
            return carry

        lax.fori_loop(0, size // 32, one, 0)

    span = rd * stretch
    for cp in own_x:
        cp.wait()
    norm_rows(xg, f * span, span)
    xs[0].wait_recv()
    norm_rows(xg, peer[0] * span, span)
    xf = []
    for n, i in enumerate(chips):
        xs[1 + n].wait_recv()
        block = act_rows(lax.bitwise_xor(f, i))
        xf.append(wire.send(xg.at[block], xg.at[block], peer))
    for n, i in enumerate(chips):
        xf[n].wait_recv()
        norm_rows(xg, lax.bitwise_xor(f, i + 1) * span, span)
        wire.sent(xf[n])
        norm_rows(xg, lax.bitwise_xor(f, i) * span, span)
    wif = []
    for n, i in enumerate(range(2, nf)):
        wis[1 + n].wait_recv()
        block = wrows(lax.bitwise_xor(f, i), mine, half_rows)
        wif.append(wire.send(wi.at[block], wi.at[block], beside))

    @pl.when(has_down)
    def _():
        for cp in halos:
            cp.wait_recv()

    hal_rows = rows * HALO
    hflat = vbuf
    for r in range(rows):
        v = hal[r].astype(F32)
        scale = lax.rsqrt(jnp.sum(v * v, axis=1, keepdims=True) * (1.0 / dmodel) + EPS)
        hflat[r * HALO : (r + 1) * HALO, :] = jnp.where(s > 0, v * scale * gain, 0.0).astype(BF16)
    own_wi.wait()
    wis[0].wait_recv()
    for cp in wif:
        cp.wait_recv()
    out_copies = []

    def put(src, dst):
        cp = pltpu.make_async_copy(src, dst, osem.at[len(out_copies)])
        out_copies.append(cp)
        cp.start()

    put(xg, normed_o)
    put(beg, beg_o)
    put(wi, wi_o)

    def inner_row(r, carry):
        v = jnp.dot(xg[rows_at(r * stretch, stretch, 16), :], wi[...], preferred_element_type=F32)
        v = v.astype(BF16).astype(F32)
        n, q = split_at(r, 4)
        base = n * (half * 8 + LEAD) + LEAD + q * 2
        for g in range(2):
            for d in range(groups):
                ext[d, pl.ds(base + g, half, stride=8), :] = v[g * half : (g + 1) * half, cut(d)]
        return carry

    lax.fori_loop(0, rows, inner_row, 0)
    hv = jnp.dot(hflat[...], wi[...], preferred_element_type=F32).astype(BF16).astype(F32)
    for d in range(groups):
        hres[d] = hv[:, cut(d)]
    for n in range(blocks):
        base = n * (half * 8 + LEAD)
        for d in range(groups):
            for j in range(3):
                before = hres[d, pl.ds(n * 4 * HALO + HALO - 3 + j, 4, stride=HALO), :]
                ext[d, pl.ds(base + j * 8, 4, stride=2), :] = before
                own = ext[d, pl.ds(base + LEAD + (half - 3 + j) * 8, 4, stride=2), :]
                ext[d, pl.ds(base + j * 8 + 1, 4, stride=2), :] = own
    put(ext, ext_o)

    span_t = half * 8
    chunk = 64
    per = span_t // chunk

    def conv_chunk(idx, carry):
        nd, c = split_at(idx, per)
        n, d = split_at(nd, groups)
        base = n * (span_t + LEAD) + c * chunk
        bb = n * (span_t + 16) + c * chunk
        same2 = jnp.where(beg[rows_at(bb + 16, chunk), :] > 0.0, 0.0, 1.0)
        same1 = jnp.where(beg[rows_at(bb + 8, chunk), :] > 0.0, 0.0, same2)
        same0 = jnp.where(beg[rows_at(bb, chunk), :] > 0.0, 0.0, same1)
        tap = [ext[d, rows_at(base + k * 8, chunk), :] for k in range(4)]
        v = vecs[d, 4:5, :] + vecs[d, 0:1, :] * (tap[0] * same0)
        v = v + vecs[d, 1:2, :] * (tap[1] * same1) + vecs[d, 2:3, :] * (tap[2] * same2) + vecs[d, 3:4, :] * tap[3]
        sig = jax.nn.sigmoid(v)
        m = (v * sig).astype(BF16)
        at_ = rows_at(n * span_t + c * chunk, chunk)
        slope[d, at_, :] = sig * (1.0 + v * (1.0 - sig))
        mixb[d, rows_at(n * span_t + c * chunk, chunk, 16), :] = m
        mix[d, at_, :] = m.astype(F32)
        return carry

    lax.fori_loop(0, blocks * groups * per, conv_chunk, 0)
    put(slope, slope_o)
    put(mix, mix_o)

    hs = tokens // 2
    other = (1 - core) * hs
    keep = core * hs

    def project(start):
        total = None
        for d in range(groups):
            term = jnp.dot(mixb[d, rows_at(start, hs, 16), :], w_sel[d * 128 : (d + 1) * 128, :], preferred_element_type=F32)
            total = term if total is None else total + term
        part[rows_at(start, hs), :] = total

    project(other)
    one = wire.send(part.at[rows_at(other, hs)], got, peer)
    project(keep)
    one.wait_recv()
    mid[...] = part[rows_at(keep, hs), :] + got[...]
    two = [wire.send(mid, far.at[n], fdev(i)) for n, i in enumerate(chips)]

    cf = []
    for n, i in enumerate(chips):
        cs[1 + n].wait_recv()
        block = act_rows(lax.bitwise_xor(f, i))
        cf.append(wire.send(cg.at[block], cg.at[block], peer))
    wgf = []
    for n, i in enumerate(range(2, nf)):
        wgs[1 + n].wait_recv()
        block = wrows(lax.bitwise_xor(f, i), mine, half_rows)
        wgf.append(wire.send(wg.at[block], wg.at[block], beside))
    for cp in own_c + [own_wg]:
        cp.wait()
    for cp in [cs[0], wgs[0]] + cf + wgf:
        cp.wait_recv()
    put(cg, cg_o)
    put(wg, wg_o)

    def gate_row(r, carry):
        at_ = rows_at(r * stretch, stretch, 16)
        gbuf[0] = jnp.dot(xg[at_, :], wg[...], preferred_element_type=F32).astype(BF16).astype(F32)
        gbuf[1] = times_transposed(cg[at_, :], w_out[...]).astype(BF16).astype(F32)
        n, q = split_at(r, 4)
        base = n * span_t + q * 2
        for g in range(2):
            for d in range(groups):
                def some(i, carry2, g=g, d=d):
                    src = rows_at(g * half + i * 32, 32)
                    v, dg = gbuf[0, src, cut(d)], gbuf[1, src, cut(d)]
                    sig = jax.nn.sigmoid(v)
                    act = v * sig
                    dst = rows_at(r * stretch + g * half + i * 32, 32)
                    ga[dst, cut(d)] = act
                    dgs[dst, cut(d)] = dg * (sig * (1.0 + v * (1.0 - sig)))
                    dy[d, pl.ds(base + g + i * 256, 32, stride=8), :] = dg * act
                    return carry2

                lax.fori_loop(0, half // 32, some, 0)
        return carry

    lax.fori_loop(0, rows, gate_row, 0)
    put(dy, dy_o)
    put(ga, ga_o)
    put(dgs, dgs_o)

    for cp in two:
        cp.wait_recv()
    acc = mid[...]
    for n in range(len(chips)):
        acc = acc + far[n]
    proj[rows_at(keep, hs), :] = acc
    three = wire.send(proj.at[rows_at(keep, hs)], proj.at[rows_at(keep, hs)], peer)

    lane = lax.broadcasted_iota(jnp.int32, (256, 128), 1)

    def step_rows(i, carry):
        at_ = rows_at(carry + i * 256, 256)
        p = proj[at_, :]
        pre = jnp.dot(p[:, :rank].astype(BF16), w_step[...], preferred_element_type=F32)
        for d in range(groups):
            v = pre[:, cut(d)] + vecs[d, 5:6, :]
            step[d, at_, :] = jnp.maximum(v, 0.0) + jnp.log1p(jnp.exp(-jnp.abs(v)))
        top = p.astype(BF16)
        rest = p - top.astype(F32)
        second = rest.astype(BF16)
        third = (rest - second.astype(F32)).astype(BF16).astype(F32)
        width = 2 * nstate
        out = pltpu.roll(top.astype(F32), 128 - rank, 1)
        out = jnp.where(lane < width, out, pltpu.roll(second.astype(F32), (128 - rank + width) % 128, 1))
        out = jnp.where(lane < 2 * width, out, pltpu.roll(third, (128 - rank + 2 * width) % 128, 1))
        packed[rows_at(carry + i * 256, 256, 16), :] = jnp.where(lane < 3 * width, out, 0.0).astype(BF16)
        return carry

    lax.fori_loop(0, hs // 256, step_rows, keep)
    three.wait_recv()
    lax.fori_loop(0, hs // 256, step_rows, other)
    put(step, step_o)
    put(proj, proj_o)
    put(packed, packed_o)
    for cp in out_copies:
        cp.wait()
    wire.drain()

    @pl.when(has_up)
    def _():
        for cp in halos:
            cp.wait_send()

    assert len(wire.copies) == sems


def front(nf, ns, x, ct, w, sm, vecs, w_sel, w_step, w_out, rank, nstate):
    rd, stretch, width = x.shape
    drow = w.shape[0]
    ch = w_step.shape[1]
    groups = ch // 128
    rows = nf * rd
    blocks = rows // 4
    tokens = rows * stretch
    half = stretch // 2
    chips = nf // 2 - 1
    ext_rows = blocks * (half * 8 + LEAD)
    beg_rows = blocks * (half + 2) * 8
    sems = 0
    sems += nf - 1
    sems += 2 * (1 + chips)
    sems += 2 * (nf - 1)
    sems += 2 * chips + 2 * (nf - 2)
    sems += 2 + chips
    shape = jax.ShapeDtypeStruct
    wide = (groups, tokens, 128)
    out_shape = (
        shape((tokens, width), BF16),
        shape((tokens, width), BF16),
        shape((groups, ext_rows, 128), F32),
        shape(wide, F32),
        shape(wide, F32),
        shape(wide, F32),
        shape((tokens, ch), F32),
        shape((tokens, ch), F32),
        shape(wide, F32),
        shape((beg_rows, 128), F32),
        shape((tokens, 128), F32),
        shape((tokens, 128), BF16),
        shape((width, ch), BF16),
        shape((width, ch), BF16),
        shape((16, 128), F32),
    )
    v = pltpu.VMEM
    scratch = [
        v((tokens, width), BF16),
        v((tokens, width), BF16),
        v((width, ch), BF16),
        v((width, ch), BF16),
        v((nf, 16, 128), F32),
        v((rows, HALO, width), BF16),
        v((groups, rows * HALO, 128), F32),
        v((rows * HALO, width), BF16),
        v((2, stretch, ch), F32),
        v((groups, ext_rows, 128), F32),
        v(wide, F32),
        v(wide, F32),
        v(wide, BF16),
        v(wide, F32),
        v((tokens, ch), F32),
        v((tokens, ch), F32),
        v(wide, F32),
        v((beg_rows, 128), F32),
        v((tokens, 128), F32),
        v((tokens // 2, 128), F32),
        v((tokens // 2, 128), F32),
        v((chips, tokens // 2, 128), F32),
        v((tokens, 128), F32),
        v((tokens, 128), BF16),
        pltpu.SemaphoreType.DMA((sems,)),
        pltpu.SemaphoreType.DMA((sems,)),
        pltpu.SemaphoreType.DMA((nf,)),
        pltpu.SemaphoreType.DMA((nf,)),
        pltpu.SemaphoreType.DMA((2 * rd + 3,)),
        pltpu.SemaphoreType.DMA((14,)),
    ]
    return pl.pallas_call(
        functools.partial(front_kernel, nf, ns, rd, rank, nstate, sems),
        out_shape=out_shape,
        in_specs=[ANY] * 4 + [VMEM] * 4,
        out_specs=[ANY] * 14 + [VMEM],
        scratch_shapes=scratch,
        compiler_params=comm_params(0, 62 << 20),
        name="front",
    )(x, ct, w, sm, vecs, w_sel, w_step, w_out)


BLOCK_TOKENS = 1024


def at(t):
    return pl.ds(pl.multiple_of(t * 8, 8), 8)


def cut(d):
    return slice(d * 128, (d + 1) * 128)


def pieces(v, count):
    out = []
    for _ in range(count):
        top = v.astype(BF16)
        out.append(top)
        v = v - top.astype(F32)
    return out


def spread_coefs(packed, cscr, first, count, nstate):
    wide = 2 * count * 128
    source = lax.broadcasted_iota(jnp.int32, (128, wide), 0)
    block = lax.broadcasted_iota(jnp.int32, (128, wide), 1) // 128
    want = jnp.where(block < count, block, nstate - count + block) + first
    pick = jnp.where(
        jnp.logical_and(source % (2 * nstate) == want, source < 6 * nstate), 1.0, 0.0
    ).astype(BF16)
    cscr[...] = jnp.dot(packed, pick, preferred_element_type=F32)


ENDS_UNROLL = 4
SCAN_UNROLL = 4


def scan_specs(tokens, ch, nstate, count):
    blocks = tokens // BLOCK_TOKENS
    groups = ch // 128
    steps = BLOCK_TOKENS // 8
    tok = pl.BlockSpec((groups, BLOCK_TOKENS, 128), lambda n, j: (0, n, 0))
    narrow = pl.BlockSpec((BLOCK_TOKENS, 128), lambda n, j: (n, 0))
    marks = pl.BlockSpec((BLOCK_TOKENS + 16, 128), lambda n, j: (n, 0))
    rates = pl.BlockSpec((1, count, ch), lambda n, j: (j, 0, 0))
    state = pl.BlockSpec((1, count, 8, ch), lambda n, j: (n, j, 0, 0))
    flat = pl.BlockSpec((BLOCK_TOKENS, ch), lambda n, j: (n, 0))
    grid = (blocks, nstate // count)
    kept = pl.BlockSpec((1, steps, count * groups, 8, 128), lambda n, j: (n * grid[1] + j, 0, 0, 0, 0))
    kept_shape = jax.ShapeDtypeStruct((math.prod(grid), steps, count * groups, 8, 128), F32)
    return grid, groups, tok, narrow, marks, rates, state, flat, kept, kept_shape


def rates_of(rate, keys):
    return [jnp.broadcast_to(rate[0, i : i + 1, cut(d)], (8, 128)) for d, i in keys]


def lane_sums(seen, coef, count, first):
    wide = count * 128
    block = lax.broadcasted_iota(jnp.int32, (wide, 128), 0) // 128
    column = lax.broadcasted_iota(jnp.int32, (wide, 128), 1)
    ones = jnp.where(column == block + first, 1.0, 0.0).astype(BF16)
    for part in pieces(seen[...], 2):
        coef[...] += jnp.dot(part, ones, preferred_element_type=F32)


def mid_kernel(nf, ns, reach, count, rank, nstate, *refs):
    (step, mix, dy, beg, packed, rate, vecs, ga_i, dgs_i) = refs[:9]
    (gated, dgate, states_o, coef, lin_o) = refs[9:14]
    (cscr, seen, y, keep, bsc, psc, gsc, run, b_out, g_out, b_in, g_in, t_out, t_up, t_down, ga, dgs) = refs[14:31]
    ssem, rsem, tsem, tsem2, ksem, lsem = refs[31:]
    f, s = here()
    groups = step.shape[0]
    blocks = step.shape[1] // BLOCK_TOKENS
    steps = BLOCK_TOKENS // 8
    parts = nstate // count
    keys = [(d, i) for d in range(groups) for i in range(count)]
    size = len(keys)
    sub = lax.broadcasted_iota(jnp.int32, (8, 128), 0)
    odd = sub % 2 == 1
    zero = jnp.zeros((8, 128), F32)
    slots = parts if blocks == 1 else 1

    peers = []
    for q in range(1, reach + 1):
        peers.append((s + q < ns, (f, s + q)))
        peers.append((s - q >= 0, (f, s - q)))
    greet(peers)
    loads = [pltpu.make_async_copy(ga_i, ga, lsem.at[0]), pltpu.make_async_copy(dgs_i, dgs, lsem.at[1])]
    for cp in loads:
        cp.start()

    def each_way(q, up, down):
        @pl.when(s + q < ns)
        def _():
            up()

        @pl.when(s - q >= 0)
        def _():
            down()

    def starts(cps):
        for cp in cps:
            cp.start()

    def rates(j):
        return [jnp.broadcast_to(rate[d, j * count + i : j * count + i + 1, :], (8, 128)) for d, i in keys]

    def tokens_of(n):
        return slice(n * BLOCK_TOKENS, (n + 1) * BLOCK_TOKENS)

    def row(n, t):
        return rows_at(n * BLOCK_TOKENS + t * 8, 8)

    def marks(n, t):
        return beg[rows_at(n * (BLOCK_TOKENS + 16) + 16 + t * 8, 8), :]

    def pair_up(values, side):
        out = []
        for k in range(0, len(values), 2):
            one, two = values[k], values[k + 1]
            if side:
                out.append(jnp.where(odd, one, pltpu.roll(two, 7, 0)))
            else:
                out.append(jnp.where(odd, pltpu.roll(two, 1, 0), one))
        return out

    def both_rows(v, side):
        return jnp.where(odd, v, pltpu.roll(v, 7, 0)) if side else jnp.where(odd, pltpu.roll(v, 1, 0), v)

    carries = []
    for n in range(blocks):
        for j in range(parts):
            slot = j if blocks == 1 else 0
            spread_coefs(packed[tokens_of(n), :], cscr.at[slot], j * count, count, nstate)
            rt = rates(j)

            def one(t, carry, n=n, j=j, slot=slot, rt=rt):
                bs, ps, gs, rs = carry
                nb, np_, ng, nr = [], [], [], []
                reset = marks(n, t)
                enter = [cscr[slot, at(t), cut(i)] for i in range(count)]
                read = [cscr[slot, at(t), cut(count + i)] for i in range(count)]
                for d in range(groups):
                    st, dt = step[d, row(n, t), :], dy[d, row(n, t), :]
                    ut = st * mix[d, row(n, t), :]
                    st = st + reset
                    if j == 0:
                        nr.append(rs[d] + st)
                    for i in range(count):
                        k = d * count + i
                        a = jnp.exp2(st * rt[k])
                        prod = ps[k] * a
                        nb.append(bs[k] * a + enter[i] * ut)
                        np_.append(prod)
                        ng.append(gs[k] + prod * (read[i] * dt))
                return tuple(nb), tuple(np_), tuple(ng), tuple(nr)

            init = ((zero,) * size, (zero + 1.0,) * size, (zero,) * size, (zero,) * (groups if j == 0 else 0))
            bs, ps, gs, rs = lax.fori_loop(0, steps, one, init, unroll=ENDS_UNROLL)
            if j == 0:
                for d in range(groups):
                    both = rs[d] + jnp.where(odd, pltpu.roll(rs[d], 1, 0), pltpu.roll(rs[d], 7, 0))
                    t_out[n, d] = both
                cps = []
                for q in range(1, reach + 1):
                    cps.append(remote(t_out.at[n], t_up.at[n, q - 1], tsem.at[0, n, q - 1], tsem.at[1, n, q - 1], (f, s + q)))
                    cps.append(remote(t_out.at[n], t_down.at[n, q - 1], tsem2.at[0, n, q - 1], tsem2.at[1, n, q - 1], (f, s - q)))
                    each_way(q, cps[-2].start, cps[-1].start)
                carries.append(cps)
            bd, gd = [], []
            for k in range(size):
                bsc[n, j, k], psc[n, j, k], gsc[n, j, k] = bs[k], ps[k], gs[k]
                bd.append(ps[k] * pltpu.roll(bs[k], 1, 0) + bs[k])
                gd.append(gs[k] + ps[k] * pltpu.roll(gs[k], 7, 0))
            bp, gp = pair_up(bd, True), pair_up(gd, False)
            for k in range(0, size // 2, 2):
                b_out[n, j, k * 8 : k * 8 + 16, :] = jnp.concatenate([bp[k], bp[k + 1]], axis=0).astype(BF16)
                g_out[n, j, k * 8 : k * 8 + 16, :] = jnp.concatenate([gp[k], gp[k + 1]], axis=0).astype(BF16)
            cps = []
            for q in range(1, reach + 1):
                cps.append(
                    remote(b_out.at[n, j], b_in.at[n, j, q - 1], ssem.at[0, n, j, q - 1], rsem.at[0, n, j, q - 1], (f, s + q))
                )
                cps.append(
                    remote(g_out.at[n, j], g_in.at[n, j, q - 1], ssem.at[1, n, j, q - 1], rsem.at[1, n, j, q - 1], (f, s - q))
                )
                each_way(q, cps[-2].start, cps[-1].start)
            carries.append(cps)

    for cp in loads:
        cp.wait()
    coef[...] = jnp.zeros_like(coef)
    outs = []
    order = 0
    for n in range(blocks):
        for d in range(groups):
            y[d] = mix[d, tokens_of(n), :] * vecs[d, 6:7, :]
        for j in range(parts):
            slot = j if blocks == 1 else 0
            if blocks > 1:
                spread_coefs(packed[tokens_of(n), :], cscr.at[slot], j * count, count, nstate)
            mine = [carries[n * (parts + 1) + 1 + j]] + ([carries[n * (parts + 1)]] if j == 0 else [])
            for cps in mine:
                for q in range(1, reach + 1):
                    up, down = cps[2 * q - 2], cps[2 * q - 1]

                    def ahead(up=up, down=down):
                        up.wait_send()
                        down.wait_recv()

                    def behind(up=up, down=down):
                        down.wait_send()
                        up.wait_recv()

                    each_way(q, ahead, behind)
            rt = rates(j)
            hin = [None] * size
            for k in range(0, size, 2):
                h, l = [zero, zero], [zero, zero]
                for q in range(reach - 1, -1, -1):
                    at_ = slice(k * 4, k * 4 + 8)
                    bv, gv = b_in[n, j, q, at_, :].astype(F32), g_in[n, j, q, at_, :].astype(F32)
                    for m in range(2):
                        d = keys[k + m][0]
                        nh = jnp.exp2(rt[k + m] * t_up[n, q, d]) * h[m] + both_rows(bv, m == 0)
                        nl = jnp.exp2(rt[k + m] * t_down[n, q, d]) * l[m] + both_rows(gv, m == 1)
                        h[m] = jnp.where(s - (q + 1) >= 0, nh, 0.0)
                        l[m] = jnp.where(s + (q + 1) < ns, nl, 0.0)
                for m in range(2):
                    d, i = keys[k + m]
                    pv, bv, gv = psc[n, j, k + m], bsc[n, j, k + m], gsc[n, j, k + m]
                    hin[k + m] = jnp.where(odd, pltpu.roll(pv, 1, 0) * h[m] + pltpu.roll(bv, 1, 0), h[m])
                    lin = jnp.where(odd, l[m], pltpu.roll(gv, 7, 0) + pltpu.roll(pv, 7, 0) * l[m])
                    lin_o[n, j * count + i, :, cut(d)] = lin
            kslot = order % 2
            if order >= 2:
                outs[order - 2].wait()

            def forward(t, state, n=n, slot=slot, rt=rt, kslot=kslot):
                reset = marks(n, t)
                enter = [cscr[slot, at(t), cut(i)] for i in range(count)]
                read = [cscr[slot, at(t), cut(count + i)] for i in range(count)]
                new = []
                total = [None] * count
                for d in range(groups):
                    st, dt = step[d, row(n, t), :], dy[d, row(n, t), :]
                    ut = st * mix[d, row(n, t), :]
                    st = st + reset
                    out = None
                    for i in range(count):
                        k = d * count + i
                        a = jnp.exp2(st * rt[k])
                        keep[kslot, t, k] = state[k]
                        h = state[k] * a + enter[i] * ut
                        new.append(h)
                        out = read[i] * h if out is None else out + read[i] * h
                        term = h * dt
                        total[i] = term if total[i] is None else total[i] + term
                    y[d, at(t), :] += out
                for i in range(count):
                    seen[at(t), cut(i)] = total[i]
                return tuple(new)

            lax.fori_loop(0, steps, forward, tuple(hin), unroll=SCAN_UNROLL)
            cp = pltpu.make_async_copy(keep.at[kslot], states_o.at[n * parts + j], ksem.at[order])
            cp.start()
            outs.append(cp)
            order += 1
            lane_sums(seen, coef.at[tokens_of(n)], count, rank + nstate + j * count)

        def some(idx, carry, n=n):
            where, i = split_at(idx, steps // 32)
            q, g = split_at(where, 2)
            for d in range(groups):
                v = y[d, pl.ds(q * 2 + g + i * 256, 32, stride=8), :]
                at_ = rows_at(n * BLOCK_TOKENS + where * steps + i * 32, 32, 16)
                gated[at_, cut(d)] = (v * ga[at_, cut(d)]).astype(BF16)
                dgate[at_, cut(d)] = (v * dgs[at_, cut(d)]).astype(BF16)
            return carry

        lax.fori_loop(0, 8 * (steps // 32), some, 0)
    for cp in outs[-2:]:
        cp.wait()


def middle(nf, ns, cid, reach, step, mix, dy, beg, packed, rate, vecs, ga, dgs, rank, count):
    groups, tokens, _ = step.shape
    nstate, ch = rate.shape[1], groups * 128
    blocks = tokens // BLOCK_TOKENS
    steps = BLOCK_TOKENS // 8
    parts = nstate // count
    size = count * groups
    shape = jax.ShapeDtypeStruct
    v = pltpu.VMEM
    sem = pltpu.SemaphoreType.DMA
    rows_ = size // 2 * 8
    slots = parts if blocks == 1 else 1
    return pl.pallas_call(
        functools.partial(mid_kernel, nf, ns, reach, count, rank, nstate),
        out_shape=(
            shape((tokens, ch), BF16),
            shape((tokens, ch), BF16),
            shape((blocks * parts, steps, size, 8, 128), F32),
            shape((tokens, 128), F32),
            shape((blocks, nstate, 8, ch), F32),
        ),
        in_specs=[VMEM] * 7 + [ANY] * 2,
        out_specs=[VMEM, VMEM, ANY, VMEM, VMEM],
        scratch_shapes=[
            v((slots, BLOCK_TOKENS, 2 * count * 128), F32),
            v((BLOCK_TOKENS, count * 128), F32),
            v((groups, BLOCK_TOKENS, 128), F32),
            v((2, steps, size, 8, 128), F32),
            v((blocks, parts, size, 8, 128), F32),
            v((blocks, parts, size, 8, 128), F32),
            v((blocks, parts, size, 8, 128), F32),
            v((8, 128), F32),
            v((blocks, parts, rows_, 128), BF16),
            v((blocks, parts, rows_, 128), BF16),
            v((blocks, parts, reach, rows_, 128), BF16),
            v((blocks, parts, reach, rows_, 128), BF16),
            v((blocks, groups, 8, 128), F32),
            v((blocks, reach, groups, 8, 128), F32),
            v((blocks, reach, groups, 8, 128), F32),
            v((tokens, ch), F32),
            v((tokens, ch), F32),
            sem((2, blocks, parts, reach)),
            sem((2, blocks, parts, reach)),
            sem((2, blocks, reach)),
            sem((2, blocks, reach)),
            sem((blocks * parts,)),
            sem((2,)),
        ],
        compiler_params=comm_params(cid, 63 << 20),
        name="middle",
    )(step, mix, dy, beg, packed, rate, vecs, ga, dgs)


def backward_kernel(
    count, groups, rank, nstate, step, mix, dy, beg, packed, rate, lin, states, reads, pulled, gs, coef, tot, cscr, seen_scr
):
    j = pl.program_id(1)
    steps = step.shape[1] // 8
    size = count * groups
    keys = [(d, i) for d in range(groups) for i in range(count)]
    rates = rates_of(rate, keys)
    spread_coefs(packed[...], cscr, j * count, count, nstate)

    @pl.when(j == 0)
    def _():
        pulled[...] = jnp.zeros_like(pulled)
        gs[...] = jnp.zeros_like(gs)
        coef[...] = reads[...]

    def backward(k0, carry):
        t = steps - 1 - k0
        passed, sums = carry
        reset = beg[rows_at(16 + t * 8, 8), :]
        enter = [cscr[at(t), cut(i)] for i in range(count)]
        read = [cscr[at(t), cut(count + i)] for i in range(count)]
        new, news = [], []
        seen = [None] * count
        for d in range(groups):
            st, dt = step[d, at(t), :], dy[d, at(t), :]
            ut = st * mix[d, at(t), :]
            st = st + reset
            pull, slope_sum = None, None
            for i in range(count):
                k = d * count + i
                adj = passed[k] + read[i] * dt
                pull = adj * enter[i] if pull is None else pull + adj * enter[i]
                back = adj * jnp.exp2(st * rates[k])
                slope = back * states[0, t, k]
                slope_sum = slope * rates[k] if slope_sum is None else slope_sum + slope * rates[k]
                new.append(back)
                news.append(sums[k] + slope * st)
                term = adj * ut
                seen[i] = term if seen[i] is None else seen[i] + term
            pulled[d, at(t), :] += pull
            gs[d, at(t), :] += slope_sum
        for i in range(count):
            seen_scr[at(t), cut(i)] = seen[i]
        return tuple(new), tuple(news)

    zero = jnp.zeros((8, 128), F32)
    init = (tuple(lin[0, i, :, cut(d)] for d, i in keys), (zero,) * size)
    passed, sums = lax.fori_loop(0, steps, backward, init, unroll=SCAN_UNROLL)
    for n, (d, i) in enumerate(keys):
        line = jnp.sum(sums[n] * rates[n], axis=0, keepdims=True) * LN2
        at_ = pl.ds(j * count + i, 1)

        @pl.when(pl.program_id(0) == 0)
        def _():
            tot[d, at_, :] = line

        @pl.when(pl.program_id(0) > 0)
        def _():
            tot[d, at_, :] += line

    lane_sums(seen_scr, coef, count, rank + j * count)


def scan_backward(step, mix, dy, beg, packed, rate, lin, states, reads, rank, count):
    groups, tokens, _ = step.shape
    nstate, ch = rate.shape
    grid, groups, tok, narrow, marks, rates, state, flat, kept, kept_shape = scan_specs(tokens, ch, nstate, count)
    shape = jax.ShapeDtypeStruct
    work = tokens * nstate * ch
    return pl.pallas_call(
        functools.partial(backward_kernel, count, groups, rank, nstate),
        out_shape=(
            shape(step.shape, F32),
            shape(step.shape, F32),
            shape((tokens, 128), F32),
            shape((groups, nstate, 128), F32),
        ),
        grid=grid,
        in_specs=[tok, tok, tok, marks, narrow, rates, state, kept, narrow],
        out_specs=[tok, tok, narrow, pl.BlockSpec((groups, nstate, 128), lambda n, j: (0, 0, 0))],
        scratch_shapes=[
            pltpu.VMEM((BLOCK_TOKENS, 2 * count * 128), F32),
            pltpu.VMEM((BLOCK_TOKENS, count * 128), F32),
        ],
        compiler_params=pltpu.CompilerParams(vmem_limit_bytes=60 << 20),
        cost_estimate=pl.CostEstimate(flops=12 * work, bytes_accessed=4 * work, transcendentals=work),
        name="scan_backward",
    )(step, mix, dy, beg, packed, rate.reshape(nstate // count, count, ch), lin, states, reads)


class Stream:
    def __init__(self, wire, place, src, got_y, mid, got_z, red, fin, out):
        self.wire, self.place = wire, place
        self.src, self.got_y, self.mid, self.got_z = src, got_y, mid, got_z
        self.red, self.fin, self.out = red, fin, out

    def start(self):
        p = self.place
        self.y = self.wire.send(self.src.at[:, 1 - p.b], self.got_y, p.beside)

    def across(self):
        p = self.place
        self.y.wait_recv()
        self.mid[...] = (self.src[:, p.b].astype(F32) + self.got_y[...].astype(F32)).astype(self.mid.dtype)
        self.z = [
            self.wire.send(self.mid.at[:, lax.bitwise_xor(p.a, i)], self.got_z.at[i - 1], p.zdev(i))
            for i in range(1, p.na)
        ]

    def swap(self):
        p = self.place
        for cp in self.z:
            cp.wait_recv()
        acc = self.mid[:, p.a].astype(F32)
        for i in range(1, p.na):
            acc = acc + self.got_z[i - 1].astype(F32)
        self.red[...] = acc.astype(self.red.dtype)
        self.w = [
            self.wire.send(self.red.at[lax.bitwise_xor(p.f, i)], self.fin.at[p.f], p.fdev(i)) for i in range(1, p.nf)
        ]
        self.fin[p.f] = self.red[p.f]

    def spread(self):
        p = self.place
        for cp in self.w:
            cp.wait_recv()
        self.out[p.b, p.a] = self.fin[...]
        self.g = [(self.wire.send(self.fin, self.out.at[p.b, p.a], p.zdev(i)), i) for i in range(1, p.na)]
        self.h = [self.wire.send(self.fin, self.out.at[p.b, p.a], p.beside)]

    def forward(self):
        p = self.place
        for cp, i in self.g:
            cp.wait_recv()
            block = self.out.at[p.b, lax.bitwise_xor(p.a, i)]
            self.h.append(self.wire.send(block, block, p.beside))

    def finish(self):
        for cp in self.h:
            cp.wait_recv()


class Place:
    def __init__(self, nf, ns):
        self.f, self.s = here()
        self.nf, self.ns, self.na = nf, ns, ns // 2
        self.a, self.b = lax.div(self.s, 2), lax.rem(self.s, 2)
        self.core = lax.rem(self.f, 2)
        self.peer = (lax.bitwise_xor(self.f, 1), self.s)
        self.beside = (self.f, lax.bitwise_xor(self.s, 1))

    def fdev(self, i):
        return (lax.bitwise_xor(self.f, i), self.s)

    def zdev(self, i):
        return (self.f, lax.bitwise_xor(self.a, i) * 2 + self.b)


def small_layout(groups, rank, nstate, ns):
    select, step, decay, vectors = 0, 128, 128 + rank, 128 + rank + nstate
    group = vectors + 8
    piece = -(-group * groups // (8 * ns)) * 8
    return select, step, decay, vectors, group, piece


def post_kernel(nf, ns, nq, rd, rank, nstate, sems, *refs):
    (pulled_i, slopes_i, mix_i, step_i, dy_i, slope_i, ext_i, beg_i, normed_i, wi_i, wg_i, dgate_i) = refs[:12]
    (ce, proj, vecs, w_sel, w_step, table, x, ct, decay) = refs[12:21]
    gates = refs[21 : 21 + nq]
    refs = refs[21 + nq :]
    rout, gain_out, small_out = refs[:3]
    outs = refs[3 : 3 + 2 * nq]
    refs = refs[3 + 2 * nq :]
    (pulled, slopes, mix, step, dy, slope, ext, beg, normed, wi, wg, dgate) = refs[:12]
    (mixb, dlin, dproj, dib, part, got, mid, far, sums) = refs[12:21]
    dconv, dp = mix, normed
    (near_d, mid_d, far_d, gain_l, gain_f, gain_m, gain_y, gain_n, gain_z, small, small_y, small_m, small_z) = refs[21:34]
    (edge_o, edge_i) = refs[34:36]
    refs = refs[36:]
    inners = refs[:nq]
    refs = refs[nq:]
    bufs = [refs[n * 2 * nq : (n + 1) * 2 * nq] for n in range(5)]
    ssem, rsem, lsem, esem = refs[10 * nq :]

    place = Place(nf, ns)
    f, s, a, b, core = place.f, place.s, place.a, place.b, place.core
    na = place.na
    chips = list(range(2, nf, 2))
    groups, tokens, _ = pulled.shape
    ch = groups * 128
    stretch = tokens // (nf * rd)
    half = stretch // 2
    span_t = half * 8
    blocks = tokens // span_t
    width = normed.shape[1]
    off_select, off_step, off_decay, off_vec, group_rows, piece = small_layout(groups, rank, nstate, ns)
    has_up, has_down = s + 1 < ns, s >= 1
    greet(
        [(None, place.fdev(i)) for i in range(1, nf)]
        + [(None, place.beside)]
        + [(None, place.zdev(i)) for i in range(1, na)]
        + [(has_up, (f, s + 1)), (has_down, (f, s - 1))]
    )
    wire = Wire(ssem, rsem)
    streams = []
    for n in range(2 * nq):
        src = gates[n] if n < nq else inners[n - nq]
        streams.append(Stream(wire, place, src, *[v[n] for v in bufs], outs[n]))
    for n in range(nq):
        streams[n].start()

    loads = []

    def load(src, dst):
        cp = pltpu.make_async_copy(src, dst, lsem.at[len(loads)])
        loads.append(cp)
        cp.start()
        return cp

    hs = tokens // 2
    other, keep = (1 - core) * hs, core * hs
    first = [(pulled_i, pulled), (slopes_i, slopes), (mix_i, mix), (step_i, step), (dy_i, dy)]
    by_half = []
    for start in (other, keep):
        rows_ = rows_at(start, hs)
        by_half.append([load(src.at[:, rows_], dst.at[:, rows_]) for src, dst in first])
    conv_in = [load(slope_i, slope), load(ext_i, ext), load(beg_i, beg.at[pl.ds(0, beg_i.shape[0])])]
    late = [load(normed_i, normed), load(wi_i, wi), load(wg_i, wg), load(dgate_i, dgate)]
    for d in range(groups):
        small[d * group_rows + off_decay : d * group_rows + off_vec, :] = decay[d]
        small[d * group_rows + off_vec : (d + 1) * group_rows, :] = jnp.zeros((8, 128), F32)
    rest = small.shape[0] - groups * group_rows
    if rest:
        small[groups * group_rows :, :] = jnp.zeros((rest, 128), F32)
    beg[beg_i.shape[0] :, :] = jnp.zeros((24, 128), F32)

    chunk = 64

    def fold(v):
        out = v[0:8]
        for q in range(1, v.shape[0] // 8):
            out = out + v[q * 8 : (q + 1) * 8]
        return out

    def add_row(d, k, v):
        at_ = slice(d * group_rows + off_vec + k, d * group_rows + off_vec + k + 1)
        small[at_, :] += jnp.sum(v, axis=0, keepdims=True)

    zero = jnp.zeros((8, 128), F32)

    def step_half(start, cps):
        for cp in cps:
            cp.wait()
        for d in range(groups):

            def one(c, carry, d=d):
                at_ = rows_at(start + c * chunk, chunk)
                pu, m, st, dv = pulled[d, at_, :], mix[d, at_, :], step[d, at_, :], dy[d, at_, :]
                tiny = st * (1.0 - st * (0.5 - st * (1.0 / 6.0 - st * (1.0 / 24.0))))
                sig = jnp.where(st < 0.03, tiny, 1.0 - jnp.exp(-st))
                dpre = (m * pu + slopes[d, at_, :] * LN2) * sig
                low_at = rows_at(start + c * chunk, chunk, 16)
                dlin[d, low_at, :] = dpre.astype(BF16)
                mixb[d, low_at, :] = m.astype(BF16)
                pulled[d, at_, :] = st * pu + dv * vecs[d, 6:7, :]
                return carry[0] + fold(dpre), carry[1] + fold(dv * m)

            bias, skip = lax.fori_loop(0, hs // chunk, one, (zero, zero))
            add_row(d, 5, bias)
            add_row(d, 6, skip)
        at_ = rows_at(start, hs)
        total = None
        for d in range(groups):
            term = times_transposed(dlin[d, rows_at(start, hs, 16), :], w_step[:, cut(d)])
            total = term if total is None else total + term
        part[at_, :] = ce[at_, :]
        part[at_, :rank] += total

    step_half(other, by_half[0])
    one = wire.send(part.at[rows_at(other, hs)], got, place.peer)
    step_half(keep, by_half[1])
    one.wait_recv()
    mid[...] = part[rows_at(keep, hs), :] + got[...]
    two = [wire.send(mid, far.at[n], place.fdev(i)) for n, i in enumerate(chips)]

    for d in range(groups):
        low = proj[...][:, :rank].astype(BF16)
        small[d * group_rows + off_step : d * group_rows + off_decay, :] = rows_inner(low, dlin[d])
    for n in range(nq):
        streams[n].across()

    for cp in two:
        cp.wait_recv()
    acc = mid[...]
    for n in range(len(chips)):
        acc = acc + far[n]
    sums[rows_at(keep, hs), :] = acc
    three = wire.send(sums.at[rows_at(keep, hs)], sums.at[rows_at(keep, hs)], place.peer)
    for cp in conv_in:
        cp.wait()

    def mask_at(base, k):
        out = jnp.where(beg[rows_at(base + 16, chunk), :] > 0.0, 0.0, 1.0)
        if k <= 1:
            out = jnp.where(beg[rows_at(base + 8, chunk), :] > 0.0, 0.0, out)
        if k == 0:
            out = jnp.where(beg[rows_at(base, chunk), :] > 0.0, 0.0, out)
        return out

    def conv_half(start):
        at_all = rows_at(start, hs)
        low_all = rows_at(start, hs, 16)
        dproj[low_all, :] = sums[at_all, :].astype(BF16)
        for d in range(groups):
            slopes[d, at_all, :] = times_transposed(dproj[low_all, :], w_sel[d * 128 : (d + 1) * 128, :])

            def one(c, carry, d=d):
                row = start + c * chunk
                n, inside = split_at(row, span_t)
                at_ = rows_at(row, chunk)
                v = (pulled[d, at_, :] + slopes[d, at_, :]) * slope[d, at_, :]
                base = n * (span_t + LEAD)
                dconv[d, rows_at(base + inside, chunk), :] = v
                bb = n * (span_t + 16) + inside
                out = [carry[0] + fold(v)]
                for k in range(4):
                    tap = ext[d, rows_at(base + inside + k * 8, chunk), :]
                    w = v * tap if k == 3 else v * tap * mask_at(bb, k)
                    out.append(carry[1 + k] + fold(w))
                return tuple(out)

            totals = lax.fori_loop(0, hs // chunk, one, (zero,) * 5)
            add_row(d, 4, totals[0])
            for k in range(4):
                add_row(d, k, totals[1 + k])

    for n in range(blocks):
        for d in range(groups):
            dconv[d, n * (span_t + LEAD) + span_t : (n + 1) * (span_t + LEAD), :] = jnp.zeros((LEAD, 128), F32)
    conv_half(keep)
    three.wait_recv()
    conv_half(other)

    sub = lax.broadcasted_iota(jnp.int32, (8, 128), 0)
    for n in range(blocks):
        base = n * (span_t + LEAD)
        bb = n * (span_t + 16)
        hit = [jnp.where(beg[bb + q * 8 : bb + q * 8 + 8, :] > 0.0, 0.0, 1.0) for q in range(5)]
        for d in range(groups):
            tail = [zero] * 3
            for q in range(3):
                v = dconv[d, base + q * 8 : base + q * 8 + 8, :]
                keepers = [hit[q + 2] * hit[q + 1] * hit[q], hit[q + 2] * hit[q + 1], hit[q + 2]]
                for k in range(3 - q):
                    tail[q + k] = tail[q + k] + vecs[d, k : k + 1, :] * (v * keepers[k])
            for q in range(3):
                edge_o[d, n * 24 + q * 8 : n * 24 + q * 8 + 8, :] = tail[q]
    edge = remote(edge_o, edge_i, esem.at[0], esem.at[1], (f, s - 1))

    @pl.when(has_down)
    def _():
        edge.start()

    for n in range(nq):
        streams[n].swap()

    per = span_t // chunk

    def inner_chunk(idx, carry):
        nd, c = split_at(idx, per)
        n, d = split_at(nd, groups)
        base = n * (span_t + LEAD) + c * chunk
        bb = n * (span_t + 16) + c * chunk
        acc = vecs[d, 3:4, :] * dconv[d, rows_at(base, chunk), :]
        for k in range(3):
            ahead = (3 - k) * 8
            acc = acc + vecs[d, k : k + 1, :] * (dconv[d, rows_at(base + ahead, chunk), :] * mask_at(bb + ahead, k))
        pulled[d, rows_at(n * span_t + c * chunk, chunk), :] = acc
        return carry

    lax.fori_loop(0, blocks * groups * per, inner_chunk, 0)

    for d in range(groups):
        small[d * group_rows + off_select : d * group_rows + off_step, :] = rows_inner(mixb[d], dproj[...])
    small_half = na * piece
    small_ys = wire.send(small.at[rows_at((1 - b) * small_half, small_half)], small_y, place.beside)
    for n in range(nq):
        streams[n].spread()

    @pl.when(has_up)
    def _():
        edge.wait_recv()

    for n in range(blocks):
        for d in range(groups):
            for q in range(3):
                at_ = slice(n * 24 + q * 8, n * 24 + q * 8 + 8)
                inward = pltpu.roll(edge_o[d, at_, :], 7, 0)
                outer = jnp.where(has_up, pltpu.roll(edge_i[d, at_, :], 1, 0), 0.0)
                row = n * span_t + (half - 3 + q) * 8
                pulled[d, row : row + 8, :] += jnp.where(sub % 2 == 0, inward, outer)

    def to_rows(idx, carry):
        r_g, i = split_at(idx, half // 32)
        r, g = split_at(r_g, 2)
        n, q = split_at(r, 4)
        at_ = rows_at(r_g * half + i * 32, 32, 16)
        for d in range(groups):
            v = pulled[d, pl.ds(n * span_t + q * 2 + g + i * 256, 32, stride=8), :]
            dib[at_, cut(d)] = v.astype(BF16)
        return carry

    lax.fori_loop(0, 2 * nf * rd * (half // 32), to_rows, 0)

    for cp in late:
        cp.wait()
    drow = width // nf
    prow = drow // ns
    lanes = max(drow, 128)
    cq = ch // nq
    for q in range(nq):

        def grad_block(k, carry, q=q):
            v = rows_inner(normed[:, pl.ds(pl.multiple_of(k * lanes, 128), lanes)], dib[:, q * cq : (q + 1) * cq])
            for m in range(lanes // drow):
                for p in range(ns):
                    r = m * drow + p * prow
                    piece_v = v[r : r + prow].astype(inners[q].dtype)
                    inners[q][k * (lanes // drow) + m, p // na, p % na] = piece_v
            return carry

        lax.fori_loop(0, width // lanes, grad_block, 0)
        streams[nq + q].start()

    span = rd * stretch

    def dn_rows(flip):
        def one(n, carry):
            who = lax.bitwise_xor(lax.bitwise_xor(f, flip), 2 * n)
            for q in range(rd):
                at_ = rows_at(who * span + q * stretch, stretch, 16)
                v = times_transposed(dib[at_, :], wi[...]) + times_transposed(dgate[at_, :], wg[...])
                dp[at_, :] = v.astype(BF16)
            return carry

        lax.fori_loop(0, nf // 2, one, 0)

    def dp_rows(who):
        return rows_at(who * span, span, 16)

    dn_rows(1)
    near = [
        wire.send(dp.at[dp_rows(lax.bitwise_xor(lax.bitwise_xor(f, 1), i))], near_d.at[n], place.peer)
        for n, i in enumerate([0] + chips)
    ]
    dn_rows(0)
    fars = []
    for n, i in reversed(list(enumerate([0] + chips))):
        near[n].wait_recv()
        if i:
            dest = lax.bitwise_xor(f, i)
            mid_d[n - 1] = (dp[dp_rows(dest), :].astype(F32) + near_d[n].astype(F32)).astype(BF16)
            fars.append(wire.send(mid_d.at[n - 1], far_d.at[n - 1], place.fdev(i)))
    for n in range(nq):
        streams[n].forward()
    small_ys.wait_recv()
    small_m[...] = small[rows_at(b * small_half, small_half), :] + small_y[...]

    def owned(who):
        return rows_at(who * piece, piece)

    small_zs = [
        wire.send(small_m.at[owned(lax.bitwise_xor(a, i))], small_z.at[i - 1], place.zdev(i)) for i in range(1, na)
    ]
    for n in range(nq, 2 * nq):
        streams[n].across()

    gain = jnp.concatenate([table[q : q + 1, :] for q in range(width // 128)], axis=1)
    for cp in fars:
        cp.wait_recv()

    def own_rows(i, total):
        at_ = rows_at(i * 16, 16, 16)
        v = x[at_, :].astype(F32)
        scale = lax.rsqrt(jnp.sum(v * v, axis=1, keepdims=True) * (1.0 / width) + EPS)
        hat = v * scale
        dn = dp[rows_at(f * span + i * 16, 16, 16), :].astype(F32) + near_d[0, at_, :].astype(F32)
        for n in range(len(chips)):
            dn = dn + far_d[n, at_, :].astype(F32)
        dh = dn * gain
        inner = jnp.sum(dh * hat, axis=1, keepdims=True) * (1.0 / width)
        rout[at_, :] = ct[at_, :].astype(F32) + scale * (dh - hat * inner)
        return total + jnp.sum(dn * hat, axis=0, keepdims=True)

    gain_l[...] = lax.fori_loop(0, x.shape[0] // 16, own_rows, jnp.zeros((1, width), F32))
    gain_a = [wire.send(gain_l, gain_f.at[i - 1], place.fdev(i)) for i in range(1, nf)]
    for cp in small_zs:
        cp.wait_recv()
    acc = small_m[owned(a), :]
    for i in range(1, na):
        acc = acc + small_z[i - 1]
    mine = rows_at(b * small_half + a * piece, piece)
    small_out[mine, :] = acc
    small_g = [(wire.send(small_out.at[mine], small_out.at[mine], place.zdev(i)), i) for i in range(1, na)]
    small_h = [wire.send(small_out.at[mine], small_out.at[mine], place.beside)]
    for n in range(nq, 2 * nq):
        streams[n].swap()
    for cp in gain_a:
        cp.wait_recv()
    acc = gain_l[...]
    for i in range(1, nf):
        acc = acc + gain_f[i - 1]
    gain_m[...] = acc
    gain_b = wire.send(gain_m, gain_y, place.beside)
    for n in range(nq, 2 * nq):
        streams[n].spread()
    for cp, i in small_g:
        cp.wait_recv()
        theirs = rows_at(b * small_half + lax.bitwise_xor(a, i) * piece, piece)
        small_h.append(wire.send(small_out.at[theirs], small_out.at[theirs], place.beside))
    gain_b.wait_recv()
    gain_n[...] = gain_m[...] + gain_y[...]
    gain_c = [wire.send(gain_n, gain_z.at[i - 1], place.zdev(i)) for i in range(1, na)]
    for n in range(nq, 2 * nq):
        streams[n].forward()
    for cp in gain_c:
        cp.wait_recv()
    acc = gain_n[...]
    for i in range(1, na):
        acc = acc + gain_z[i - 1]
    gain_out[...] = acc
    for cp in small_h:
        cp.wait_recv()
    for st in streams:
        st.finish()
    wire.drain()

    @pl.when(has_down)
    def _():
        edge.wait_send()

    assert len(wire.copies) == sems


def post(nf, ns, nq, cid, rd, rank, nstate, big, little, gates):
    shape = jax.ShapeDtypeStruct
    v = pltpu.VMEM
    pulled, ext, beg, normed, wi = big[0], big[6], big[7], big[8], big[9]
    x = little[6]
    groups, tokens, _ = pulled.shape
    ch = groups * 128
    width = normed.shape[1]
    na = ns // 2
    chips = nf // 2 - 1
    block = x.shape
    piece_shape = gates[0].shape[3:]
    piece = small_layout(groups, rank, nstate, ns)[-1]
    total = piece * ns
    hs = tokens // 2
    blocks = tokens // BLOCK_TOKENS
    stream = 1 + (na - 1) + (nf - 1) + (na - 1) + 1 + (na - 1)
    sems = 2 * nq * stream
    sems += 2 + chips
    sems += 1 + 2 * chips
    sems += 1 + (na - 1) + (na - 1) + 1 + (na - 1)
    sems += (nf - 1) + 1 + (na - 1)
    outs = [shape(block, F32), shape((1, width), F32), shape((total, 128), F32)]
    kind = gates[0].dtype
    outs += [shape((2, na, nf) + piece_shape, kind)] * (2 * nq)
    scratch = [v(m.shape, m.dtype) for m in big]
    scratch[2] = v(ext.shape, F32)
    scratch[7] = v((beg.shape[0] + 24, 128), F32)
    scratch += [
        v(pulled.shape, BF16),
        v(pulled.shape, BF16),
        v((tokens, 128), BF16),
        v((tokens, ch), BF16),
        v((tokens, 128), F32),
        v((hs, 128), F32),
        v((hs, 128), F32),
        v((chips, hs, 128), F32),
        v((tokens, 128), F32),
        v((chips + 1,) + block, BF16),
        v((chips,) + block, BF16),
        v((chips,) + block, BF16),
        v((1, width), F32),
        v((nf - 1, 1, width), F32),
        v((1, width), F32),
        v((1, width), F32),
        v((1, width), F32),
        v((na - 1, 1, width), F32),
        v((total, 128), F32),
        v((na * piece, 128), F32),
        v((na * piece, 128), F32),
        v((na - 1, piece, 128), F32),
        v((groups, blocks * 24, 128), F32),
        v((groups, blocks * 24, 128), F32),
    ]
    scratch += [v(gates[0].shape, kind)] * nq
    scratch += [v((nf, na) + piece_shape, kind)] * (2 * nq)
    scratch += [v((nf, na) + piece_shape, kind)] * (2 * nq)
    scratch += [v((na - 1, nf) + piece_shape, kind)] * (2 * nq)
    scratch += [v((nf,) + piece_shape, kind)] * (2 * nq)
    scratch += [v((nf,) + piece_shape, kind)] * (2 * nq)
    scratch += [
        pltpu.SemaphoreType.DMA((sems,)),
        pltpu.SemaphoreType.DMA((sems,)),
        pltpu.SemaphoreType.DMA((17,)),
        pltpu.SemaphoreType.DMA((2,)),
    ]
    return pl.pallas_call(
        functools.partial(post_kernel, nf, ns, nq, rd, rank, nstate, sems),
        out_shape=outs,
        in_specs=[ANY] * 12 + [VMEM] * (9 + nq),
        out_specs=[VMEM] * len(outs),
        scratch_shapes=scratch,
        compiler_params=comm_params(cid, 63 << 20),
        name="post",
    )(*big, *little, *gates)


def rows_inner(left, right):
    return lax.dot_general(left, right, (((0,), (0,)), ((), ())), preferred_element_type=F32)


def times_transposed(left, right):
    return lax.dot_general(left, right, (((1,), (1,)), ((), ())), preferred_element_type=F32)


def silu_slope(value):
    sig = jax.nn.sigmoid(value)
    return sig * (1.0 + value * (1.0 - sig))


def shards(
    nf,
    ns,
    residual,
    out_cotangent,
    doc_lengths,
    norm_gain,
    input_proj,
    conv_kernel,
    conv_bias,
    select_proj,
    step_proj,
    step_bias,
    log_decay,
    skip_gain,
    output_proj,
):
    rd, stretch, width = residual.shape
    rows = nf * rd
    docs = doc_lengths.shape[1]
    ch = conv_bias.shape[0]
    rank = step_proj.shape[0]
    nstate = log_decay.shape[0]
    taps = conv_kernel.shape[0]
    edge = taps - 1
    tokens = rows * stretch
    half = stretch // 2
    blocks = rows // 4
    f, s = here()
    reach = -(-(stretch * ns // 2 - 1) // stretch)
    count = 4

    groups = ch // 128
    grows = norm_gain.shape[0]
    spot = lax.broadcasted_iota(jnp.int32, (width,), 0) // grows == f
    small = jnp.where(spot, jnp.tile(norm_gain.astype(F32), nf), 0.0).reshape(width // 128, 128)
    marks = jnp.pad(doc_lengths.astype(F32), ((0, 8 - rd), (0, 128 - docs)))
    small = jnp.concatenate([small, marks], axis=0)
    vecs = jnp.concatenate(
        [conv_kernel, conv_bias[None], step_bias[None], skip_gain[None], jnp.zeros((1, ch), BF16)], axis=0
    ).astype(F32)
    vecs = jnp.moveaxis(vecs.reshape(8, groups, 128), 1, 0)
    w_sel = jnp.pad(select_proj, ((0, 0), (0, 128 - select_proj.shape[1])))
    normed, cot, ext, slope, mix, dy, ga, dgs, step, beg, proj, packed, w_inner, w_gate, gain = front(
        nf, ns, residual, out_cotangent, input_proj, small, vecs, w_sel, step_proj, output_proj, rank, nstate
    )
    rate = -jnp.exp(log_decay.astype(F32))
    rate2 = rate * LOG2E

    rates = jnp.moveaxis(rate2.reshape(nstate, groups, 128), 1, 0)
    gated, d_gate, states, coef_read, lin = middle(
        nf, ns, 2, reach, step, mix, dy, beg, packed, rates, vecs, ga, dgs, rank, count
    )
    nq = 2 if ch % 256 == 0 else 1
    cq = ch // nq
    piece_rows = width // nf // ns
    kind = BF16
    output_grad = rows_inner(gated, cot).astype(BF16)
    out_part = jnp.dot(gated, output_proj, preferred_element_type=F32).astype(BF16)
    gate_grads = [
        rows_inner(normed, d_gate[:, q * cq : (q + 1) * cq]).astype(kind).reshape(nf, 2, ns // 2, piece_rows, cq)
        for q in range(nq)
    ]
    output_grad, out_part, lin, *gate_grads = lax.optimization_barrier((output_grad, out_part, lin, *gate_grads))
    output_grad = lax.psum(output_grad, "seq")
    out_sum = lax.psum_scatter(out_part, "fsdp", scatter_dimension=0, tiled=True)

    pulled, slopes, coefs, decay = scan_backward(step, mix, dy, beg, packed, rate2, lin, states, coef_read, rank, count)
    big = (pulled, slopes, mix, step, dy, slope, ext, beg, normed, w_inner, w_gate, d_gate)
    little = (
        coefs,
        proj,
        vecs,
        w_sel,
        step_proj,
        gain,
        residual.reshape(rd * stretch, width),
        out_cotangent.reshape(rd * stretch, width),
        decay,
    )
    residual_grad, gain_sum, small_sum, *sums = post(nf, ns, nq, 3, rd, rank, nstate, big, little, gate_grads)
    layer_output = (residual.reshape(rd * stretch, width).astype(F32) + out_sum.astype(F32)).astype(BF16)

    def side(parts):
        parts = [v.reshape(ns, nf, piece_rows, cq) for v in parts]
        return jnp.moveaxis(jnp.concatenate(parts, axis=3), 1, 2).reshape(width // nf, nf * ch)

    input_grad = jnp.concatenate([side(sums[nq:]), side(sums[:nq])], axis=1).astype(F32)
    off_select, off_step, off_decay, off_vec, group_rows, _ = small_layout(groups, rank, nstate, ns)
    small_sum = small_sum[: groups * group_rows].reshape(groups, group_rows, 128)

    def section(start, count_):
        return jnp.moveaxis(small_sum[:, start : start + count_], 0, 1).reshape(count_, ch)

    vectors = section(off_vec, 8)
    return (
        layer_output.reshape(rd, stretch, width),
        residual_grad.reshape(rd, stretch, width),
        lax.dynamic_slice(gain_sum[0], (f * grows,), (grows,)),
        input_grad,
        vectors[:4],
        vectors[4],
        small_sum[:, :off_step, : select_proj.shape[1]].reshape(ch, select_proj.shape[1]),
        section(off_step, rank),
        vectors[5],
        section(off_decay, nstate),
        vectors[6],
        output_grad.astype(F32),
    )


def solution(mesh):
    nf, ns = mesh.shape["fsdp"], mesh.shape["seq"]
    in_specs = (
        P("fsdp", "seq", None),
        P("fsdp", "seq", None),
        P("fsdp", None),
        P("fsdp"),
        P("fsdp", None),
        P(None, "fsdp"),
        P("fsdp"),
        P("fsdp", None),
        P(None, "fsdp"),
        P("fsdp"),
        P(None, "fsdp"),
        P("fsdp"),
        P("fsdp", None),
    )
    out_specs = (
        P("fsdp", "seq", None),
        P("fsdp", "seq", None),
        P("fsdp"),
        P("fsdp", None),
        P(None, "fsdp"),
        P("fsdp"),
        P("fsdp", None),
        P(None, "fsdp"),
        P("fsdp"),
        P(None, "fsdp"),
        P("fsdp"),
        P("fsdp", None),
    )
    return jax.shard_map(
        functools.partial(shards, nf, ns), mesh=mesh, in_specs=in_specs, out_specs=out_specs, check_vma=False
    )
```

```python
import functools
import math

import jax
import jax.numpy as jnp
from jax import lax
from jax.experimental import pallas as pl
from jax.experimental.pallas import tpu as pltpu
from jax.sharding import PartitionSpec as P

EPS = 1e-05
MESH = pl.DeviceIdType.MESH
LOG2E = math.log2(math.e)
LN2 = math.log(2.0)
BF16 = jnp.bfloat16
F32 = jnp.float32
ANY = pl.BlockSpec(memory_space=pl.ANY)
VMEM = pl.BlockSpec(memory_space=pltpu.VMEM)
RESET = 1e30
HALO = 16
DOCS = 8


def here():
    return lax.axis_index("fsdp"), lax.axis_index("seq")


def greet(peers):
    barrier = pltpu.get_barrier_semaphore()
    count = 0
    for ok, device in peers:
        if ok is None:
            pl.semaphore_signal(barrier, inc=1, device_id=device, device_id_type=MESH)
            count = count + 1
        else:

            @pl.when(ok)
            def _():
                pl.semaphore_signal(barrier, inc=1, device_id=device, device_id_type=MESH)

            count = count + ok.astype(jnp.int32)
    pl.semaphore_wait(barrier, count)


def remote(src, dst, send, recv, device):
    return pltpu.make_async_remote_copy(
        src_ref=src, dst_ref=dst, send_sem=send, recv_sem=recv, device_id=device, device_id_type=MESH
    )


def comm_params(cid, vmem=None):
    return pltpu.CompilerParams(collective_id=cid, has_side_effects=True, vmem_limit_bytes=vmem)


class Wire:
    def __init__(self, ssem, rsem):
        self.ssem, self.rsem, self.copies, self.done = ssem, rsem, [], []

    def send(self, src, dst, device):
        k = len(self.copies)
        cp = remote(src, dst, self.ssem.at[k], self.rsem.at[k], device)
        self.copies.append(cp)
        cp.start()
        return cp

    def sent(self, cp):
        cp.wait_send()
        self.done.append(cp)

    def drain(self):
        for cp in self.copies:
            if all(cp is not other for other in self.done):
                cp.wait_send()


LEAD = 24


def rows_at(base, size, unit=8):
    return pl.ds(pl.multiple_of(base, unit), size)


def split_at(i, n):
    return lax.div(i, n), lax.rem(i, n)


def front_kernel(nf, ns, rd, rank, nstate, sems, *refs):
    (x, ct, w, sm, vecs, w_sel, w_step, w_out) = refs[:8]
    (normed_o, cg_o, ext_o, slope_o, mix_o, dy_o, ga_o, dgs_o, step_o, beg_o, proj_o, packed_o, wi_o, wg_o, gain_o) = refs[8:23]
    (xg, cg, wi, wg, sg, hal, hres, vbuf, gbuf, ext, slope, mix, mixb, dy, ga, dgs, step, beg, part, got, mid, far, proj, packed) = refs[
        23:47
    ]
    ssem, rsem, hsem, hrem, lsem, osem = refs[47:]
    f, s = here()
    core, b = lax.rem(f, 2), lax.rem(s, 2)
    stretch = x.shape[1]
    half = stretch // 2
    dmodel = xg.shape[1]
    ch = wi.shape[1]
    groups = ch // 128
    rows = nf * rd
    blocks = rows // 4
    tokens = rows * stretch
    drow = w.shape[0]
    inner_all = w.shape[1] // 2
    chips = list(range(2, nf, 2))
    peer = (lax.bitwise_xor(f, 1), s)
    beside = (f, lax.bitwise_xor(s, 1))
    up, down = s + 1, s - 1
    has_up, has_down = up < ns, down >= 0

    def fdev(i):
        return (lax.bitwise_xor(f, i), s)

    greeted = [(None, fdev(i)) for i in range(1, nf)] + [(None, beside)]
    for i in range(nf):
        greeted.append((has_up, (lax.bitwise_xor(f, i), up)))
        greeted.append((has_down, (lax.bitwise_xor(f, i), down)))
    greet(greeted)
    wire = Wire(ssem, rsem)

    def act_rows(who):
        return rows_at(who * (rd * stretch), rd * stretch, 16)

    def wcols(who, base, start, size):
        return w.at[pl.ds(start, size), pl.ds(pl.multiple_of(base + who * ch, 128), ch)]

    def wrows(who, start, size):
        return pl.ds(pl.multiple_of(who * drow + start, 16), size)

    half_rows = drow // 2
    mine = pl.multiple_of(b * half_rows, 16)

    locals_ = []

    def local(src, dst):
        cp = pltpu.make_async_copy(src, dst, lsem.at[len(locals_)])
        locals_.append(cp)
        cp.start()
        return cp

    x2 = [x.at[q] for q in range(rd)]
    smalls = [wire.send(sm, sg.at[f], fdev(i)) for i in range(1, nf)]
    own_x = [local(x2[q], xg.at[rows_at((f * rd + q) * stretch, stretch, 16)]) for q in range(rd)]
    own_s = local(sm, sg.at[f])

    def send_rows(src, dst):
        if rd == 1:
            return [wire.send(src.at[0], dst.at[act_rows(f)], fdev(i)) for i in [1] + chips]
        return [wire.send(src, dst.at[act_rows(f)], fdev(i)) for i in [1] + chips]

    def send_weight(base, dst):
        out = [wire.send(wcols(peer[0], base, 0, drow), dst.at[wrows(f, 0, drow)], peer)]
        for i in range(2, nf):
            out.append(
                wire.send(wcols(lax.bitwise_xor(f, i), base, mine, half_rows), dst.at[wrows(f, mine, half_rows)], fdev(i))
            )
        return out

    xs = send_rows(x, xg)
    wis = send_weight(0, wi)
    halos = [
        remote(
            x.at[:, pl.ds(stretch - HALO, HALO), :],
            hal.at[pl.ds(f * rd, rd)],
            hsem.at[i],
            hrem.at[i],
            (lax.bitwise_xor(f, i), up),
        )
        for i in range(nf)
    ]

    @pl.when(has_up)
    def _():
        for cp in halos:
            cp.start()

    own_wi = local(wcols(f, 0, 0, drow), wi.at[wrows(f, 0, drow)])
    cs = send_rows(ct, cg)
    wgs = send_weight(inner_all, wg)
    own_c = [local(ct.at[q], cg.at[rows_at((f * rd + q) * stretch, stretch, 16)]) for q in range(rd)]
    own_wg = local(wcols(f, inner_all, 0, drow), wg.at[wrows(f, 0, drow)])

    own_s.wait()
    for cp in smalls:
        cp.wait_recv()
    table = sg[0]
    for k in range(1, nf):
        table = table + sg[k]
    gain = jnp.concatenate([table[q : q + 1, :] for q in range(dmodel // 128)], axis=1)
    gain_o[...] = table
    sub = lax.broadcasted_iota(jnp.int32, (8, 128), 0)
    for n in range(blocks):
        lens = jnp.zeros((8, 128), F32)
        for q in range(4):
            r = n * 4 + q
            line = sg[r // rd, 8 + r % rd : 9 + r % rd, :]
            lens = jnp.where(sub // 2 == q, jnp.broadcast_to(line, (8, 128)), lens)
        starts = [jnp.zeros((8, 128), F32)]
        for j in range(DOCS - 1):
            starts.append(starts[-1] + jnp.broadcast_to(lens[:, j : j + 1], (8, 128)))
        first = (s * stretch + (sub % 2) * half).astype(F32)

        def mark(t, carry, n=n, starts=starts, first=first):
            place = first + (t - 2).astype(F32)
            hit = starts[0] == place
            for j in range(1, DOCS):
                hit = jnp.logical_or(hit, starts[j] == place)
            beg[rows_at(n * (half + 2) * 8 + t * 8, 8), :] = jnp.where(hit, RESET, 0.0)
            return carry

        lax.fori_loop(0, half + 2, mark, 0)

    def norm_rows(ref, start, size):
        def one(i, carry):
            at_ = rows_at(start + i * 32, 32, 16)
            v = ref[at_, :].astype(F32)
            scale = lax.rsqrt(jnp.sum(v * v, axis=1, keepdims=True) * (1.0 / dmodel) + EPS)
            ref[at_, :] = (v * scale * gain).astype(BF16)
            return carry

        lax.fori_loop(0, size // 32, one, 0)

    span = rd * stretch
    for cp in own_x:
        cp.wait()
    norm_rows(xg, f * span, span)
    xs[0].wait_recv()
    norm_rows(xg, peer[0] * span, span)
    xf = []
    for n, i in enumerate(chips):
        xs[1 + n].wait_recv()
        block = act_rows(lax.bitwise_xor(f, i))
        xf.append(wire.send(xg.at[block], xg.at[block], peer))
    for n, i in enumerate(chips):
        xf[n].wait_recv()
        norm_rows(xg, lax.bitwise_xor(f, i + 1) * span, span)
        wire.sent(xf[n])
        norm_rows(xg, lax.bitwise_xor(f, i) * span, span)
    wif = []
    for n, i in enumerate(range(2, nf)):
        wis[1 + n].wait_recv()
        block = wrows(lax.bitwise_xor(f, i), mine, half_rows)
        wif.append(wire.send(wi.at[block], wi.at[block], beside))

    @pl.when(has_down)
    def _():
        for cp in halos:
            cp.wait_recv()

    hal_rows = rows * HALO
    hflat = vbuf
    for r in range(rows):
        v = hal[r].astype(F32)
        scale = lax.rsqrt(jnp.sum(v * v, axis=1, keepdims=True) * (1.0 / dmodel) + EPS)
        hflat[r * HALO : (r + 1) * HALO, :] = jnp.where(s > 0, v * scale * gain, 0.0).astype(BF16)
    own_wi.wait()
    wis[0].wait_recv()
    for cp in wif:
        cp.wait_recv()
    out_copies = []

    def put(src, dst):
        cp = pltpu.make_async_copy(src, dst, osem.at[len(out_copies)])
        out_copies.append(cp)
        cp.start()

    put(xg, normed_o)
    put(beg, beg_o)
    put(wi, wi_o)

    def inner_row(r, carry):
        v = jnp.dot(xg[rows_at(r * stretch, stretch, 16), :], wi[...], preferred_element_type=F32)
        v = v.astype(BF16).astype(F32)
        n, q = split_at(r, 4)
        base = n * (half * 8 + LEAD) + LEAD + q * 2
        for g in range(2):
            for d in range(groups):
                ext[d, pl.ds(base + g, half, stride=8), :] = v[g * half : (g + 1) * half, cut(d)]
        return carry

    lax.fori_loop(0, rows, inner_row, 0)
    hv = jnp.dot(hflat[...], wi[...], preferred_element_type=F32).astype(BF16).astype(F32)
    for d in range(groups):
        hres[d] = hv[:, cut(d)]
    for n in range(blocks):
        base = n * (half * 8 + LEAD)
        for d in range(groups):
            for j in range(3):
                before = hres[d, pl.ds(n * 4 * HALO + HALO - 3 + j, 4, stride=HALO), :]
                ext[d, pl.ds(base + j * 8, 4, stride=2), :] = before
                own = ext[d, pl.ds(base + LEAD + (half - 3 + j) * 8, 4, stride=2), :]
                ext[d, pl.ds(base + j * 8 + 1, 4, stride=2), :] = own
    put(ext, ext_o)

    span_t = half * 8
    chunk = 64
    per = span_t // chunk

    def conv_chunk(idx, carry):
        nd, c = split_at(idx, per)
        n, d = split_at(nd, groups)
        base = n * (span_t + LEAD) + c * chunk
        bb = n * (span_t + 16) + c * chunk
        same2 = jnp.where(beg[rows_at(bb + 16, chunk), :] > 0.0, 0.0, 1.0)
        same1 = jnp.where(beg[rows_at(bb + 8, chunk), :] > 0.0, 0.0, same2)
        same0 = jnp.where(beg[rows_at(bb, chunk), :] > 0.0, 0.0, same1)
        tap = [ext[d, rows_at(base + k * 8, chunk), :] for k in range(4)]
        v = vecs[d, 4:5, :] + vecs[d, 0:1, :] * (tap[0] * same0)
        v = v + vecs[d, 1:2, :] * (tap[1] * same1) + vecs[d, 2:3, :] * (tap[2] * same2) + vecs[d, 3:4, :] * tap[3]
        sig = jax.nn.sigmoid(v)
        m = (v * sig).astype(BF16)
        at_ = rows_at(n * span_t + c * chunk, chunk)
        slope[d, at_, :] = sig * (1.0 + v * (1.0 - sig))
        mixb[d, rows_at(n * span_t + c * chunk, chunk, 16), :] = m
        mix[d, at_, :] = m.astype(F32)
        return carry

    lax.fori_loop(0, blocks * groups * per, conv_chunk, 0)
    put(slope, slope_o)
    put(mix, mix_o)

    hs = tokens // 2
    other = (1 - core) * hs
    keep = core * hs

    def project(start):
        total = None
        for d in range(groups):
            term = jnp.dot(mixb[d, rows_at(start, hs, 16), :], w_sel[d * 128 : (d + 1) * 128, :], preferred_element_type=F32)
            total = term if total is None else total + term
        part[rows_at(start, hs), :] = total

    project(other)
    one = wire.send(part.at[rows_at(other, hs)], got, peer)
    project(keep)
    one.wait_recv()
    mid[...] = part[rows_at(keep, hs), :] + got[...]
    two = [wire.send(mid, far.at[n], fdev(i)) for n, i in enumerate(chips)]

    cf = []
    for n, i in enumerate(chips):
        cs[1 + n].wait_recv()
        block = act_rows(lax.bitwise_xor(f, i))
        cf.append(wire.send(cg.at[block], cg.at[block], peer))
    wgf = []
    for n, i in enumerate(range(2, nf)):
        wgs[1 + n].wait_recv()
        block = wrows(lax.bitwise_xor(f, i), mine, half_rows)
        wgf.append(wire.send(wg.at[block], wg.at[block], beside))
    for cp in own_c + [own_wg]:
        cp.wait()
    for cp in [cs[0], wgs[0]] + cf + wgf:
        cp.wait_recv()
    put(cg, cg_o)
    put(wg, wg_o)

    def gate_row(r, carry):
        at_ = rows_at(r * stretch, stretch, 16)
        gbuf[0] = jnp.dot(xg[at_, :], wg[...], preferred_element_type=F32).astype(BF16).astype(F32)
        gbuf[1] = times_transposed(cg[at_, :], w_out[...]).astype(BF16).astype(F32)
        n, q = split_at(r, 4)
        base = n * span_t + q * 2
        for g in range(2):
            for d in range(groups):
                def some(i, carry2, g=g, d=d):
                    src = rows_at(g * half + i * 32, 32)
                    v, dg = gbuf[0, src, cut(d)], gbuf[1, src, cut(d)]
                    sig = jax.nn.sigmoid(v)
                    act = v * sig
                    dst = rows_at(r * stretch + g * half + i * 32, 32)
                    ga[dst, cut(d)] = act
                    dgs[dst, cut(d)] = dg * (sig * (1.0 + v * (1.0 - sig)))
                    dy[d, pl.ds(base + g + i * 256, 32, stride=8), :] = dg * act
                    return carry2

                lax.fori_loop(0, half // 32, some, 0)
        return carry

    lax.fori_loop(0, rows, gate_row, 0)
    put(dy, dy_o)
    put(ga, ga_o)
    put(dgs, dgs_o)

    for cp in two:
        cp.wait_recv()
    acc = mid[...]
    for n in range(len(chips)):
        acc = acc + far[n]
    proj[rows_at(keep, hs), :] = acc
    three = wire.send(proj.at[rows_at(keep, hs)], proj.at[rows_at(keep, hs)], peer)

    lane = lax.broadcasted_iota(jnp.int32, (256, 128), 1)

    def step_rows(i, carry):
        at_ = rows_at(carry + i * 256, 256)
        p = proj[at_, :]
        pre = jnp.dot(p[:, :rank].astype(BF16), w_step[...], preferred_element_type=F32)
        for d in range(groups):
            v = pre[:, cut(d)] + vecs[d, 5:6, :]
            step[d, at_, :] = jnp.maximum(v, 0.0) + jnp.log1p(jnp.exp(-jnp.abs(v)))
        top = p.astype(BF16)
        rest = p - top.astype(F32)
        second = rest.astype(BF16)
        third = (rest - second.astype(F32)).astype(BF16).astype(F32)
        width = 2 * nstate
        out = pltpu.roll(top.astype(F32), 128 - rank, 1)
        out = jnp.where(lane < width, out, pltpu.roll(second.astype(F32), (128 - rank + width) % 128, 1))
        out = jnp.where(lane < 2 * width, out, pltpu.roll(third, (128 - rank + 2 * width) % 128, 1))
        packed[rows_at(carry + i * 256, 256, 16), :] = jnp.where(lane < 3 * width, out, 0.0).astype(BF16)
        return carry

    lax.fori_loop(0, hs // 256, step_rows, keep)
    three.wait_recv()
    lax.fori_loop(0, hs // 256, step_rows, other)
    put(step, step_o)
    put(proj, proj_o)
    put(packed, packed_o)
    for cp in out_copies:
        cp.wait()
    wire.drain()

    @pl.when(has_up)
    def _():
        for cp in halos:
            cp.wait_send()

    assert len(wire.copies) == sems


def front(nf, ns, x, ct, w, sm, vecs, w_sel, w_step, w_out, rank, nstate):
    rd, stretch, width = x.shape
    drow = w.shape[0]
    ch = w_step.shape[1]
    groups = ch // 128
    rows = nf * rd
    blocks = rows // 4
    tokens = rows * stretch
    half = stretch // 2
    chips = nf // 2 - 1
    ext_rows = blocks * (half * 8 + LEAD)
    beg_rows = blocks * (half + 2) * 8
    sems = 0
    sems += nf - 1
    sems += 2 * (1 + chips)
    sems += 2 * (nf - 1)
    sems += 2 * chips + 2 * (nf - 2)
    sems += 2 + chips
    shape = jax.ShapeDtypeStruct
    wide = (groups, tokens, 128)
    out_shape = (
        shape((tokens, width), BF16),
        shape((tokens, width), BF16),
        shape((groups, ext_rows, 128), F32),
        shape(wide, F32),
        shape(wide, F32),
        shape(wide, F32),
        shape((tokens, ch), F32),
        shape((tokens, ch), F32),
        shape(wide, F32),
        shape((beg_rows, 128), F32),
        shape((tokens, 128), F32),
        shape((tokens, 128), BF16),
        shape((width, ch), BF16),
        shape((width, ch), BF16),
        shape((16, 128), F32),
    )
    v = pltpu.VMEM
    scratch = [
        v((tokens, width), BF16),
        v((tokens, width), BF16),
        v((width, ch), BF16),
        v((width, ch), BF16),
        v((nf, 16, 128), F32),
        v((rows, HALO, width), BF16),
        v((groups, rows * HALO, 128), F32),
        v((rows * HALO, width), BF16),
        v((2, stretch, ch), F32),
        v((groups, ext_rows, 128), F32),
        v(wide, F32),
        v(wide, F32),
        v(wide, BF16),
        v(wide, F32),
        v((tokens, ch), F32),
        v((tokens, ch), F32),
        v(wide, F32),
        v((beg_rows, 128), F32),
        v((tokens, 128), F32),
        v((tokens // 2, 128), F32),
        v((tokens // 2, 128), F32),
        v((chips, tokens // 2, 128), F32),
        v((tokens, 128), F32),
        v((tokens, 128), BF16),
        pltpu.SemaphoreType.DMA((sems,)),
        pltpu.SemaphoreType.DMA((sems,)),
        pltpu.SemaphoreType.DMA((nf,)),
        pltpu.SemaphoreType.DMA((nf,)),
        pltpu.SemaphoreType.DMA((2 * rd + 3,)),
        pltpu.SemaphoreType.DMA((14,)),
    ]
    return pl.pallas_call(
        functools.partial(front_kernel, nf, ns, rd, rank, nstate, sems),
        out_shape=out_shape,
        in_specs=[ANY] * 4 + [VMEM] * 4,
        out_specs=[ANY] * 14 + [VMEM],
        scratch_shapes=scratch,
        compiler_params=comm_params(0, 62 << 20),
        name="front",
    )(x, ct, w, sm, vecs, w_sel, w_step, w_out)


BLOCK_TOKENS = 1024


def at(t):
    return pl.ds(pl.multiple_of(t * 8, 8), 8)


def cut(d):
    return slice(d * 128, (d + 1) * 128)


def pieces(v, count):
    out = []
    for _ in range(count):
        top = v.astype(BF16)
        out.append(top)
        v = v - top.astype(F32)
    return out


def spread_coefs(packed, cscr, first, count, nstate):
    wide = 2 * count * 128
    source = lax.broadcasted_iota(jnp.int32, (128, wide), 0)
    block = lax.broadcasted_iota(jnp.int32, (128, wide), 1) // 128
    want = jnp.where(block < count, block, nstate - count + block) + first
    pick = jnp.where(
        jnp.logical_and(source % (2 * nstate) == want, source < 6 * nstate), 1.0, 0.0
    ).astype(BF16)
    cscr[...] = jnp.dot(packed, pick, preferred_element_type=F32)


ENDS_UNROLL = 4
SCAN_UNROLL = 4


def scan_specs(tokens, ch, nstate, count):
    blocks = tokens // BLOCK_TOKENS
    groups = ch // 128
    steps = BLOCK_TOKENS // 8
    tok = pl.BlockSpec((groups, BLOCK_TOKENS, 128), lambda n, j: (0, n, 0))
    narrow = pl.BlockSpec((BLOCK_TOKENS, 128), lambda n, j: (n, 0))
    marks = pl.BlockSpec((BLOCK_TOKENS + 16, 128), lambda n, j: (n, 0))
    rates = pl.BlockSpec((1, count, ch), lambda n, j: (j, 0, 0))
    state = pl.BlockSpec((1, count, 8, ch), lambda n, j: (n, j, 0, 0))
    flat = pl.BlockSpec((BLOCK_TOKENS, ch), lambda n, j: (n, 0))
    grid = (blocks, nstate // count)
    kept = pl.BlockSpec((1, steps, count * groups, 8, 128), lambda n, j: (n * grid[1] + j, 0, 0, 0, 0))
    kept_shape = jax.ShapeDtypeStruct((math.prod(grid), steps, count * groups, 8, 128), F32)
    return grid, groups, tok, narrow, marks, rates, state, flat, kept, kept_shape


def rates_of(rate, keys):
    return [jnp.broadcast_to(rate[0, i : i + 1, cut(d)], (8, 128)) for d, i in keys]


def lane_sums(seen, coef, count, first):
    wide = count * 128
    block = lax.broadcasted_iota(jnp.int32, (wide, 128), 0) // 128
    column = lax.broadcasted_iota(jnp.int32, (wide, 128), 1)
    ones = jnp.where(column == block + first, 1.0, 0.0).astype(BF16)
    for part in pieces(seen[...], 2):
        coef[...] += jnp.dot(part, ones, preferred_element_type=F32)


def mid_kernel(nf, ns, reach, count, rank, nstate, *refs):
    (step, mix, dy, beg, packed, rate, vecs, ga_i, dgs_i) = refs[:9]
    (gated, dgate, states_o, coef, lin_o) = refs[9:14]
    (cscr, seen, y, keep, bsc, psc, gsc, run, b_out, g_out, b_in, g_in, t_out, t_up, t_down, ga, dgs) = refs[14:31]
    ssem, rsem, tsem, tsem2, ksem, lsem = refs[31:]
    f, s = here()
    groups = step.shape[0]
    blocks = step.shape[1] // BLOCK_TOKENS
    steps = BLOCK_TOKENS // 8
    parts = nstate // count
    keys = [(d, i) for d in range(groups) for i in range(count)]
    size = len(keys)
    sub = lax.broadcasted_iota(jnp.int32, (8, 128), 0)
    odd = sub % 2 == 1
    zero = jnp.zeros((8, 128), F32)
    slots = parts if blocks == 1 else 1

    peers = []
    for q in range(1, reach + 1):
        peers.append((s + q < ns, (f, s + q)))
        peers.append((s - q >= 0, (f, s - q)))
    greet(peers)
    loads = [pltpu.make_async_copy(ga_i, ga, lsem.at[0]), pltpu.make_async_copy(dgs_i, dgs, lsem.at[1])]
    for cp in loads:
        cp.start()

    def each_way(q, up, down):
        @pl.when(s + q < ns)
        def _():
            up()

        @pl.when(s - q >= 0)
        def _():
            down()

    def starts(cps):
        for cp in cps:
            cp.start()

    def rates(j):
        return [jnp.broadcast_to(rate[d, j * count + i : j * count + i + 1, :], (8, 128)) for d, i in keys]

    def tokens_of(n):
        return slice(n * BLOCK_TOKENS, (n + 1) * BLOCK_TOKENS)

    def row(n, t):
        return rows_at(n * BLOCK_TOKENS + t * 8, 8)

    def marks(n, t):
        return beg[rows_at(n * (BLOCK_TOKENS + 16) + 16 + t * 8, 8), :]

    def pair_up(values, side):
        out = []
        for k in range(0, len(values), 2):
            one, two = values[k], values[k + 1]
            if side:
                out.append(jnp.where(odd, one, pltpu.roll(two, 7, 0)))
            else:
                out.append(jnp.where(odd, pltpu.roll(two, 1, 0), one))
        return out

    def both_rows(v, side):
        return jnp.where(odd, v, pltpu.roll(v, 7, 0)) if side else jnp.where(odd, pltpu.roll(v, 1, 0), v)

    carries = []
    for n in range(blocks):
        for j in range(parts):
            slot = j if blocks == 1 else 0
            spread_coefs(packed[tokens_of(n), :], cscr.at[slot], j * count, count, nstate)
            rt = rates(j)

            def one(t, carry, n=n, j=j, slot=slot, rt=rt):
                bs, ps, gs, rs = carry
                nb, np_, ng, nr = [], [], [], []
                reset = marks(n, t)
                enter = [cscr[slot, at(t), cut(i)] for i in range(count)]
                read = [cscr[slot, at(t), cut(count + i)] for i in range(count)]
                for d in range(groups):
                    st, dt = step[d, row(n, t), :], dy[d, row(n, t), :]
                    ut = st * mix[d, row(n, t), :]
                    st = st + reset
                    if j == 0:
                        nr.append(rs[d] + st)
                    for i in range(count):
                        k = d * count + i
                        a = jnp.exp2(st * rt[k])
                        prod = ps[k] * a
                        nb.append(bs[k] * a + enter[i] * ut)
                        np_.append(prod)
                        ng.append(gs[k] + prod * (read[i] * dt))
                return tuple(nb), tuple(np_), tuple(ng), tuple(nr)

            init = ((zero,) * size, (zero + 1.0,) * size, (zero,) * size, (zero,) * (groups if j == 0 else 0))
            bs, ps, gs, rs = lax.fori_loop(0, steps, one, init, unroll=ENDS_UNROLL)
            if j == 0:
                for d in range(groups):
                    both = rs[d] + jnp.where(odd, pltpu.roll(rs[d], 1, 0), pltpu.roll(rs[d], 7, 0))
                    t_out[n, d] = both
                cps = []
                for q in range(1, reach + 1):
                    cps.append(remote(t_out.at[n], t_up.at[n, q - 1], tsem.at[0, n, q - 1], tsem.at[1, n, q - 1], (f, s + q)))
                    cps.append(remote(t_out.at[n], t_down.at[n, q - 1], tsem2.at[0, n, q - 1], tsem2.at[1, n, q - 1], (f, s - q)))
                    each_way(q, cps[-2].start, cps[-1].start)
                carries.append(cps)
            bd, gd = [], []
            for k in range(size):
                bsc[n, j, k], psc[n, j, k], gsc[n, j, k] = bs[k], ps[k], gs[k]
                bd.append(ps[k] * pltpu.roll(bs[k], 1, 0) + bs[k])
                gd.append(gs[k] + ps[k] * pltpu.roll(gs[k], 7, 0))
            bp, gp = pair_up(bd, True), pair_up(gd, False)
            for k in range(0, size // 2, 2):
                b_out[n, j, k * 8 : k * 8 + 16, :] = jnp.concatenate([bp[k], bp[k + 1]], axis=0).astype(BF16)
                g_out[n, j, k * 8 : k * 8 + 16, :] = jnp.concatenate([gp[k], gp[k + 1]], axis=0).astype(BF16)
            cps = []
            for q in range(1, reach + 1):
                cps.append(
                    remote(b_out.at[n, j], b_in.at[n, j, q - 1], ssem.at[0, n, j, q - 1], rsem.at[0, n, j, q - 1], (f, s + q))
                )
                cps.append(
                    remote(g_out.at[n, j], g_in.at[n, j, q - 1], ssem.at[1, n, j, q - 1], rsem.at[1, n, j, q - 1], (f, s - q))
                )
                each_way(q, cps[-2].start, cps[-1].start)
            carries.append(cps)

    for cp in loads:
        cp.wait()
    coef[...] = jnp.zeros_like(coef)
    outs = []
    order = 0
    for n in range(blocks):
        for d in range(groups):
            y[d] = mix[d, tokens_of(n), :] * vecs[d, 6:7, :]
        for j in range(parts):
            slot = j if blocks == 1 else 0
            if blocks > 1:
                spread_coefs(packed[tokens_of(n), :], cscr.at[slot], j * count, count, nstate)
            mine = [carries[n * (parts + 1) + 1 + j]] + ([carries[n * (parts + 1)]] if j == 0 else [])
            for cps in mine:
                for q in range(1, reach + 1):
                    up, down = cps[2 * q - 2], cps[2 * q - 1]

                    def ahead(up=up, down=down):
                        up.wait_send()
                        down.wait_recv()

                    def behind(up=up, down=down):
                        down.wait_send()
                        up.wait_recv()

                    each_way(q, ahead, behind)
            rt = rates(j)
            hin = [None] * size
            for k in range(0, size, 2):
                h, l = [zero, zero], [zero, zero]
                for q in range(reach - 1, -1, -1):
                    at_ = slice(k * 4, k * 4 + 8)
                    bv, gv = b_in[n, j, q, at_, :].astype(F32), g_in[n, j, q, at_, :].astype(F32)
                    for m in range(2):
                        d = keys[k + m][0]
                        nh = jnp.exp2(rt[k + m] * t_up[n, q, d]) * h[m] + both_rows(bv, m == 0)
                        nl = jnp.exp2(rt[k + m] * t_down[n, q, d]) * l[m] + both_rows(gv, m == 1)
                        h[m] = jnp.where(s - (q + 1) >= 0, nh, 0.0)
                        l[m] = jnp.where(s + (q + 1) < ns, nl, 0.0)
                for m in range(2):
                    d, i = keys[k + m]
                    pv, bv, gv = psc[n, j, k + m], bsc[n, j, k + m], gsc[n, j, k + m]
                    hin[k + m] = jnp.where(odd, pltpu.roll(pv, 1, 0) * h[m] + pltpu.roll(bv, 1, 0), h[m])
                    lin = jnp.where(odd, l[m], pltpu.roll(gv, 7, 0) + pltpu.roll(pv, 7, 0) * l[m])
                    lin_o[n, j * count + i, :, cut(d)] = lin
            kslot = order % 2
            if order >= 2:
                outs[order - 2].wait()

            def forward(t, state, n=n, slot=slot, rt=rt, kslot=kslot):
                reset = marks(n, t)
                enter = [cscr[slot, at(t), cut(i)] for i in range(count)]
                read = [cscr[slot, at(t), cut(count + i)] for i in range(count)]
                new = []
                total = [None] * count
                for d in range(groups):
                    st, dt = step[d, row(n, t), :], dy[d, row(n, t), :]
                    ut = st * mix[d, row(n, t), :]
                    st = st + reset
                    out = None
                    for i in range(count):
                        k = d * count + i
                        a = jnp.exp2(st * rt[k])
                        keep[kslot, t, k] = state[k]
                        h = state[k] * a + enter[i] * ut
                        new.append(h)
                        out = read[i] * h if out is None else out + read[i] * h
                        term = h * dt
                        total[i] = term if total[i] is None else total[i] + term
                    y[d, at(t), :] += out
                for i in range(count):
                    seen[at(t), cut(i)] = total[i]
                return tuple(new)

            lax.fori_loop(0, steps, forward, tuple(hin), unroll=SCAN_UNROLL)
            cp = pltpu.make_async_copy(keep.at[kslot], states_o.at[n * parts + j], ksem.at[order])
            cp.start()
            outs.append(cp)
            order += 1
            lane_sums(seen, coef.at[tokens_of(n)], count, rank + nstate + j * count)

        def some(idx, carry, n=n):
            where, i = split_at(idx, steps // 32)
            q, g = split_at(where, 2)
            for d in range(groups):
                v = y[d, pl.ds(q * 2 + g + i * 256, 32, stride=8), :]
                at_ = rows_at(n * BLOCK_TOKENS + where * steps + i * 32, 32, 16)
                gated[at_, cut(d)] = (v * ga[at_, cut(d)]).astype(BF16)
                dgate[at_, cut(d)] = (v * dgs[at_, cut(d)]).astype(BF16)
            return carry

        lax.fori_loop(0, 8 * (steps // 32), some, 0)
    for cp in outs[-2:]:
        cp.wait()


def middle(nf, ns, cid, reach, step, mix, dy, beg, packed, rate, vecs, ga, dgs, rank, count):
    groups, tokens, _ = step.shape
    nstate, ch = rate.shape[1], groups * 128
    blocks = tokens // BLOCK_TOKENS
    steps = BLOCK_TOKENS // 8
    parts = nstate // count
    size = count * groups
    shape = jax.ShapeDtypeStruct
    v = pltpu.VMEM
    sem = pltpu.SemaphoreType.DMA
    rows_ = size // 2 * 8
    slots = parts if blocks == 1 else 1
    return pl.pallas_call(
        functools.partial(mid_kernel, nf, ns, reach, count, rank, nstate),
        out_shape=(
            shape((tokens, ch), BF16),
            shape((tokens, ch), BF16),
            shape((blocks * parts, steps, size, 8, 128), F32),
            shape((tokens, 128), F32),
            shape((blocks, nstate, 8, ch), F32),
        ),
        in_specs=[VMEM] * 7 + [ANY] * 2,
        out_specs=[VMEM, VMEM, ANY, VMEM, VMEM],
        scratch_shapes=[
            v((slots, BLOCK_TOKENS, 2 * count * 128), F32),
            v((BLOCK_TOKENS, count * 128), F32),
            v((groups, BLOCK_TOKENS, 128), F32),
            v((2, steps, size, 8, 128), F32),
            v((blocks, parts, size, 8, 128), F32),
            v((blocks, parts, size, 8, 128), F32),
            v((blocks, parts, size, 8, 128), F32),
            v((8, 128), F32),
            v((blocks, parts, rows_, 128), BF16),
            v((blocks, parts, rows_, 128), BF16),
            v((blocks, parts, reach, rows_, 128), BF16),
            v((blocks, parts, reach, rows_, 128), BF16),
            v((blocks, groups, 8, 128), F32),
            v((blocks, reach, groups, 8, 128), F32),
            v((blocks, reach, groups, 8, 128), F32),
            v((tokens, ch), F32),
            v((tokens, ch), F32),
            sem((2, blocks, parts, reach)),
            sem((2, blocks, parts, reach)),
            sem((2, blocks, reach)),
            sem((2, blocks, reach)),
            sem((blocks * parts,)),
            sem((2,)),
        ],
        compiler_params=comm_params(cid, 63 << 20),
        name="middle",
    )(step, mix, dy, beg, packed, rate, vecs, ga, dgs)


def backward_kernel(
    count, groups, rank, nstate, step, mix, dy, beg, packed, rate, lin, states, reads, pulled, gs, coef, tot, cscr, seen_scr
):
    j = pl.program_id(1)
    steps = step.shape[1] // 8
    size = count * groups
    keys = [(d, i) for d in range(groups) for i in range(count)]
    rates = rates_of(rate, keys)
    spread_coefs(packed[...], cscr, j * count, count, nstate)

    @pl.when(j == 0)
    def _():
        pulled[...] = jnp.zeros_like(pulled)
        gs[...] = jnp.zeros_like(gs)
        coef[...] = reads[...]

    def backward(k0, carry):
        t = steps - 1 - k0
        passed, sums = carry
        reset = beg[rows_at(16 + t * 8, 8), :]
        enter = [cscr[at(t), cut(i)] for i in range(count)]
        read = [cscr[at(t), cut(count + i)] for i in range(count)]
        new, news = [], []
        seen = [None] * count
        for d in range(groups):
            st, dt = step[d, at(t), :], dy[d, at(t), :]
            ut = st * mix[d, at(t), :]
            st = st + reset
            pull, slope_sum = None, None
            for i in range(count):
                k = d * count + i
                adj = passed[k] + read[i] * dt
                pull = adj * enter[i] if pull is None else pull + adj * enter[i]
                back = adj * jnp.exp2(st * rates[k])
                slope = back * states[0, t, k]
                slope_sum = slope * rates[k] if slope_sum is None else slope_sum + slope * rates[k]
                new.append(back)
                news.append(sums[k] + slope * st)
                term = adj * ut
                seen[i] = term if seen[i] is None else seen[i] + term
            pulled[d, at(t), :] += pull
            gs[d, at(t), :] += slope_sum
        for i in range(count):
            seen_scr[at(t), cut(i)] = seen[i]
        return tuple(new), tuple(news)

    zero = jnp.zeros((8, 128), F32)
    init = (tuple(lin[0, i, :, cut(d)] for d, i in keys), (zero,) * size)
    passed, sums = lax.fori_loop(0, steps, backward, init, unroll=SCAN_UNROLL)
    for n, (d, i) in enumerate(keys):
        line = jnp.sum(sums[n] * rates[n], axis=0, keepdims=True) * LN2
        at_ = pl.ds(j * count + i, 1)

        @pl.when(pl.program_id(0) == 0)
        def _():
            tot[d, at_, :] = line

        @pl.when(pl.program_id(0) > 0)
        def _():
            tot[d, at_, :] += line

    lane_sums(seen_scr, coef, count, rank + j * count)


def scan_backward(step, mix, dy, beg, packed, rate, lin, states, reads, rank, count):
    groups, tokens, _ = step.shape
    nstate, ch = rate.shape
    grid, groups, tok, narrow, marks, rates, state, flat, kept, kept_shape = scan_specs(tokens, ch, nstate, count)
    shape = jax.ShapeDtypeStruct
    work = tokens * nstate * ch
    return pl.pallas_call(
        functools.partial(backward_kernel, count, groups, rank, nstate),
        out_shape=(
            shape(step.shape, F32),
            shape(step.shape, F32),
            shape((tokens, 128), F32),
            shape((groups, nstate, 128), F32),
        ),
        grid=grid,
        in_specs=[tok, tok, tok, marks, narrow, rates, state, kept, narrow],
        out_specs=[tok, tok, narrow, pl.BlockSpec((groups, nstate, 128), lambda n, j: (0, 0, 0))],
        scratch_shapes=[
            pltpu.VMEM((BLOCK_TOKENS, 2 * count * 128), F32),
            pltpu.VMEM((BLOCK_TOKENS, count * 128), F32),
        ],
        compiler_params=pltpu.CompilerParams(vmem_limit_bytes=60 << 20),
        cost_estimate=pl.CostEstimate(flops=12 * work, bytes_accessed=4 * work, transcendentals=work),
        name="scan_backward",
    )(step, mix, dy, beg, packed, rate.reshape(nstate // count, count, ch), lin, states, reads)


class Stream:
    def __init__(self, wire, place, src, got_y, mid, got_z, red, fin, out):
        self.wire, self.place = wire, place
        self.src, self.got_y, self.mid, self.got_z = src, got_y, mid, got_z
        self.red, self.fin, self.out = red, fin, out

    def start(self):
        p = self.place
        self.y = self.wire.send(self.src.at[:, 1 - p.b], self.got_y, p.beside)

    def across(self):
        p = self.place
        self.y.wait_recv()
        self.mid[...] = (self.src[:, p.b].astype(F32) + self.got_y[...].astype(F32)).astype(self.mid.dtype)
        self.z = [
            self.wire.send(self.mid.at[:, lax.bitwise_xor(p.a, i)], self.got_z.at[i - 1], p.zdev(i))
            for i in range(1, p.na)
        ]

    def swap(self):
        p = self.place
        for cp in self.z:
            cp.wait_recv()
        acc = self.mid[:, p.a].astype(F32)
        for i in range(1, p.na):
            acc = acc + self.got_z[i - 1].astype(F32)
        self.red[...] = acc.astype(self.red.dtype)
        self.w = [
            self.wire.send(self.red.at[lax.bitwise_xor(p.f, i)], self.fin.at[p.f], p.fdev(i)) for i in range(1, p.nf)
        ]
        self.fin[p.f] = self.red[p.f]

    def spread(self):
        p = self.place
        for cp in self.w:
            cp.wait_recv()
        self.out[p.b, p.a] = self.fin[...]
        self.g = [(self.wire.send(self.fin, self.out.at[p.b, p.a], p.zdev(i)), i) for i in range(1, p.na)]
        self.h = [self.wire.send(self.fin, self.out.at[p.b, p.a], p.beside)]

    def forward(self):
        p = self.place
        for cp, i in self.g:
            cp.wait_recv()
            block = self.out.at[p.b, lax.bitwise_xor(p.a, i)]
            self.h.append(self.wire.send(block, block, p.beside))

    def finish(self):
        for cp in self.h:
            cp.wait_recv()


class Place:
    def __init__(self, nf, ns):
        self.f, self.s = here()
        self.nf, self.ns, self.na = nf, ns, ns // 2
        self.a, self.b = lax.div(self.s, 2), lax.rem(self.s, 2)
        self.core = lax.rem(self.f, 2)
        self.peer = (lax.bitwise_xor(self.f, 1), self.s)
        self.beside = (self.f, lax.bitwise_xor(self.s, 1))

    def fdev(self, i):
        return (lax.bitwise_xor(self.f, i), self.s)

    def zdev(self, i):
        return (self.f, lax.bitwise_xor(self.a, i) * 2 + self.b)


def small_layout(groups, rank, nstate, ns):
    select, step, decay, vectors = 0, 128, 128 + rank, 128 + rank + nstate
    group = vectors + 8
    piece = -(-group * groups // (8 * ns)) * 8
    return select, step, decay, vectors, group, piece


def post_kernel(nf, ns, nq, rd, rank, nstate, sems, *refs):
    (pulled_i, slopes_i, mix_i, step_i, dy_i, slope_i, ext_i, beg_i, normed_i, wi_i, wg_i, dgate_i) = refs[:12]
    (ce, proj, vecs, w_sel, w_step, table, x, ct, decay) = refs[12:21]
    gates = refs[21 : 21 + nq]
    refs = refs[21 + nq :]
    rout, gain_out, small_out = refs[:3]
    outs = refs[3 : 3 + 2 * nq]
    refs = refs[3 + 2 * nq :]
    (pulled, slopes, mix, step, dy, slope, ext, beg, normed, wi, wg, dgate) = refs[:12]
    (mixb, dlin, dproj, dib, part, got, mid, far, sums) = refs[12:21]
    dconv, dp = mix, normed
    (near_d, mid_d, far_d, gain_l, gain_f, gain_m, gain_y, gain_n, gain_z, small, small_y, small_m, small_z) = refs[21:34]
    (edge_o, edge_i) = refs[34:36]
    refs = refs[36:]
    inners = refs[:nq]
    refs = refs[nq:]
    bufs = [refs[n * 2 * nq : (n + 1) * 2 * nq] for n in range(5)]
    ssem, rsem, lsem, esem = refs[10 * nq :]

    place = Place(nf, ns)
    f, s, a, b, core = place.f, place.s, place.a, place.b, place.core
    na = place.na
    chips = list(range(2, nf, 2))
    groups, tokens, _ = pulled.shape
    ch = groups * 128
    stretch = tokens // (nf * rd)
    half = stretch // 2
    span_t = half * 8
    blocks = tokens // span_t
    width = normed.shape[1]
    off_select, off_step, off_decay, off_vec, group_rows, piece = small_layout(groups, rank, nstate, ns)
    has_up, has_down = s + 1 < ns, s >= 1
    greet(
        [(None, place.fdev(i)) for i in range(1, nf)]
        + [(None, place.beside)]
        + [(None, place.zdev(i)) for i in range(1, na)]
        + [(has_up, (f, s + 1)), (has_down, (f, s - 1))]
    )
    wire = Wire(ssem, rsem)
    streams = []
    for n in range(2 * nq):
        src = gates[n] if n < nq else inners[n - nq]
        streams.append(Stream(wire, place, src, *[v[n] for v in bufs], outs[n]))
    for n in range(nq):
        streams[n].start()

    loads = []

    def load(src, dst):
        cp = pltpu.make_async_copy(src, dst, lsem.at[len(loads)])
        loads.append(cp)
        cp.start()
        return cp

    hs = tokens // 2
    other, keep = (1 - core) * hs, core * hs
    first = [(pulled_i, pulled), (slopes_i, slopes), (mix_i, mix), (step_i, step), (dy_i, dy)]
    by_half = []
    for start in (other, keep):
        rows_ = rows_at(start, hs)
        by_half.append([load(src.at[:, rows_], dst.at[:, rows_]) for src, dst in first])
    conv_in = [load(slope_i, slope), load(ext_i, ext), load(beg_i, beg.at[pl.ds(0, beg_i.shape[0])])]
    late = [load(normed_i, normed), load(wi_i, wi), load(wg_i, wg), load(dgate_i, dgate)]
    for d in range(groups):
        small[d * group_rows + off_decay : d * group_rows + off_vec, :] = decay[d]
        small[d * group_rows + off_vec : (d + 1) * group_rows, :] = jnp.zeros((8, 128), F32)
    rest = small.shape[0] - groups * group_rows
    if rest:
        small[groups * group_rows :, :] = jnp.zeros((rest, 128), F32)
    beg[beg_i.shape[0] :, :] = jnp.zeros((24, 128), F32)

    chunk = 64

    def fold(v):
        out = v[0:8]
        for q in range(1, v.shape[0] // 8):
            out = out + v[q * 8 : (q + 1) * 8]
        return out

    def add_row(d, k, v):
        at_ = slice(d * group_rows + off_vec + k, d * group_rows + off_vec + k + 1)
        small[at_, :] += jnp.sum(v, axis=0, keepdims=True)

    zero = jnp.zeros((8, 128), F32)

    def step_half(start, cps):
        for cp in cps:
            cp.wait()
        for d in range(groups):

            def one(c, carry, d=d):
                at_ = rows_at(start + c * chunk, chunk)
                pu, m, st, dv = pulled[d, at_, :], mix[d, at_, :], step[d, at_, :], dy[d, at_, :]
                tiny = st * (1.0 - st * (0.5 - st * (1.0 / 6.0 - st * (1.0 / 24.0))))
                sig = jnp.where(st < 0.03, tiny, 1.0 - jnp.exp(-st))
                dpre = (m * pu + slopes[d, at_, :] * LN2) * sig
                low_at = rows_at(start + c * chunk, chunk, 16)
                dlin[d, low_at, :] = dpre.astype(BF16)
                mixb[d, low_at, :] = m.astype(BF16)
                pulled[d, at_, :] = st * pu + dv * vecs[d, 6:7, :]
                return carry[0] + fold(dpre), carry[1] + fold(dv * m)

            bias, skip = lax.fori_loop(0, hs // chunk, one, (zero, zero))
            add_row(d, 5, bias)
            add_row(d, 6, skip)
        at_ = rows_at(start, hs)
        total = None
        for d in range(groups):
            term = times_transposed(dlin[d, rows_at(start, hs, 16), :], w_step[:, cut(d)])
            total = term if total is None else total + term
        part[at_, :] = ce[at_, :]
        part[at_, :rank] += total

    step_half(other, by_half[0])
    one = wire.send(part.at[rows_at(other, hs)], got, place.peer)
    step_half(keep, by_half[1])
    one.wait_recv()
    mid[...] = part[rows_at(keep, hs), :] + got[...]
    two = [wire.send(mid, far.at[n], place.fdev(i)) for n, i in enumerate(chips)]

    for d in range(groups):
        low = proj[...][:, :rank].astype(BF16)
        small[d * group_rows + off_step : d * group_rows + off_decay, :] = rows_inner(low, dlin[d])
    for n in range(nq):
        streams[n].across()

    for cp in two:
        cp.wait_recv()
    acc = mid[...]
    for n in range(len(chips)):
        acc = acc + far[n]
    sums[rows_at(keep, hs), :] = acc
    three = wire.send(sums.at[rows_at(keep, hs)], sums.at[rows_at(keep, hs)], place.peer)
    for cp in conv_in:
        cp.wait()

    def mask_at(base, k):
        out = jnp.where(beg[rows_at(base + 16, chunk), :] > 0.0, 0.0, 1.0)
        if k <= 1:
            out = jnp.where(beg[rows_at(base + 8, chunk), :] > 0.0, 0.0, out)
        if k == 0:
            out = jnp.where(beg[rows_at(base, chunk), :] > 0.0, 0.0, out)
        return out

    def conv_half(start):
        at_all = rows_at(start, hs)
        low_all = rows_at(start, hs, 16)
        dproj[low_all, :] = sums[at_all, :].astype(BF16)
        for d in range(groups):
            slopes[d, at_all, :] = times_transposed(dproj[low_all, :], w_sel[d * 128 : (d + 1) * 128, :])

            def one(c, carry, d=d):
                row = start + c * chunk
                n, inside = split_at(row, span_t)
                at_ = rows_at(row, chunk)
                v = (pulled[d, at_, :] + slopes[d, at_, :]) * slope[d, at_, :]
                base = n * (span_t + LEAD)
                dconv[d, rows_at(base + inside, chunk), :] = v
                bb = n * (span_t + 16) + inside
                out = [carry[0] + fold(v)]
                for k in range(4):
                    tap = ext[d, rows_at(base + inside + k * 8, chunk), :]
                    w = v * tap if k == 3 else v * tap * mask_at(bb, k)
                    out.append(carry[1 + k] + fold(w))
                return tuple(out)

            totals = lax.fori_loop(0, hs // chunk, one, (zero,) * 5)
            add_row(d, 4, totals[0])
            for k in range(4):
                add_row(d, k, totals[1 + k])

    for n in range(blocks):
        for d in range(groups):
            dconv[d, n * (span_t + LEAD) + span_t : (n + 1) * (span_t + LEAD), :] = jnp.zeros((LEAD, 128), F32)
    conv_half(keep)
    three.wait_recv()
    conv_half(other)

    sub = lax.broadcasted_iota(jnp.int32, (8, 128), 0)
    for n in range(blocks):
        base = n * (span_t + LEAD)
        bb = n * (span_t + 16)
        hit = [jnp.where(beg[bb + q * 8 : bb + q * 8 + 8, :] > 0.0, 0.0, 1.0) for q in range(5)]
        for d in range(groups):
            tail = [zero] * 3
            for q in range(3):
                v = dconv[d, base + q * 8 : base + q * 8 + 8, :]
                keepers = [hit[q + 2] * hit[q + 1] * hit[q], hit[q + 2] * hit[q + 1], hit[q + 2]]
                for k in range(3 - q):
                    tail[q + k] = tail[q + k] + vecs[d, k : k + 1, :] * (v * keepers[k])
            for q in range(3):
                edge_o[d, n * 24 + q * 8 : n * 24 + q * 8 + 8, :] = tail[q]
    edge = remote(edge_o, edge_i, esem.at[0], esem.at[1], (f, s - 1))

    @pl.when(has_down)
    def _():
        edge.start()

    for n in range(nq):
        streams[n].swap()

    per = span_t // chunk

    def inner_chunk(idx, carry):
        nd, c = split_at(idx, per)
        n, d = split_at(nd, groups)
        base = n * (span_t + LEAD) + c * chunk
        bb = n * (span_t + 16) + c * chunk
        acc = vecs[d, 3:4, :] * dconv[d, rows_at(base, chunk), :]
        for k in range(3):
            ahead = (3 - k) * 8
            acc = acc + vecs[d, k : k + 1, :] * (dconv[d, rows_at(base + ahead, chunk), :] * mask_at(bb + ahead, k))
        pulled[d, rows_at(n * span_t + c * chunk, chunk), :] = acc
        return carry

    lax.fori_loop(0, blocks * groups * per, inner_chunk, 0)

    for d in range(groups):
        small[d * group_rows + off_select : d * group_rows + off_step, :] = rows_inner(mixb[d], dproj[...])
    small_half = na * piece
    small_ys = wire.send(small.at[rows_at((1 - b) * small_half, small_half)], small_y, place.beside)
    for n in range(nq):
        streams[n].spread()

    @pl.when(has_up)
    def _():
        edge.wait_recv()

    for n in range(blocks):
        for d in range(groups):
            for q in range(3):
                at_ = slice(n * 24 + q * 8, n * 24 + q * 8 + 8)
                inward = pltpu.roll(edge_o[d, at_, :], 7, 0)
                outer = jnp.where(has_up, pltpu.roll(edge_i[d, at_, :], 1, 0), 0.0)
                row = n * span_t + (half - 3 + q) * 8
                pulled[d, row : row + 8, :] += jnp.where(sub % 2 == 0, inward, outer)

    def to_rows(idx, carry):
        r_g, i = split_at(idx, half // 32)
        r, g = split_at(r_g, 2)
        n, q = split_at(r, 4)
        at_ = rows_at(r_g * half + i * 32, 32, 16)
        for d in range(groups):
            v = pulled[d, pl.ds(n * span_t + q * 2 + g + i * 256, 32, stride=8), :]
            dib[at_, cut(d)] = v.astype(BF16)
        return carry

    lax.fori_loop(0, 2 * nf * rd * (half // 32), to_rows, 0)

    for cp in late:
        cp.wait()
    drow = width // nf
    prow = drow // ns
    lanes = max(drow, 128)
    cq = ch // nq
    for q in range(nq):

        def grad_block(k, carry, q=q):
            v = rows_inner(normed[:, pl.ds(pl.multiple_of(k * lanes, 128), lanes)], dib[:, q * cq : (q + 1) * cq])
            for m in range(lanes // drow):
                for p in range(ns):
                    r = m * drow + p * prow
                    piece_v = v[r : r + prow].astype(inners[q].dtype)
                    inners[q][k * (lanes // drow) + m, p // na, p % na] = piece_v
            return carry

        lax.fori_loop(0, width // lanes, grad_block, 0)
        streams[nq + q].start()

    span = rd * stretch

    def dn_rows(flip):
        def one(n, carry):
            who = lax.bitwise_xor(lax.bitwise_xor(f, flip), 2 * n)
            for q in range(rd):
                at_ = rows_at(who * span + q * stretch, stretch, 16)
                v = times_transposed(dib[at_, :], wi[...]) + times_transposed(dgate[at_, :], wg[...])
                dp[at_, :] = v.astype(BF16)
            return carry

        lax.fori_loop(0, nf // 2, one, 0)

    def dp_rows(who):
        return rows_at(who * span, span, 16)

    dn_rows(1)
    near = [
        wire.send(dp.at[dp_rows(lax.bitwise_xor(lax.bitwise_xor(f, 1), i))], near_d.at[n], place.peer)
        for n, i in enumerate([0] + chips)
    ]
    dn_rows(0)
    fars = []
    for n, i in reversed(list(enumerate([0] + chips))):
        near[n].wait_recv()
        if i:
            dest = lax.bitwise_xor(f, i)
            mid_d[n - 1] = (dp[dp_rows(dest), :].astype(F32) + near_d[n].astype(F32)).astype(BF16)
            fars.append(wire.send(mid_d.at[n - 1], far_d.at[n - 1], place.fdev(i)))
    for n in range(nq):
        streams[n].forward()
    small_ys.wait_recv()
    small_m[...] = small[rows_at(b * small_half, small_half), :] + small_y[...]

    def owned(who):
        return rows_at(who * piece, piece)

    small_zs = [
        wire.send(small_m.at[owned(lax.bitwise_xor(a, i))], small_z.at[i - 1], place.zdev(i)) for i in range(1, na)
    ]
    for n in range(nq, 2 * nq):
        streams[n].across()

    gain = jnp.concatenate([table[q : q + 1, :] for q in range(width // 128)], axis=1)
    for cp in fars:
        cp.wait_recv()

    def own_rows(i, total):
        at_ = rows_at(i * 16, 16, 16)
        v = x[at_, :].astype(F32)
        scale = lax.rsqrt(jnp.sum(v * v, axis=1, keepdims=True) * (1.0 / width) + EPS)
        hat = v * scale
        dn = dp[rows_at(f * span + i * 16, 16, 16), :].astype(F32) + near_d[0, at_, :].astype(F32)
        for n in range(len(chips)):
            dn = dn + far_d[n, at_, :].astype(F32)
        dh = dn * gain
        inner = jnp.sum(dh * hat, axis=1, keepdims=True) * (1.0 / width)
        rout[at_, :] = ct[at_, :].astype(F32) + scale * (dh - hat * inner)
        return total + jnp.sum(dn * hat, axis=0, keepdims=True)

    gain_l[...] = lax.fori_loop(0, x.shape[0] // 16, own_rows, jnp.zeros((1, width), F32))
    gain_a = [wire.send(gain_l, gain_f.at[i - 1], place.fdev(i)) for i in range(1, nf)]
    for cp in small_zs:
        cp.wait_recv()
    acc = small_m[owned(a), :]
    for i in range(1, na):
        acc = acc + small_z[i - 1]
    mine = rows_at(b * small_half + a * piece, piece)
    small_out[mine, :] = acc
    small_g = [(wire.send(small_out.at[mine], small_out.at[mine], place.zdev(i)), i) for i in range(1, na)]
    small_h = [wire.send(small_out.at[mine], small_out.at[mine], place.beside)]
    for n in range(nq, 2 * nq):
        streams[n].swap()
    for cp in gain_a:
        cp.wait_recv()
    acc = gain_l[...]
    for i in range(1, nf):
        acc = acc + gain_f[i - 1]
    gain_m[...] = acc
    gain_b = wire.send(gain_m, gain_y, place.beside)
    for n in range(nq, 2 * nq):
        streams[n].spread()
    for cp, i in small_g:
        cp.wait_recv()
        theirs = rows_at(b * small_half + lax.bitwise_xor(a, i) * piece, piece)
        small_h.append(wire.send(small_out.at[theirs], small_out.at[theirs], place.beside))
    gain_b.wait_recv()
    gain_n[...] = gain_m[...] + gain_y[...]
    gain_c = [wire.send(gain_n, gain_z.at[i - 1], place.zdev(i)) for i in range(1, na)]
    for n in range(nq, 2 * nq):
        streams[n].forward()
    for cp in gain_c:
        cp.wait_recv()
    acc = gain_n[...]
    for i in range(1, na):
        acc = acc + gain_z[i - 1]
    gain_out[...] = acc
    for cp in small_h:
        cp.wait_recv()
    for st in streams:
        st.finish()
    wire.drain()

    @pl.when(has_down)
    def _():
        edge.wait_send()

    assert len(wire.copies) == sems


def post(nf, ns, nq, cid, rd, rank, nstate, big, little, gates):
    shape = jax.ShapeDtypeStruct
    v = pltpu.VMEM
    pulled, ext, beg, normed, wi = big[0], big[6], big[7], big[8], big[9]
    x = little[6]
    groups, tokens, _ = pulled.shape
    ch = groups * 128
    width = normed.shape[1]
    na = ns // 2
    chips = nf // 2 - 1
    block = x.shape
    piece_shape = gates[0].shape[3:]
    piece = small_layout(groups, rank, nstate, ns)[-1]
    total = piece * ns
    hs = tokens // 2
    blocks = tokens // BLOCK_TOKENS
    stream = 1 + (na - 1) + (nf - 1) + (na - 1) + 1 + (na - 1)
    sems = 2 * nq * stream
    sems += 2 + chips
    sems += 1 + 2 * chips
    sems += 1 + (na - 1) + (na - 1) + 1 + (na - 1)
    sems += (nf - 1) + 1 + (na - 1)
    outs = [shape(block, F32), shape((1, width), F32), shape((total, 128), F32)]
    kind = gates[0].dtype
    outs += [shape((2, na, nf) + piece_shape, kind)] * (2 * nq)
    scratch = [v(m.shape, m.dtype) for m in big]
    scratch[2] = v(ext.shape, F32)
    scratch[7] = v((beg.shape[0] + 24, 128), F32)
    scratch += [
        v(pulled.shape, BF16),
        v(pulled.shape, BF16),
        v((tokens, 128), BF16),
        v((tokens, ch), BF16),
        v((tokens, 128), F32),
        v((hs, 128), F32),
        v((hs, 128), F32),
        v((chips, hs, 128), F32),
        v((tokens, 128), F32),
        v((chips + 1,) + block, BF16),
        v((chips,) + block, BF16),
        v((chips,) + block, BF16),
        v((1, width), F32),
        v((nf - 1, 1, width), F32),
        v((1, width), F32),
        v((1, width), F32),
        v((1, width), F32),
        v((na - 1, 1, width), F32),
        v((total, 128), F32),
        v((na * piece, 128), F32),
        v((na * piece, 128), F32),
        v((na - 1, piece, 128), F32),
        v((groups, blocks * 24, 128), F32),
        v((groups, blocks * 24, 128), F32),
    ]
    scratch += [v(gates[0].shape, kind)] * nq
    scratch += [v((nf, na) + piece_shape, kind)] * (2 * nq)
    scratch += [v((nf, na) + piece_shape, kind)] * (2 * nq)
    scratch += [v((na - 1, nf) + piece_shape, kind)] * (2 * nq)
    scratch += [v((nf,) + piece_shape, kind)] * (2 * nq)
    scratch += [v((nf,) + piece_shape, kind)] * (2 * nq)
    scratch += [
        pltpu.SemaphoreType.DMA((sems,)),
        pltpu.SemaphoreType.DMA((sems,)),
        pltpu.SemaphoreType.DMA((17,)),
        pltpu.SemaphoreType.DMA((2,)),
    ]
    return pl.pallas_call(
        functools.partial(post_kernel, nf, ns, nq, rd, rank, nstate, sems),
        out_shape=outs,
        in_specs=[ANY] * 12 + [VMEM] * (9 + nq),
        out_specs=[VMEM] * len(outs),
        scratch_shapes=scratch,
        compiler_params=comm_params(cid, 63 << 20),
        name="post",
    )(*big, *little, *gates)


def last_kernel(ns, nf, nq, ni, rank, nstate, nsel, nextra, *refs):
    gates, inners = refs[:nq], refs[nq : nq + ni]
    og, x, rout, small = refs[nq + ni : nq + ni + 4]
    extras = refs[nq + ni + 4 : nq + ni + 4 + nextra]
    outs = refs[nq + ni + 4 + nextra :]
    layer, residual, grad_o, taps, select, step, decay, vectors, ogf, grad, sem = outs
    groups = select.shape[0] // 128
    ch = groups * 128
    na = ns // 2
    prow = gates[0].shape[3]
    inner_all = nf * ch
    copies = []
    for p in range(ns):
        at_ = slice(p * prow, (p + 1) * prow)
        for parts, base in ((inners, 0), (gates, inner_all)):
            cq = ch // len(parts)
            for q, part in enumerate(parts):
                for k in range(nf):
                    start = base + k * ch + q * cq
                    grad[at_, start : start + cq] = part[p // na, p % na, k].astype(F32)
        if prow % 8 == 0:
            copies.append(pltpu.make_async_copy(grad.at[at_], grad_o.at[at_], sem.at[p]))
            copies[-1].start()
    if prow % 8:
        copies.append(pltpu.make_async_copy(grad, grad_o, sem.at[0]))
        copies[-1].start()
    ogf[...] = og[...].astype(F32)
    residual[...] = rout[...]
    total = x[...].astype(F32)
    for e in extras:
        total = total + e[...].astype(F32)
    layer[...] = total.astype(BF16)
    off_select, off_step, off_decay, off_vec, group_rows, _ = small_layout(groups, rank, nstate, ns)
    for d in range(groups):
        base = d * group_rows
        select[d * 128 : (d + 1) * 128, :] = small[base + off_select : base + off_step, :].astype(F32)[:, :nsel]
        step[:, cut(d)] = small[base + off_step : base + off_decay, :].astype(F32)
        decay[:, cut(d)] = small[base + off_decay : base + off_vec, :].astype(F32)
        line = small[base + off_vec : base + group_rows, :].astype(F32)
        vectors[:, cut(d)] = line
        taps[:, cut(d)] = line[:4]
    for cp in copies:
        cp.wait()


def last(nf, ns, rank, nstate, nsel, gates, inners, og, x, rout, small, extras):
    shape = jax.ShapeDtypeStruct
    nq, ni = len(gates), len(inners)
    ch = og.shape[0]
    drow = gates[0].shape[3] * ns
    return pl.pallas_call(
        functools.partial(last_kernel, ns, nf, nq, ni, rank, nstate, nsel, len(extras)),
        out_shape=(
            shape(x.shape, BF16),
            shape(rout.shape, F32),
            shape((drow, 2 * nf * ch), F32),
            shape((4, ch), F32),
            shape((ch, nsel), F32),
            shape((rank, ch), F32),
            shape((nstate, ch), F32),
            shape((8, ch), F32),
            shape(og.shape, F32),
        ),
        in_specs=[VMEM] * (nq + ni + 4 + len(extras)),
        out_specs=[VMEM, VMEM, ANY] + [VMEM] * 6,
        scratch_shapes=[pltpu.VMEM((drow, 2 * nf * ch), F32), pltpu.SemaphoreType.DMA((ns,))],
        compiler_params=pltpu.CompilerParams(vmem_limit_bytes=56 << 20),
        name="last",
    )(*gates, *inners, og, x, rout, small, *extras)


def rows_inner(left, right):
    return lax.dot_general(left, right, (((0,), (0,)), ((), ())), preferred_element_type=F32)


def times_transposed(left, right):
    return lax.dot_general(left, right, (((1,), (1,)), ((), ())), preferred_element_type=F32)


def silu_slope(value):
    sig = jax.nn.sigmoid(value)
    return sig * (1.0 + value * (1.0 - sig))


def shards(
    nf,
    ns,
    residual,
    out_cotangent,
    doc_lengths,
    norm_gain,
    input_proj,
    conv_kernel,
    conv_bias,
    select_proj,
    step_proj,
    step_bias,
    log_decay,
    skip_gain,
    output_proj,
):
    rd, stretch, width = residual.shape
    rows = nf * rd
    docs = doc_lengths.shape[1]
    ch = conv_bias.shape[0]
    rank = step_proj.shape[0]
    nstate = log_decay.shape[0]
    taps = conv_kernel.shape[0]
    edge = taps - 1
    tokens = rows * stretch
    half = stretch // 2
    blocks = rows // 4
    f, s = here()
    reach = -(-(stretch * ns // 2 - 1) // stretch)
    count = 4

    groups = ch // 128
    grows = norm_gain.shape[0]
    spot = lax.broadcasted_iota(jnp.int32, (width,), 0) // grows == f
    small = jnp.where(spot, jnp.tile(norm_gain.astype(F32), nf), 0.0).reshape(width // 128, 128)
    marks = jnp.pad(doc_lengths.astype(F32), ((0, 8 - rd), (0, 128 - docs)))
    small = jnp.concatenate([small, marks], axis=0)
    vecs = jnp.concatenate(
        [conv_kernel, conv_bias[None], step_bias[None], skip_gain[None], jnp.zeros((1, ch), BF16)], axis=0
    ).astype(F32)
    vecs = jnp.moveaxis(vecs.reshape(8, groups, 128), 1, 0)
    w_sel = jnp.pad(select_proj, ((0, 0), (0, 128 - select_proj.shape[1])))
    normed, cot, ext, slope, mix, dy, ga, dgs, step, beg, proj, packed, w_inner, w_gate, gain = front(
        nf, ns, residual, out_cotangent, input_proj, small, vecs, w_sel, step_proj, output_proj, rank, nstate
    )
    rate = -jnp.exp(log_decay.astype(F32))
    rate2 = rate * LOG2E

    rates = jnp.moveaxis(rate2.reshape(nstate, groups, 128), 1, 0)
    gated, d_gate, states, coef_read, lin = middle(
        nf, ns, 2, reach, step, mix, dy, beg, packed, rates, vecs, ga, dgs, rank, count
    )
    nq = 2 if ch % 256 == 0 else 1
    cq = ch // nq
    piece_rows = width // nf // ns
    kind = BF16
    output_grad = rows_inner(gated, cot).astype(BF16)
    out_part = jnp.dot(gated, output_proj, preferred_element_type=F32).astype(BF16)
    gate_grads = [
        rows_inner(normed, d_gate[:, q * cq : (q + 1) * cq]).astype(kind).reshape(nf, 2, ns // 2, piece_rows, cq)
        for q in range(nq)
    ]
    output_grad, out_part, lin, *gate_grads = lax.optimization_barrier((output_grad, out_part, lin, *gate_grads))
    output_grad = lax.psum(output_grad, "seq")
    out_sum = lax.psum_scatter(out_part, "fsdp", scatter_dimension=0, tiled=True)

    pulled, slopes, coefs, decay = scan_backward(step, mix, dy, beg, packed, rate2, lin, states, coef_read, rank, count)
    big = (pulled, slopes, mix, step, dy, slope, ext, beg, normed, w_inner, w_gate, d_gate)
    little = (
        coefs,
        proj,
        vecs,
        w_sel,
        step_proj,
        gain,
        residual.reshape(rd * stretch, width),
        out_cotangent.reshape(rd * stretch, width),
        decay,
    )
    residual_grad, gain_sum, small_sum, *sums = post(nf, ns, nq, 3, rd, rank, nstate, big, little, gate_grads)
    layer_output, residual_grad, input_grad, kernel_grad, select_grad, step_grad, decay_grad, vectors, output_grad = last(
        nf,
        ns,
        rank,
        nstate,
        select_proj.shape[1],
        sums[:nq],
        sums[nq:],
        output_grad,
        residual.reshape(rd * stretch, width),
        residual_grad,
        small_sum,
        [out_sum],
    )
    return (
        layer_output.reshape(rd, stretch, width),
        residual_grad.reshape(rd, stretch, width),
        lax.dynamic_slice(gain_sum[0], (f * grows,), (grows,)),
        input_grad,
        kernel_grad,
        vectors[4],
        select_grad,
        step_grad,
        vectors[5],
        decay_grad,
        vectors[6],
        output_grad,
    )


def solution(mesh):
    nf, ns = mesh.shape["fsdp"], mesh.shape["seq"]
    in_specs = (
        P("fsdp", "seq", None),
        P("fsdp", "seq", None),
        P("fsdp", None),
        P("fsdp"),
        P("fsdp", None),
        P(None, "fsdp"),
        P("fsdp"),
        P("fsdp", None),
        P(None, "fsdp"),
        P("fsdp"),
        P(None, "fsdp"),
        P("fsdp"),
        P("fsdp", None),
    )
    out_specs = (
        P("fsdp", "seq", None),
        P("fsdp", "seq", None),
        P("fsdp"),
        P("fsdp", None),
        P(None, "fsdp"),
        P("fsdp"),
        P("fsdp", None),
        P(None, "fsdp"),
        P("fsdp"),
        P(None, "fsdp"),
        P("fsdp"),
        P("fsdp", None),
    )
    return jax.shard_map(
        functools.partial(shards, nf, ns), mesh=mesh, in_specs=in_specs, out_specs=out_specs, check_vma=False
    )
```

```python
import functools
import math

import jax
import jax.numpy as jnp
from jax import lax
from jax.experimental import pallas as pl
from jax.experimental.pallas import tpu as pltpu
from jax.sharding import PartitionSpec as P

EPS = 1e-05
MESH = pl.DeviceIdType.MESH
LOG2E = math.log2(math.e)
LN2 = math.log(2.0)
BF16 = jnp.bfloat16
F32 = jnp.float32
ANY = pl.BlockSpec(memory_space=pl.ANY)
VMEM = pl.BlockSpec(memory_space=pltpu.VMEM)
RESET = 1e30
HALO = 16
DOCS = 8


def here():
    return lax.axis_index("fsdp"), lax.axis_index("seq")


def greet(peers):
    barrier = pltpu.get_barrier_semaphore()
    count = 0
    for ok, device in peers:
        if ok is None:
            pl.semaphore_signal(barrier, inc=1, device_id=device, device_id_type=MESH)
            count = count + 1
        else:

            @pl.when(ok)
            def _():
                pl.semaphore_signal(barrier, inc=1, device_id=device, device_id_type=MESH)

            count = count + ok.astype(jnp.int32)
    pl.semaphore_wait(barrier, count)


def remote(src, dst, send, recv, device):
    return pltpu.make_async_remote_copy(
        src_ref=src, dst_ref=dst, send_sem=send, recv_sem=recv, device_id=device, device_id_type=MESH
    )


def comm_params(cid, vmem=None):
    return pltpu.CompilerParams(collective_id=cid, has_side_effects=True, vmem_limit_bytes=vmem)


class Wire:
    def __init__(self, ssem, rsem):
        self.ssem, self.rsem, self.copies, self.done = ssem, rsem, [], []

    def send(self, src, dst, device):
        k = len(self.copies)
        cp = remote(src, dst, self.ssem.at[k], self.rsem.at[k], device)
        self.copies.append(cp)
        cp.start()
        return cp

    def sent(self, cp):
        cp.wait_send()
        self.done.append(cp)

    def drain(self):
        for cp in self.copies:
            if all(cp is not other for other in self.done):
                cp.wait_send()


LEAD = 24


def rows_at(base, size, unit=8):
    return pl.ds(pl.multiple_of(base, unit), size)


def split_at(i, n):
    return lax.div(i, n), lax.rem(i, n)


def front_kernel(nf, ns, rd, rank, nstate, sems, *refs):
    (x, ct, w, sm, vecs, w_sel, w_step, w_out) = refs[:8]
    (normed_o, cg_o, ext_o, slope_o, mix_o, dy_o, ga_o, dgs_o, step_o, beg_o, proj_o, packed_o, wi_o, wg_o, gain_o) = refs[8:23]
    (xg, cg, wi, wg, sg, hal, hres, vbuf, gbuf, ext, slope, mix, mixb, dy, ga, dgs, step, beg, part, got, mid, far, proj, packed) = refs[
        23:47
    ]
    ssem, rsem, hsem, hrem, lsem, osem = refs[47:]
    f, s = here()
    core, b = lax.rem(f, 2), lax.rem(s, 2)
    stretch = x.shape[1]
    half = stretch // 2
    dmodel = xg.shape[1]
    ch = wi.shape[1]
    groups = ch // 128
    rows = nf * rd
    blocks = rows // 4
    tokens = rows * stretch
    drow = w.shape[0]
    inner_all = w.shape[1] // 2
    chips = list(range(2, nf, 2))
    peer = (lax.bitwise_xor(f, 1), s)
    beside = (f, lax.bitwise_xor(s, 1))
    up, down = s + 1, s - 1
    has_up, has_down = up < ns, down >= 0

    def fdev(i):
        return (lax.bitwise_xor(f, i), s)

    greeted = [(None, fdev(i)) for i in range(1, nf)] + [(None, beside)]
    for i in range(nf):
        greeted.append((has_up, (lax.bitwise_xor(f, i), up)))
        greeted.append((has_down, (lax.bitwise_xor(f, i), down)))
    greet(greeted)
    wire = Wire(ssem, rsem)

    def act_rows(who):
        return rows_at(who * (rd * stretch), rd * stretch, 16)

    def wcols(who, base, start, size):
        return w.at[pl.ds(start, size), pl.ds(pl.multiple_of(base + who * ch, 128), ch)]

    def wrows(who, start, size):
        return pl.ds(pl.multiple_of(who * drow + start, 16), size)

    half_rows = drow // 2
    mine = pl.multiple_of(b * half_rows, 16)

    locals_ = []

    def local(src, dst):
        cp = pltpu.make_async_copy(src, dst, lsem.at[len(locals_)])
        locals_.append(cp)
        cp.start()
        return cp

    x2 = [x.at[q] for q in range(rd)]
    smalls = [wire.send(sm, sg.at[f], fdev(i)) for i in range(1, nf)]
    own_x = [local(x2[q], xg.at[rows_at((f * rd + q) * stretch, stretch, 16)]) for q in range(rd)]
    own_s = local(sm, sg.at[f])

    def send_rows(src, dst):
        if rd == 1:
            return [wire.send(src.at[0], dst.at[act_rows(f)], fdev(i)) for i in [1] + chips]
        return [wire.send(src, dst.at[act_rows(f)], fdev(i)) for i in [1] + chips]

    def send_weight(base, dst):
        out = [wire.send(wcols(peer[0], base, 0, drow), dst.at[wrows(f, 0, drow)], peer)]
        for i in range(2, nf):
            out.append(
                wire.send(wcols(lax.bitwise_xor(f, i), base, mine, half_rows), dst.at[wrows(f, mine, half_rows)], fdev(i))
            )
        return out

    xs = send_rows(x, xg)
    wis = send_weight(0, wi)
    halos = [
        remote(
            x.at[:, pl.ds(stretch - HALO, HALO), :],
            hal.at[pl.ds(f * rd, rd)],
            hsem.at[i],
            hrem.at[i],
            (lax.bitwise_xor(f, i), up),
        )
        for i in range(nf)
    ]

    @pl.when(has_up)
    def _():
        for cp in halos:
            cp.start()

    own_wi = local(wcols(f, 0, 0, drow), wi.at[wrows(f, 0, drow)])
    cs = send_rows(ct, cg)
    wgs = send_weight(inner_all, wg)
    own_c = [local(ct.at[q], cg.at[rows_at((f * rd + q) * stretch, stretch, 16)]) for q in range(rd)]
    own_wg = local(wcols(f, inner_all, 0, drow), wg.at[wrows(f, 0, drow)])

    own_s.wait()
    for cp in smalls:
        cp.wait_recv()
    table = sg[0]
    for k in range(1, nf):
        table = table + sg[k]
    gain = jnp.concatenate([table[q : q + 1, :] for q in range(dmodel // 128)], axis=1)
    gain_o[...] = table
    sub = lax.broadcasted_iota(jnp.int32, (8, 128), 0)
    for n in range(blocks):
        lens = jnp.zeros((8, 128), F32)
        for q in range(4):
            r = n * 4 + q
            line = sg[r // rd, 8 + r % rd : 9 + r % rd, :]
            lens = jnp.where(sub // 2 == q, jnp.broadcast_to(line, (8, 128)), lens)
        starts = [jnp.zeros((8, 128), F32)]
        for j in range(DOCS - 1):
            starts.append(starts[-1] + jnp.broadcast_to(lens[:, j : j + 1], (8, 128)))
        first = (s * stretch + (sub % 2) * half).astype(F32)

        def mark(t, carry, n=n, starts=starts, first=first):
            place = first + (t - 2).astype(F32)
            hit = starts[0] == place
            for j in range(1, DOCS):
                hit = jnp.logical_or(hit, starts[j] == place)
            beg[rows_at(n * (half + 2) * 8 + t * 8, 8), :] = jnp.where(hit, RESET, 0.0)
            return carry

        lax.fori_loop(0, half + 2, mark, 0)

    def norm_rows(ref, start, size):
        def one(i, carry):
            at_ = rows_at(start + i * 32, 32, 16)
            v = ref[at_, :].astype(F32)
            scale = lax.rsqrt(jnp.sum(v * v, axis=1, keepdims=True) * (1.0 / dmodel) + EPS)
            ref[at_, :] = (v * scale * gain).astype(BF16)
            return carry

        lax.fori_loop(0, size // 32, one, 0)

    span = rd * stretch
    for cp in own_x:
        cp.wait()
    norm_rows(xg, f * span, span)
    xs[0].wait_recv()
    norm_rows(xg, peer[0] * span, span)
    xf = []
    for n, i in enumerate(chips):
        xs[1 + n].wait_recv()
        block = act_rows(lax.bitwise_xor(f, i))
        xf.append(wire.send(xg.at[block], xg.at[block], peer))
    for n, i in enumerate(chips):
        xf[n].wait_recv()
        norm_rows(xg, lax.bitwise_xor(f, i + 1) * span, span)
        wire.sent(xf[n])
        norm_rows(xg, lax.bitwise_xor(f, i) * span, span)
    wif = []
    for n, i in enumerate(range(2, nf)):
        wis[1 + n].wait_recv()
        block = wrows(lax.bitwise_xor(f, i), mine, half_rows)
        wif.append(wire.send(wi.at[block], wi.at[block], beside))

    @pl.when(has_down)
    def _():
        for cp in halos:
            cp.wait_recv()

    hal_rows = rows * HALO
    hflat = vbuf
    for r in range(rows):
        v = hal[r].astype(F32)
        scale = lax.rsqrt(jnp.sum(v * v, axis=1, keepdims=True) * (1.0 / dmodel) + EPS)
        hflat[r * HALO : (r + 1) * HALO, :] = jnp.where(s > 0, v * scale * gain, 0.0).astype(BF16)
    own_wi.wait()
    wis[0].wait_recv()
    for cp in wif:
        cp.wait_recv()
    out_copies = []

    def put(src, dst):
        cp = pltpu.make_async_copy(src, dst, osem.at[len(out_copies)])
        out_copies.append(cp)
        cp.start()

    put(xg, normed_o)
    put(beg, beg_o)
    put(wi, wi_o)

    def inner_row(r, carry):
        v = jnp.dot(xg[rows_at(r * stretch, stretch, 16), :], wi[...], preferred_element_type=F32)
        v = v.astype(BF16).astype(F32)
        n, q = split_at(r, 4)
        base = n * (half * 8 + LEAD) + LEAD + q * 2
        for g in range(2):
            for d in range(groups):
                ext[d, pl.ds(base + g, half, stride=8), :] = v[g * half : (g + 1) * half, cut(d)]
        return carry

    lax.fori_loop(0, rows, inner_row, 0)
    hv = jnp.dot(hflat[...], wi[...], preferred_element_type=F32).astype(BF16).astype(F32)
    for d in range(groups):
        hres[d] = hv[:, cut(d)]
    for n in range(blocks):
        base = n * (half * 8 + LEAD)
        for d in range(groups):
            for j in range(3):
                before = hres[d, pl.ds(n * 4 * HALO + HALO - 3 + j, 4, stride=HALO), :]
                ext[d, pl.ds(base + j * 8, 4, stride=2), :] = before
                own = ext[d, pl.ds(base + LEAD + (half - 3 + j) * 8, 4, stride=2), :]
                ext[d, pl.ds(base + j * 8 + 1, 4, stride=2), :] = own
    put(ext, ext_o)

    span_t = half * 8
    chunk = 64
    per = span_t // chunk

    def conv_chunk(idx, carry):
        nd, c = split_at(idx, per)
        n, d = split_at(nd, groups)
        base = n * (span_t + LEAD) + c * chunk
        bb = n * (span_t + 16) + c * chunk
        same2 = jnp.where(beg[rows_at(bb + 16, chunk), :] > 0.0, 0.0, 1.0)
        same1 = jnp.where(beg[rows_at(bb + 8, chunk), :] > 0.0, 0.0, same2)
        same0 = jnp.where(beg[rows_at(bb, chunk), :] > 0.0, 0.0, same1)
        tap = [ext[d, rows_at(base + k * 8, chunk), :] for k in range(4)]
        v = vecs[d, 4:5, :] + vecs[d, 0:1, :] * (tap[0] * same0)
        v = v + vecs[d, 1:2, :] * (tap[1] * same1) + vecs[d, 2:3, :] * (tap[2] * same2) + vecs[d, 3:4, :] * tap[3]
        sig = jax.nn.sigmoid(v)
        m = (v * sig).astype(BF16)
        at_ = rows_at(n * span_t + c * chunk, chunk)
        slope[d, at_, :] = sig * (1.0 + v * (1.0 - sig))
        mixb[d, rows_at(n * span_t + c * chunk, chunk, 16), :] = m
        mix[d, at_, :] = m.astype(F32)
        return carry

    lax.fori_loop(0, blocks * groups * per, conv_chunk, 0)
    put(slope, slope_o)
    put(mix, mix_o)

    hs = tokens // 2
    other = (1 - core) * hs
    keep = core * hs

    def project(start):
        total = None
        for d in range(groups):
            term = times_transposed(mixb[d, rows_at(start, hs, 16), :], w_sel[:, cut(d)])
            total = term if total is None else total + term
        part[rows_at(start, hs), :] = total

    project(other)
    one = wire.send(part.at[rows_at(other, hs)], got, peer)
    project(keep)
    one.wait_recv()
    mid[...] = part[rows_at(keep, hs), :] + got[...]
    two = [wire.send(mid, far.at[n], fdev(i)) for n, i in enumerate(chips)]

    cf = []
    for n, i in enumerate(chips):
        cs[1 + n].wait_recv()
        block = act_rows(lax.bitwise_xor(f, i))
        cf.append(wire.send(cg.at[block], cg.at[block], peer))
    wgf = []
    for n, i in enumerate(range(2, nf)):
        wgs[1 + n].wait_recv()
        block = wrows(lax.bitwise_xor(f, i), mine, half_rows)
        wgf.append(wire.send(wg.at[block], wg.at[block], beside))
    for cp in own_c + [own_wg]:
        cp.wait()
    for cp in [cs[0], wgs[0]] + cf + wgf:
        cp.wait_recv()
    put(cg, cg_o)
    put(wg, wg_o)

    def gate_row(r, carry):
        at_ = rows_at(r * stretch, stretch, 16)
        gbuf[0] = jnp.dot(xg[at_, :], wg[...], preferred_element_type=F32).astype(BF16).astype(F32)
        gbuf[1] = times_transposed(cg[at_, :], w_out[...]).astype(BF16).astype(F32)
        n, q = split_at(r, 4)
        base = n * span_t + q * 2
        for g in range(2):
            for d in range(groups):
                def some(i, carry2, g=g, d=d):
                    src = rows_at(g * half + i * 32, 32)
                    v, dg = gbuf[0, src, cut(d)], gbuf[1, src, cut(d)]
                    sig = jax.nn.sigmoid(v)
                    act = v * sig
                    dst = rows_at(r * stretch + g * half + i * 32, 32)
                    ga[dst, cut(d)] = act
                    dgs[dst, cut(d)] = dg * (sig * (1.0 + v * (1.0 - sig)))
                    dy[d, pl.ds(base + g + i * 256, 32, stride=8), :] = dg * act
                    return carry2

                lax.fori_loop(0, half // 32, some, 0)
        return carry

    lax.fori_loop(0, rows, gate_row, 0)
    put(dy, dy_o)
    put(ga, ga_o)
    put(dgs, dgs_o)

    for cp in two:
        cp.wait_recv()
    acc = mid[...]
    for n in range(len(chips)):
        acc = acc + far[n]
    proj[rows_at(keep, hs), :] = acc
    three = wire.send(proj.at[rows_at(keep, hs)], proj.at[rows_at(keep, hs)], peer)

    lane = lax.broadcasted_iota(jnp.int32, (256, 128), 1)

    def step_rows(i, carry):
        at_ = rows_at(carry + i * 256, 256)
        p = proj[at_, :]
        pre = jnp.dot(p[:, :rank].astype(BF16), w_step[...], preferred_element_type=F32)
        for d in range(groups):
            v = pre[:, cut(d)] + vecs[d, 5:6, :]
            step[d, at_, :] = jnp.maximum(v, 0.0) + jnp.log1p(jnp.exp(-jnp.abs(v)))
        top = p.astype(BF16)
        rest = p - top.astype(F32)
        second = rest.astype(BF16)
        third = (rest - second.astype(F32)).astype(BF16).astype(F32)
        width = 2 * nstate
        out = pltpu.roll(top.astype(F32), 128 - rank, 1)
        out = jnp.where(lane < width, out, pltpu.roll(second.astype(F32), (128 - rank + width) % 128, 1))
        out = jnp.where(lane < 2 * width, out, pltpu.roll(third, (128 - rank + 2 * width) % 128, 1))
        packed[rows_at(carry + i * 256, 256, 16), :] = jnp.where(lane < 3 * width, out, 0.0).astype(BF16)
        return carry

    lax.fori_loop(0, hs // 256, step_rows, keep)
    three.wait_recv()
    lax.fori_loop(0, hs // 256, step_rows, other)
    put(step, step_o)
    put(proj, proj_o)
    put(packed, packed_o)
    for cp in out_copies:
        cp.wait()
    wire.drain()

    @pl.when(has_up)
    def _():
        for cp in halos:
            cp.wait_send()

    assert len(wire.copies) == sems


def front(nf, ns, x, ct, w, sm, vecs, w_sel, w_step, w_out, rank, nstate):
    rd, stretch, width = x.shape
    drow = w.shape[0]
    ch = w_step.shape[1]
    groups = ch // 128
    rows = nf * rd
    blocks = rows // 4
    tokens = rows * stretch
    half = stretch // 2
    chips = nf // 2 - 1
    ext_rows = blocks * (half * 8 + LEAD)
    beg_rows = blocks * (half + 2) * 8
    sems = 0
    sems += nf - 1
    sems += 2 * (1 + chips)
    sems += 2 * (nf - 1)
    sems += 2 * chips + 2 * (nf - 2)
    sems += 2 + chips
    shape = jax.ShapeDtypeStruct
    wide = (groups, tokens, 128)
    out_shape = (
        shape((tokens, width), BF16),
        shape((tokens, width), BF16),
        shape((groups, ext_rows, 128), F32),
        shape(wide, F32),
        shape(wide, F32),
        shape(wide, F32),
        shape((tokens, ch), F32),
        shape((tokens, ch), F32),
        shape(wide, F32),
        shape((beg_rows, 128), F32),
        shape((tokens, 128), F32),
        shape((tokens, 128), BF16),
        shape((width, ch), BF16),
        shape((width, ch), BF16),
        shape((16, 128), F32),
    )
    v = pltpu.VMEM
    scratch = [
        v((tokens, width), BF16),
        v((tokens, width), BF16),
        v((width, ch), BF16),
        v((width, ch), BF16),
        v((nf, 16, 128), F32),
        v((rows, HALO, width), BF16),
        v((groups, rows * HALO, 128), F32),
        v((rows * HALO, width), BF16),
        v((2, stretch, ch), F32),
        v((groups, ext_rows, 128), F32),
        v(wide, F32),
        v(wide, F32),
        v(wide, BF16),
        v(wide, F32),
        v((tokens, ch), F32),
        v((tokens, ch), F32),
        v(wide, F32),
        v((beg_rows, 128), F32),
        v((tokens, 128), F32),
        v((tokens // 2, 128), F32),
        v((tokens // 2, 128), F32),
        v((chips, tokens // 2, 128), F32),
        v((tokens, 128), F32),
        v((tokens, 128), BF16),
        pltpu.SemaphoreType.DMA((sems,)),
        pltpu.SemaphoreType.DMA((sems,)),
        pltpu.SemaphoreType.DMA((nf,)),
        pltpu.SemaphoreType.DMA((nf,)),
        pltpu.SemaphoreType.DMA((2 * rd + 3,)),
        pltpu.SemaphoreType.DMA((14,)),
    ]
    return pl.pallas_call(
        functools.partial(front_kernel, nf, ns, rd, rank, nstate, sems),
        out_shape=out_shape,
        in_specs=[ANY] * 4 + [VMEM] * 4,
        out_specs=[ANY] * 14 + [VMEM],
        scratch_shapes=scratch,
        compiler_params=comm_params(0, 62 << 20),
        name="front",
    )(x, ct, w, sm, vecs, w_sel, w_step, w_out)


BLOCK_TOKENS = 1024


def at(t):
    return pl.ds(pl.multiple_of(t * 8, 8), 8)


def cut(d):
    return slice(d * 128, (d + 1) * 128)


def pieces(v, count):
    out = []
    for _ in range(count):
        top = v.astype(BF16)
        out.append(top)
        v = v - top.astype(F32)
    return out


def spread_coefs(packed, cscr, first, count, nstate):
    wide = 2 * count * 128
    source = lax.broadcasted_iota(jnp.int32, (128, wide), 0)
    block = lax.broadcasted_iota(jnp.int32, (128, wide), 1) // 128
    want = jnp.where(block < count, block, nstate - count + block) + first
    pick = jnp.where(
        jnp.logical_and(source % (2 * nstate) == want, source < 6 * nstate), 1.0, 0.0
    ).astype(BF16)
    cscr[...] = jnp.dot(packed, pick, preferred_element_type=F32)


ENDS_UNROLL = 4
SCAN_UNROLL = 4


def scan_specs(tokens, ch, nstate, count):
    blocks = tokens // BLOCK_TOKENS
    groups = ch // 128
    steps = BLOCK_TOKENS // 8
    tok = pl.BlockSpec((groups, BLOCK_TOKENS, 128), lambda n, j: (0, n, 0))
    narrow = pl.BlockSpec((BLOCK_TOKENS, 128), lambda n, j: (n, 0))
    marks = pl.BlockSpec((BLOCK_TOKENS + 16, 128), lambda n, j: (n, 0))
    rates = pl.BlockSpec((1, count, ch), lambda n, j: (j, 0, 0))
    state = pl.BlockSpec((1, count, 8, ch), lambda n, j: (n, j, 0, 0))
    flat = pl.BlockSpec((BLOCK_TOKENS, ch), lambda n, j: (n, 0))
    grid = (blocks, nstate // count)
    kept = pl.BlockSpec((1, steps, count * groups, 8, 128), lambda n, j: (n * grid[1] + j, 0, 0, 0, 0))
    kept_shape = jax.ShapeDtypeStruct((math.prod(grid), steps, count * groups, 8, 128), F32)
    return grid, groups, tok, narrow, marks, rates, state, flat, kept, kept_shape


def rates_of(rate, keys):
    return [jnp.broadcast_to(rate[0, i : i + 1, cut(d)], (8, 128)) for d, i in keys]


def lane_sums(seen, coef, count, first):
    wide = count * 128
    block = lax.broadcasted_iota(jnp.int32, (wide, 128), 0) // 128
    column = lax.broadcasted_iota(jnp.int32, (wide, 128), 1)
    ones = jnp.where(column == block + first, 1.0, 0.0).astype(BF16)
    for part in pieces(seen[...], 2):
        coef[...] += jnp.dot(part, ones, preferred_element_type=F32)


def mid_kernel(nf, ns, reach, count, rank, nstate, *refs):
    (step, mix, dy, beg, packed, rate, vecs, ga_i, dgs_i) = refs[:9]
    (gated, dgate, states_o, coef, lin_o) = refs[9:14]
    (cscr, seen, y, keep, bsc, psc, gsc, run, b_out, g_out, b_in, g_in, t_out, t_up, t_down, ga, dgs) = refs[14:31]
    ssem, rsem, tsem, tsem2, ksem, lsem = refs[31:]
    f, s = here()
    groups = step.shape[0]
    blocks = step.shape[1] // BLOCK_TOKENS
    steps = BLOCK_TOKENS // 8
    parts = nstate // count
    keys = [(d, i) for d in range(groups) for i in range(count)]
    size = len(keys)
    sub = lax.broadcasted_iota(jnp.int32, (8, 128), 0)
    odd = sub % 2 == 1
    zero = jnp.zeros((8, 128), F32)
    slots = parts if blocks == 1 else 1

    peers = []
    for q in range(1, reach + 1):
        peers.append((s + q < ns, (f, s + q)))
        peers.append((s - q >= 0, (f, s - q)))
    greet(peers)
    loads = [pltpu.make_async_copy(ga_i, ga, lsem.at[0]), pltpu.make_async_copy(dgs_i, dgs, lsem.at[1])]
    for cp in loads:
        cp.start()

    def each_way(q, up, down):
        @pl.when(s + q < ns)
        def _():
            up()

        @pl.when(s - q >= 0)
        def _():
            down()

    def starts(cps):
        for cp in cps:
            cp.start()

    def rates(j):
        return [jnp.broadcast_to(rate[d, j * count + i : j * count + i + 1, :], (8, 128)) for d, i in keys]

    def tokens_of(n):
        return slice(n * BLOCK_TOKENS, (n + 1) * BLOCK_TOKENS)

    def row(n, t):
        return rows_at(n * BLOCK_TOKENS + t * 8, 8)

    def marks(n, t):
        return beg[rows_at(n * (BLOCK_TOKENS + 16) + 16 + t * 8, 8), :]

    def pair_up(values, side):
        out = []
        for k in range(0, len(values), 2):
            one, two = values[k], values[k + 1]
            if side:
                out.append(jnp.where(odd, one, pltpu.roll(two, 7, 0)))
            else:
                out.append(jnp.where(odd, pltpu.roll(two, 1, 0), one))
        return out

    def both_rows(v, side):
        return jnp.where(odd, v, pltpu.roll(v, 7, 0)) if side else jnp.where(odd, pltpu.roll(v, 1, 0), v)

    carries = []
    for n in range(blocks):
        for j in range(parts):
            slot = j if blocks == 1 else 0
            spread_coefs(packed[tokens_of(n), :], cscr.at[slot], j * count, count, nstate)
            rt = rates(j)

            def one(t, carry, n=n, j=j, slot=slot, rt=rt):
                bs, ps, gs, rs = carry
                nb, np_, ng, nr = [], [], [], []
                reset = marks(n, t)
                enter = [cscr[slot, at(t), cut(i)] for i in range(count)]
                read = [cscr[slot, at(t), cut(count + i)] for i in range(count)]
                for d in range(groups):
                    st, dt = step[d, row(n, t), :], dy[d, row(n, t), :]
                    ut = st * mix[d, row(n, t), :]
                    st = st + reset
                    if j == 0:
                        nr.append(rs[d] + st)
                    for i in range(count):
                        k = d * count + i
                        a = jnp.exp2(st * rt[k])
                        prod = ps[k] * a
                        nb.append(bs[k] * a + enter[i] * ut)
                        np_.append(prod)
                        ng.append(gs[k] + prod * (read[i] * dt))
                return tuple(nb), tuple(np_), tuple(ng), tuple(nr)

            init = ((zero,) * size, (zero + 1.0,) * size, (zero,) * size, (zero,) * (groups if j == 0 else 0))
            bs, ps, gs, rs = lax.fori_loop(0, steps, one, init, unroll=ENDS_UNROLL)
            if j == 0:
                for d in range(groups):
                    both = rs[d] + jnp.where(odd, pltpu.roll(rs[d], 1, 0), pltpu.roll(rs[d], 7, 0))
                    t_out[n, d] = both
                cps = []
                for q in range(1, reach + 1):
                    cps.append(remote(t_out.at[n], t_up.at[n, q - 1], tsem.at[0, n, q - 1], tsem.at[1, n, q - 1], (f, s + q)))
                    cps.append(remote(t_out.at[n], t_down.at[n, q - 1], tsem2.at[0, n, q - 1], tsem2.at[1, n, q - 1], (f, s - q)))
                    each_way(q, cps[-2].start, cps[-1].start)
                carries.append(cps)
            bd, gd = [], []
            for k in range(size):
                bsc[n, j, k], psc[n, j, k], gsc[n, j, k] = bs[k], ps[k], gs[k]
                bd.append(ps[k] * pltpu.roll(bs[k], 1, 0) + bs[k])
                gd.append(gs[k] + ps[k] * pltpu.roll(gs[k], 7, 0))
            bp, gp = pair_up(bd, True), pair_up(gd, False)
            for k in range(0, size // 2, 2):
                b_out[n, j, k * 8 : k * 8 + 16, :] = jnp.concatenate([bp[k], bp[k + 1]], axis=0).astype(BF16)
                g_out[n, j, k * 8 : k * 8 + 16, :] = jnp.concatenate([gp[k], gp[k + 1]], axis=0).astype(BF16)
            cps = []
            for q in range(1, reach + 1):
                cps.append(
                    remote(b_out.at[n, j], b_in.at[n, j, q - 1], ssem.at[0, n, j, q - 1], rsem.at[0, n, j, q - 1], (f, s + q))
                )
                cps.append(
                    remote(g_out.at[n, j], g_in.at[n, j, q - 1], ssem.at[1, n, j, q - 1], rsem.at[1, n, j, q - 1], (f, s - q))
                )
                each_way(q, cps[-2].start, cps[-1].start)
            carries.append(cps)

    for cp in loads:
        cp.wait()
    coef[...] = jnp.zeros_like(coef)
    outs = []
    order = 0
    for n in range(blocks):
        for d in range(groups):
            y[d] = mix[d, tokens_of(n), :] * vecs[d, 6:7, :]
        for j in range(parts):
            slot = j if blocks == 1 else 0
            if blocks > 1:
                spread_coefs(packed[tokens_of(n), :], cscr.at[slot], j * count, count, nstate)
            mine = [carries[n * (parts + 1) + 1 + j]] + ([carries[n * (parts + 1)]] if j == 0 else [])
            for cps in mine:
                for q in range(1, reach + 1):
                    up, down = cps[2 * q - 2], cps[2 * q - 1]

                    def ahead(up=up, down=down):
                        up.wait_send()
                        down.wait_recv()

                    def behind(up=up, down=down):
                        down.wait_send()
                        up.wait_recv()

                    each_way(q, ahead, behind)
            rt = rates(j)
            hin = [None] * size
            for k in range(0, size, 2):
                h, l = [zero, zero], [zero, zero]
                for q in range(reach - 1, -1, -1):
                    at_ = slice(k * 4, k * 4 + 8)
                    bv, gv = b_in[n, j, q, at_, :].astype(F32), g_in[n, j, q, at_, :].astype(F32)
                    for m in range(2):
                        d = keys[k + m][0]
                        nh = jnp.exp2(rt[k + m] * t_up[n, q, d]) * h[m] + both_rows(bv, m == 0)
                        nl = jnp.exp2(rt[k + m] * t_down[n, q, d]) * l[m] + both_rows(gv, m == 1)
                        h[m] = jnp.where(s - (q + 1) >= 0, nh, 0.0)
                        l[m] = jnp.where(s + (q + 1) < ns, nl, 0.0)
                for m in range(2):
                    d, i = keys[k + m]
                    pv, bv, gv = psc[n, j, k + m], bsc[n, j, k + m], gsc[n, j, k + m]
                    hin[k + m] = jnp.where(odd, pltpu.roll(pv, 1, 0) * h[m] + pltpu.roll(bv, 1, 0), h[m])
                    lin = jnp.where(odd, l[m], pltpu.roll(gv, 7, 0) + pltpu.roll(pv, 7, 0) * l[m])
                    lin_o[n, j * count + i, :, cut(d)] = lin
            kslot = order % 2
            if order >= 2:
                outs[order - 2].wait()

            def forward(t, state, n=n, slot=slot, rt=rt, kslot=kslot):
                reset = marks(n, t)
                enter = [cscr[slot, at(t), cut(i)] for i in range(count)]
                read = [cscr[slot, at(t), cut(count + i)] for i in range(count)]
                new = []
                total = [None] * count
                for d in range(groups):
                    st, dt = step[d, row(n, t), :], dy[d, row(n, t), :]
                    ut = st * mix[d, row(n, t), :]
                    st = st + reset
                    out = None
                    for i in range(count):
                        k = d * count + i
                        a = jnp.exp2(st * rt[k])
                        keep[kslot, t, k] = state[k]
                        h = state[k] * a + enter[i] * ut
                        new.append(h)
                        out = read[i] * h if out is None else out + read[i] * h
                        term = h * dt
                        total[i] = term if total[i] is None else total[i] + term
                    y[d, at(t), :] += out
                for i in range(count):
                    seen[at(t), cut(i)] = total[i]
                return tuple(new)

            lax.fori_loop(0, steps, forward, tuple(hin), unroll=SCAN_UNROLL)
            cp = pltpu.make_async_copy(keep.at[kslot], states_o.at[n * parts + j], ksem.at[order])
            cp.start()
            outs.append(cp)
            order += 1
            lane_sums(seen, coef.at[tokens_of(n)], count, rank + nstate + j * count)

        def some(idx, carry, n=n):
            where, i = split_at(idx, steps // 32)
            q, g = split_at(where, 2)
            for d in range(groups):
                v = y[d, pl.ds(q * 2 + g + i * 256, 32, stride=8), :]
                at_ = rows_at(n * BLOCK_TOKENS + where * steps + i * 32, 32, 16)
                gated[at_, cut(d)] = (v * ga[at_, cut(d)]).astype(BF16)
                dgate[at_, cut(d)] = (v * dgs[at_, cut(d)]).astype(BF16)
            return carry

        lax.fori_loop(0, 8 * (steps // 32), some, 0)
    for cp in outs[-2:]:
        cp.wait()


def middle(nf, ns, cid, reach, step, mix, dy, beg, packed, rate, vecs, ga, dgs, rank, count):
    groups, tokens, _ = step.shape
    nstate, ch = rate.shape[1], groups * 128
    blocks = tokens // BLOCK_TOKENS
    steps = BLOCK_TOKENS // 8
    parts = nstate // count
    size = count * groups
    shape = jax.ShapeDtypeStruct
    v = pltpu.VMEM
    sem = pltpu.SemaphoreType.DMA
    rows_ = size // 2 * 8
    slots = parts if blocks == 1 else 1
    return pl.pallas_call(
        functools.partial(mid_kernel, nf, ns, reach, count, rank, nstate),
        out_shape=(
            shape((tokens, ch), BF16),
            shape((tokens, ch), BF16),
            shape((blocks * parts, steps, size, 8, 128), F32),
            shape((tokens, 128), F32),
            shape((blocks, nstate, 8, ch), F32),
        ),
        in_specs=[VMEM] * 7 + [ANY] * 2,
        out_specs=[VMEM, VMEM, ANY, VMEM, VMEM],
        scratch_shapes=[
            v((slots, BLOCK_TOKENS, 2 * count * 128), F32),
            v((BLOCK_TOKENS, count * 128), F32),
            v((groups, BLOCK_TOKENS, 128), F32),
            v((2, steps, size, 8, 128), F32),
            v((blocks, parts, size, 8, 128), F32),
            v((blocks, parts, size, 8, 128), F32),
            v((blocks, parts, size, 8, 128), F32),
            v((8, 128), F32),
            v((blocks, parts, rows_, 128), BF16),
            v((blocks, parts, rows_, 128), BF16),
            v((blocks, parts, reach, rows_, 128), BF16),
            v((blocks, parts, reach, rows_, 128), BF16),
            v((blocks, groups, 8, 128), F32),
            v((blocks, reach, groups, 8, 128), F32),
            v((blocks, reach, groups, 8, 128), F32),
            v((tokens, ch), F32),
            v((tokens, ch), F32),
            sem((2, blocks, parts, reach)),
            sem((2, blocks, parts, reach)),
            sem((2, blocks, reach)),
            sem((2, blocks, reach)),
            sem((blocks * parts,)),
            sem((2,)),
        ],
        compiler_params=comm_params(cid, 63 << 20),
        name="middle",
    )(step, mix, dy, beg, packed, rate, vecs, ga, dgs)


def backward_kernel(
    count, groups, rank, nstate, step, mix, dy, beg, packed, rate, lin, states, reads, pulled, gs, coef, tot, cscr, seen_scr
):
    j = pl.program_id(1)
    steps = step.shape[1] // 8
    size = count * groups
    keys = [(d, i) for d in range(groups) for i in range(count)]
    rates = rates_of(rate, keys)
    spread_coefs(packed[...], cscr, j * count, count, nstate)

    @pl.when(j == 0)
    def _():
        pulled[...] = jnp.zeros_like(pulled)
        gs[...] = jnp.zeros_like(gs)
        coef[...] = reads[...]

    def backward(k0, carry):
        t = steps - 1 - k0
        passed, sums = carry
        reset = beg[rows_at(16 + t * 8, 8), :]
        enter = [cscr[at(t), cut(i)] for i in range(count)]
        read = [cscr[at(t), cut(count + i)] for i in range(count)]
        new, news = [], []
        seen = [None] * count
        for d in range(groups):
            st, dt = step[d, at(t), :], dy[d, at(t), :]
            ut = st * mix[d, at(t), :]
            st = st + reset
            pull, slope_sum = None, None
            for i in range(count):
                k = d * count + i
                adj = passed[k] + read[i] * dt
                pull = adj * enter[i] if pull is None else pull + adj * enter[i]
                back = adj * jnp.exp2(st * rates[k])
                slope = back * states[0, t, k]
                slope_sum = slope * rates[k] if slope_sum is None else slope_sum + slope * rates[k]
                new.append(back)
                news.append(sums[k] + slope * st)
                term = adj * ut
                seen[i] = term if seen[i] is None else seen[i] + term
            pulled[d, at(t), :] += pull
            gs[d, at(t), :] += slope_sum
        for i in range(count):
            seen_scr[at(t), cut(i)] = seen[i]
        return tuple(new), tuple(news)

    zero = jnp.zeros((8, 128), F32)
    init = (tuple(lin[0, i, :, cut(d)] for d, i in keys), (zero,) * size)
    passed, sums = lax.fori_loop(0, steps, backward, init, unroll=SCAN_UNROLL)
    for n, (d, i) in enumerate(keys):
        line = jnp.sum(sums[n] * rates[n], axis=0, keepdims=True) * LN2
        at_ = pl.ds(j * count + i, 1)

        @pl.when(pl.program_id(0) == 0)
        def _():
            tot[d, at_, :] = line

        @pl.when(pl.program_id(0) > 0)
        def _():
            tot[d, at_, :] += line

    lane_sums(seen_scr, coef, count, rank + j * count)


def scan_backward(step, mix, dy, beg, packed, rate, lin, states, reads, rank, count):
    groups, tokens, _ = step.shape
    nstate, ch = rate.shape
    grid, groups, tok, narrow, marks, rates, state, flat, kept, kept_shape = scan_specs(tokens, ch, nstate, count)
    shape = jax.ShapeDtypeStruct
    work = tokens * nstate * ch
    return pl.pallas_call(
        functools.partial(backward_kernel, count, groups, rank, nstate),
        out_shape=(
            shape(step.shape, F32),
            shape(step.shape, F32),
            shape((tokens, 128), F32),
            shape((groups, nstate, 128), F32),
        ),
        grid=grid,
        in_specs=[tok, tok, tok, marks, narrow, rates, state, kept, narrow],
        out_specs=[tok, tok, narrow, pl.BlockSpec((groups, nstate, 128), lambda n, j: (0, 0, 0))],
        scratch_shapes=[
            pltpu.VMEM((BLOCK_TOKENS, 2 * count * 128), F32),
            pltpu.VMEM((BLOCK_TOKENS, count * 128), F32),
        ],
        compiler_params=pltpu.CompilerParams(vmem_limit_bytes=60 << 20),
        cost_estimate=pl.CostEstimate(flops=12 * work, bytes_accessed=4 * work, transcendentals=work),
        name="scan_backward",
    )(step, mix, dy, beg, packed, rate.reshape(nstate // count, count, ch), lin, states, reads)


class Stream:
    def __init__(self, wire, place, src, got_y, mid, got_z, red, fin, out):
        self.wire, self.place = wire, place
        self.src, self.got_y, self.mid, self.got_z = src, got_y, mid, got_z
        self.red, self.fin, self.out = red, fin, out

    def start(self):
        p = self.place
        self.y = self.wire.send(self.src.at[:, 1 - p.b], self.got_y, p.beside)

    def across(self):
        p = self.place
        self.y.wait_recv()
        self.mid[...] = (self.src[:, p.b].astype(F32) + self.got_y[...].astype(F32)).astype(self.mid.dtype)
        self.z = [
            self.wire.send(self.mid.at[:, lax.bitwise_xor(p.a, i)], self.got_z.at[i - 1], p.zdev(i))
            for i in range(1, p.na)
        ]

    def swap(self):
        p = self.place
        for cp in self.z:
            cp.wait_recv()
        acc = self.mid[:, p.a].astype(F32)
        for i in range(1, p.na):
            acc = acc + self.got_z[i - 1].astype(F32)
        self.red[...] = acc.astype(self.red.dtype)
        self.w = [
            self.wire.send(self.red.at[lax.bitwise_xor(p.f, i)], self.fin.at[p.f], p.fdev(i)) for i in range(1, p.nf)
        ]
        self.fin[p.f] = self.red[p.f]

    def spread(self):
        p = self.place
        for cp in self.w:
            cp.wait_recv()
        self.out[p.b, p.a] = self.fin[...]
        self.g = [(self.wire.send(self.fin, self.out.at[p.b, p.a], p.zdev(i)), i) for i in range(1, p.na)]
        self.h = [self.wire.send(self.fin, self.out.at[p.b, p.a], p.beside)]

    def forward(self):
        p = self.place
        for cp, i in self.g:
            cp.wait_recv()
            block = self.out.at[p.b, lax.bitwise_xor(p.a, i)]
            self.h.append(self.wire.send(block, block, p.beside))

    def finish(self):
        for cp in self.h:
            cp.wait_recv()


class Place:
    def __init__(self, nf, ns):
        self.f, self.s = here()
        self.nf, self.ns, self.na = nf, ns, ns // 2
        self.a, self.b = lax.div(self.s, 2), lax.rem(self.s, 2)
        self.core = lax.rem(self.f, 2)
        self.peer = (lax.bitwise_xor(self.f, 1), self.s)
        self.beside = (self.f, lax.bitwise_xor(self.s, 1))

    def fdev(self, i):
        return (lax.bitwise_xor(self.f, i), self.s)

    def zdev(self, i):
        return (self.f, lax.bitwise_xor(self.a, i) * 2 + self.b)


def small_layout(groups, rank, nstate, ns):
    select, step, decay, vectors = 0, 128, 128 + rank, 128 + rank + nstate
    group = vectors + 8
    piece = -(-group * groups // (8 * ns)) * 8
    return select, step, decay, vectors, group, piece


def post_kernel(nf, ns, nq, rd, rank, nstate, sems, *refs):
    (pulled_i, slopes_i, mix_i, step_i, dy_i, slope_i, ext_i, beg_i, normed_i, wi_i, wg_i, dgate_i) = refs[:12]
    (ce, proj, vecs, w_sel, w_step, table, x, ct, decay) = refs[12:21]
    gates = refs[21 : 21 + nq]
    refs = refs[21 + nq :]
    rout, gain_out, small_out = refs[:3]
    outs = refs[3 : 3 + 2 * nq]
    refs = refs[3 + 2 * nq :]
    (pulled, slopes, mix, step, dy, slope, ext, beg, normed, wi, wg, dgate) = refs[:12]
    (mixb, dlin, dproj, dib, part, got, mid, far, sums) = refs[12:21]
    dconv, dp = mix, normed
    (near_d, mid_d, far_d, gain_l, gain_f, gain_m, gain_y, gain_n, gain_z, small, small_y, small_m, small_z) = refs[21:34]
    (edge_o, edge_i) = refs[34:36]
    refs = refs[36:]
    inners = refs[:nq]
    refs = refs[nq:]
    bufs = [refs[n * 2 * nq : (n + 1) * 2 * nq] for n in range(5)]
    ssem, rsem, lsem, esem = refs[10 * nq :]

    place = Place(nf, ns)
    f, s, a, b, core = place.f, place.s, place.a, place.b, place.core
    na = place.na
    chips = list(range(2, nf, 2))
    groups, tokens, _ = pulled.shape
    ch = groups * 128
    stretch = tokens // (nf * rd)
    half = stretch // 2
    span_t = half * 8
    blocks = tokens // span_t
    width = normed.shape[1]
    off_select, off_step, off_decay, off_vec, group_rows, piece = small_layout(groups, rank, nstate, ns)
    has_up, has_down = s + 1 < ns, s >= 1
    greet(
        [(None, place.fdev(i)) for i in range(1, nf)]
        + [(None, place.beside)]
        + [(None, place.zdev(i)) for i in range(1, na)]
        + [(has_up, (f, s + 1)), (has_down, (f, s - 1))]
    )
    wire = Wire(ssem, rsem)
    streams = []
    for n in range(2 * nq):
        src = gates[n] if n < nq else inners[n - nq]
        streams.append(Stream(wire, place, src, *[v[n] for v in bufs], outs[n]))
    for n in range(nq):
        streams[n].start()

    loads = []

    def load(src, dst):
        cp = pltpu.make_async_copy(src, dst, lsem.at[len(loads)])
        loads.append(cp)
        cp.start()
        return cp

    hs = tokens // 2
    other, keep = (1 - core) * hs, core * hs
    first = [(pulled_i, pulled), (slopes_i, slopes), (mix_i, mix), (step_i, step), (dy_i, dy)]
    by_half = []
    for start in (other, keep):
        rows_ = rows_at(start, hs)
        by_half.append([load(src.at[:, rows_], dst.at[:, rows_]) for src, dst in first])
    conv_in = [load(slope_i, slope), load(ext_i, ext), load(beg_i, beg.at[pl.ds(0, beg_i.shape[0])])]
    late = [load(normed_i, normed), load(wi_i, wi), load(wg_i, wg), load(dgate_i, dgate)]
    for d in range(groups):
        small[d * group_rows + off_decay : d * group_rows + off_vec, :] = decay[d]
        small[d * group_rows + off_vec : (d + 1) * group_rows, :] = jnp.zeros((8, 128), F32)
    rest = small.shape[0] - groups * group_rows
    if rest:
        small[groups * group_rows :, :] = jnp.zeros((rest, 128), F32)
    beg[beg_i.shape[0] :, :] = jnp.zeros((24, 128), F32)

    chunk = 64

    def fold(v):
        out = v[0:8]
        for q in range(1, v.shape[0] // 8):
            out = out + v[q * 8 : (q + 1) * 8]
        return out

    def add_row(d, k, v):
        at_ = slice(d * group_rows + off_vec + k, d * group_rows + off_vec + k + 1)
        small[at_, :] += jnp.sum(v, axis=0, keepdims=True)

    zero = jnp.zeros((8, 128), F32)

    def step_half(start, cps):
        for cp in cps:
            cp.wait()
        for d in range(groups):

            def one(c, carry, d=d):
                at_ = rows_at(start + c * chunk, chunk)
                pu, m, st, dv = pulled[d, at_, :], mix[d, at_, :], step[d, at_, :], dy[d, at_, :]
                tiny = st * (1.0 - st * (0.5 - st * (1.0 / 6.0 - st * (1.0 / 24.0))))
                sig = jnp.where(st < 0.03, tiny, 1.0 - jnp.exp(-st))
                dpre = (m * pu + slopes[d, at_, :] * LN2) * sig
                low_at = rows_at(start + c * chunk, chunk, 16)
                dlin[d, low_at, :] = dpre.astype(BF16)
                mixb[d, low_at, :] = m.astype(BF16)
                pulled[d, at_, :] = st * pu + dv * vecs[d, 6:7, :]
                return carry[0] + fold(dpre), carry[1] + fold(dv * m)

            bias, skip = lax.fori_loop(0, hs // chunk, one, (zero, zero))
            add_row(d, 5, bias)
            add_row(d, 6, skip)
        at_ = rows_at(start, hs)
        total = None
        for d in range(groups):
            term = times_transposed(dlin[d, rows_at(start, hs, 16), :], w_step[:, cut(d)])
            total = term if total is None else total + term
        part[at_, :] = ce[at_, :]
        part[at_, :rank] += total

    step_half(other, by_half[0])
    one = wire.send(part.at[rows_at(other, hs)], got, place.peer)
    step_half(keep, by_half[1])
    one.wait_recv()
    mid[...] = part[rows_at(keep, hs), :] + got[...]
    two = [wire.send(mid, far.at[n], place.fdev(i)) for n, i in enumerate(chips)]

    for d in range(groups):
        low = proj[...][:, :rank].astype(BF16)
        small[d * group_rows + off_step : d * group_rows + off_decay, :] = rows_inner(low, dlin[d])
    for n in range(nq):
        streams[n].across()

    for cp in two:
        cp.wait_recv()
    acc = mid[...]
    for n in range(len(chips)):
        acc = acc + far[n]
    sums[rows_at(keep, hs), :] = acc
    three = wire.send(sums.at[rows_at(keep, hs)], sums.at[rows_at(keep, hs)], place.peer)
    for cp in conv_in:
        cp.wait()

    def mask_at(base, k):
        out = jnp.where(beg[rows_at(base + 16, chunk), :] > 0.0, 0.0, 1.0)
        if k <= 1:
            out = jnp.where(beg[rows_at(base + 8, chunk), :] > 0.0, 0.0, out)
        if k == 0:
            out = jnp.where(beg[rows_at(base, chunk), :] > 0.0, 0.0, out)
        return out

    def conv_half(start):
        at_all = rows_at(start, hs)
        low_all = rows_at(start, hs, 16)
        dproj[low_all, :] = sums[at_all, :].astype(BF16)
        for d in range(groups):
            slopes[d, at_all, :] = jnp.dot(dproj[low_all, :], w_sel[:, cut(d)], preferred_element_type=F32)

            def one(c, carry, d=d):
                row = start + c * chunk
                n, inside = split_at(row, span_t)
                at_ = rows_at(row, chunk)
                v = (pulled[d, at_, :] + slopes[d, at_, :]) * slope[d, at_, :]
                base = n * (span_t + LEAD)
                dconv[d, rows_at(base + inside, chunk), :] = v
                bb = n * (span_t + 16) + inside
                out = [carry[0] + fold(v)]
                for k in range(4):
                    tap = ext[d, rows_at(base + inside + k * 8, chunk), :]
                    w = v * tap if k == 3 else v * tap * mask_at(bb, k)
                    out.append(carry[1 + k] + fold(w))
                return tuple(out)

            totals = lax.fori_loop(0, hs // chunk, one, (zero,) * 5)
            add_row(d, 4, totals[0])
            for k in range(4):
                add_row(d, k, totals[1 + k])

    for n in range(blocks):
        for d in range(groups):
            dconv[d, n * (span_t + LEAD) + span_t : (n + 1) * (span_t + LEAD), :] = jnp.zeros((LEAD, 128), F32)
    conv_half(keep)
    three.wait_recv()
    conv_half(other)

    sub = lax.broadcasted_iota(jnp.int32, (8, 128), 0)
    for n in range(blocks):
        base = n * (span_t + LEAD)
        bb = n * (span_t + 16)
        hit = [jnp.where(beg[bb + q * 8 : bb + q * 8 + 8, :] > 0.0, 0.0, 1.0) for q in range(5)]
        for d in range(groups):
            tail = [zero] * 3
            for q in range(3):
                v = dconv[d, base + q * 8 : base + q * 8 + 8, :]
                keepers = [hit[q + 2] * hit[q + 1] * hit[q], hit[q + 2] * hit[q + 1], hit[q + 2]]
                for k in range(3 - q):
                    tail[q + k] = tail[q + k] + vecs[d, k : k + 1, :] * (v * keepers[k])
            for q in range(3):
                edge_o[d, n * 24 + q * 8 : n * 24 + q * 8 + 8, :] = tail[q]
    edge = remote(edge_o, edge_i, esem.at[0], esem.at[1], (f, s - 1))

    @pl.when(has_down)
    def _():
        edge.start()

    for n in range(nq):
        streams[n].swap()

    per = span_t // chunk

    def inner_chunk(idx, carry):
        nd, c = split_at(idx, per)
        n, d = split_at(nd, groups)
        base = n * (span_t + LEAD) + c * chunk
        bb = n * (span_t + 16) + c * chunk
        acc = vecs[d, 3:4, :] * dconv[d, rows_at(base, chunk), :]
        for k in range(3):
            ahead = (3 - k) * 8
            acc = acc + vecs[d, k : k + 1, :] * (dconv[d, rows_at(base + ahead, chunk), :] * mask_at(bb + ahead, k))
        pulled[d, rows_at(n * span_t + c * chunk, chunk), :] = acc
        return carry

    lax.fori_loop(0, blocks * groups * per, inner_chunk, 0)

    for d in range(groups):
        small[d * group_rows + off_select : d * group_rows + off_step, :] = rows_inner(mixb[d], dproj[...])
    small_half = na * piece
    small_ys = wire.send(small.at[rows_at((1 - b) * small_half, small_half)], small_y, place.beside)
    for n in range(nq):
        streams[n].spread()

    @pl.when(has_up)
    def _():
        edge.wait_recv()

    for n in range(blocks):
        for d in range(groups):
            for q in range(3):
                at_ = slice(n * 24 + q * 8, n * 24 + q * 8 + 8)
                inward = pltpu.roll(edge_o[d, at_, :], 7, 0)
                outer = jnp.where(has_up, pltpu.roll(edge_i[d, at_, :], 1, 0), 0.0)
                row = n * span_t + (half - 3 + q) * 8
                pulled[d, row : row + 8, :] += jnp.where(sub % 2 == 0, inward, outer)

    def to_rows(idx, carry):
        r_g, i = split_at(idx, half // 32)
        r, g = split_at(r_g, 2)
        n, q = split_at(r, 4)
        at_ = rows_at(r_g * half + i * 32, 32, 16)
        for d in range(groups):
            v = pulled[d, pl.ds(n * span_t + q * 2 + g + i * 256, 32, stride=8), :]
            dib[at_, cut(d)] = v.astype(BF16)
        return carry

    lax.fori_loop(0, 2 * nf * rd * (half // 32), to_rows, 0)

    for cp in late:
        cp.wait()
    drow = width // nf
    prow = drow // ns
    lanes = max(drow, 128)
    cq = ch // nq
    for q in range(nq):

        def grad_block(k, carry, q=q):
            v = rows_inner(normed[:, pl.ds(pl.multiple_of(k * lanes, 128), lanes)], dib[:, q * cq : (q + 1) * cq])
            for m in range(lanes // drow):
                for p in range(ns):
                    r = m * drow + p * prow
                    piece_v = v[r : r + prow].astype(inners[q].dtype)
                    inners[q][k * (lanes // drow) + m, p // na, p % na] = piece_v
            return carry

        lax.fori_loop(0, width // lanes, grad_block, 0)
        streams[nq + q].start()

    span = rd * stretch

    def dn_rows(flip):
        def one(n, carry):
            who = lax.bitwise_xor(lax.bitwise_xor(f, flip), 2 * n)
            for q in range(rd):
                at_ = rows_at(who * span + q * stretch, stretch, 16)
                v = times_transposed(dib[at_, :], wi[...]) + times_transposed(dgate[at_, :], wg[...])
                dp[at_, :] = v.astype(BF16)
            return carry

        lax.fori_loop(0, nf // 2, one, 0)

    def dp_rows(who):
        return rows_at(who * span, span, 16)

    dn_rows(1)
    near = [
        wire.send(dp.at[dp_rows(lax.bitwise_xor(lax.bitwise_xor(f, 1), i))], near_d.at[n], place.peer)
        for n, i in enumerate([0] + chips)
    ]
    dn_rows(0)
    fars = []
    for n, i in reversed(list(enumerate([0] + chips))):
        near[n].wait_recv()
        if i:
            dest = lax.bitwise_xor(f, i)
            mid_d[n - 1] = (dp[dp_rows(dest), :].astype(F32) + near_d[n].astype(F32)).astype(BF16)
            fars.append(wire.send(mid_d.at[n - 1], far_d.at[n - 1], place.fdev(i)))
    for n in range(nq):
        streams[n].forward()
    small_ys.wait_recv()
    small_m[...] = small[rows_at(b * small_half, small_half), :] + small_y[...]

    def owned(who):
        return rows_at(who * piece, piece)

    small_zs = [
        wire.send(small_m.at[owned(lax.bitwise_xor(a, i))], small_z.at[i - 1], place.zdev(i)) for i in range(1, na)
    ]
    for n in range(nq, 2 * nq):
        streams[n].across()

    gain = jnp.concatenate([table[q : q + 1, :] for q in range(width // 128)], axis=1)
    for cp in fars:
        cp.wait_recv()

    def own_rows(i, total):
        at_ = rows_at(i * 16, 16, 16)
        v = x[at_, :].astype(F32)
        scale = lax.rsqrt(jnp.sum(v * v, axis=1, keepdims=True) * (1.0 / width) + EPS)
        hat = v * scale
        dn = dp[rows_at(f * span + i * 16, 16, 16), :].astype(F32) + near_d[0, at_, :].astype(F32)
        for n in range(len(chips)):
            dn = dn + far_d[n, at_, :].astype(F32)
        dh = dn * gain
        inner = jnp.sum(dh * hat, axis=1, keepdims=True) * (1.0 / width)
        rout[at_, :] = ct[at_, :].astype(F32) + scale * (dh - hat * inner)
        return total + jnp.sum(dn * hat, axis=0, keepdims=True)

    gain_l[...] = lax.fori_loop(0, x.shape[0] // 16, own_rows, jnp.zeros((1, width), F32))
    gain_a = [wire.send(gain_l, gain_f.at[i - 1], place.fdev(i)) for i in range(1, nf)]
    for cp in small_zs:
        cp.wait_recv()
    acc = small_m[owned(a), :]
    for i in range(1, na):
        acc = acc + small_z[i - 1]
    mine = rows_at(b * small_half + a * piece, piece)
    small_out[mine, :] = acc
    small_g = [(wire.send(small_out.at[mine], small_out.at[mine], place.zdev(i)), i) for i in range(1, na)]
    small_h = [wire.send(small_out.at[mine], small_out.at[mine], place.beside)]
    for n in range(nq, 2 * nq):
        streams[n].swap()
    for cp in gain_a:
        cp.wait_recv()
    acc = gain_l[...]
    for i in range(1, nf):
        acc = acc + gain_f[i - 1]
    gain_m[...] = acc
    gain_b = wire.send(gain_m, gain_y, place.beside)
    for n in range(nq, 2 * nq):
        streams[n].spread()
    for cp, i in small_g:
        cp.wait_recv()
        theirs = rows_at(b * small_half + lax.bitwise_xor(a, i) * piece, piece)
        small_h.append(wire.send(small_out.at[theirs], small_out.at[theirs], place.beside))
    gain_b.wait_recv()
    gain_n[...] = gain_m[...] + gain_y[...]
    gain_c = [wire.send(gain_n, gain_z.at[i - 1], place.zdev(i)) for i in range(1, na)]
    for n in range(nq, 2 * nq):
        streams[n].forward()
    for cp in gain_c:
        cp.wait_recv()
    acc = gain_n[...]
    for i in range(1, na):
        acc = acc + gain_z[i - 1]
    gain_out[...] = acc
    for cp in small_h:
        cp.wait_recv()
    for st in streams:
        st.finish()
    wire.drain()

    @pl.when(has_down)
    def _():
        edge.wait_send()

    assert len(wire.copies) == sems


def post(nf, ns, nq, cid, rd, rank, nstate, big, little, gates):
    shape = jax.ShapeDtypeStruct
    v = pltpu.VMEM
    pulled, ext, beg, normed, wi = big[0], big[6], big[7], big[8], big[9]
    x = little[6]
    groups, tokens, _ = pulled.shape
    ch = groups * 128
    width = normed.shape[1]
    na = ns // 2
    chips = nf // 2 - 1
    block = x.shape
    piece_shape = gates[0].shape[3:]
    piece = small_layout(groups, rank, nstate, ns)[-1]
    total = piece * ns
    hs = tokens // 2
    blocks = tokens // BLOCK_TOKENS
    stream = 1 + (na - 1) + (nf - 1) + (na - 1) + 1 + (na - 1)
    sems = 2 * nq * stream
    sems += 2 + chips
    sems += 1 + 2 * chips
    sems += 1 + (na - 1) + (na - 1) + 1 + (na - 1)
    sems += (nf - 1) + 1 + (na - 1)
    outs = [shape(block, F32), shape((1, width), F32), shape((total, 128), F32)]
    kind = gates[0].dtype
    outs += [shape((2, na, nf) + piece_shape, kind)] * (2 * nq)
    scratch = [v(m.shape, m.dtype) for m in big]
    scratch[2] = v(ext.shape, F32)
    scratch[7] = v((beg.shape[0] + 24, 128), F32)
    scratch += [
        v(pulled.shape, BF16),
        v(pulled.shape, BF16),
        v((tokens, 128), BF16),
        v((tokens, ch), BF16),
        v((tokens, 128), F32),
        v((hs, 128), F32),
        v((hs, 128), F32),
        v((chips, hs, 128), F32),
        v((tokens, 128), F32),
        v((chips + 1,) + block, BF16),
        v((chips,) + block, BF16),
        v((chips,) + block, BF16),
        v((1, width), F32),
        v((nf - 1, 1, width), F32),
        v((1, width), F32),
        v((1, width), F32),
        v((1, width), F32),
        v((na - 1, 1, width), F32),
        v((total, 128), F32),
        v((na * piece, 128), F32),
        v((na * piece, 128), F32),
        v((na - 1, piece, 128), F32),
        v((groups, blocks * 24, 128), F32),
        v((groups, blocks * 24, 128), F32),
    ]
    scratch += [v(gates[0].shape, kind)] * nq
    scratch += [v((nf, na) + piece_shape, kind)] * (2 * nq)
    scratch += [v((nf, na) + piece_shape, kind)] * (2 * nq)
    scratch += [v((na - 1, nf) + piece_shape, kind)] * (2 * nq)
    scratch += [v((nf,) + piece_shape, kind)] * (2 * nq)
    scratch += [v((nf,) + piece_shape, kind)] * (2 * nq)
    scratch += [
        pltpu.SemaphoreType.DMA((sems,)),
        pltpu.SemaphoreType.DMA((sems,)),
        pltpu.SemaphoreType.DMA((17,)),
        pltpu.SemaphoreType.DMA((2,)),
    ]
    return pl.pallas_call(
        functools.partial(post_kernel, nf, ns, nq, rd, rank, nstate, sems),
        out_shape=outs,
        in_specs=[ANY] * 12 + [VMEM] * (9 + nq),
        out_specs=[VMEM] * len(outs),
        scratch_shapes=scratch,
        compiler_params=comm_params(cid, 63 << 20),
        name="post",
    )(*big, *little, *gates)


def last_kernel(ns, nf, nq, ni, rank, nstate, nsel, nextra, *refs):
    gates, inners = refs[:nq], refs[nq : nq + ni]
    og, x, rout, small, gain = refs[nq + ni : nq + ni + 5]
    extras = refs[nq + ni + 5 : nq + ni + 5 + nextra]
    outs = refs[nq + ni + 5 + nextra :]
    layer, residual, grad_o, taps, select, step, decay, ogf, one, two, three, gain_o, grad, sem = outs
    groups = select.shape[1] // 128
    ch = groups * 128
    na = ns // 2
    prow = gates[0].shape[3]
    inner_all = nf * ch
    copies = []
    for p in range(ns):
        at_ = slice(p * prow, (p + 1) * prow)
        for parts, base in ((inners, 0), (gates, inner_all)):
            cq = ch // len(parts)
            for q, part in enumerate(parts):
                for k in range(nf):
                    start = base + k * ch + q * cq
                    grad[at_, start : start + cq] = part[p // na, p % na, k].astype(F32)
        if prow % 8 == 0:
            copies.append(pltpu.make_async_copy(grad.at[at_], grad_o.at[at_], sem.at[p]))
            copies[-1].start()
    if prow % 8:
        copies.append(pltpu.make_async_copy(grad, grad_o, sem.at[0]))
        copies[-1].start()
    ogf[...] = og[...].astype(F32)
    residual[...] = rout[...]
    total = x[...].astype(F32)
    for e in extras:
        total = total + e[...].astype(F32)
    layer[...] = total.astype(BF16)
    off_select, off_step, off_decay, off_vec, group_rows, _ = small_layout(groups, rank, nstate, ns)
    for d in range(groups):
        base = d * group_rows
        select[:, cut(d)] = jnp.transpose(small[base + off_select : base + off_step, :])[:nsel]
        step[:, cut(d)] = small[base + off_step : base + off_decay, :].astype(F32)
        decay[:, cut(d)] = small[base + off_decay : base + off_vec, :].astype(F32)
        line = small[base + off_vec : base + group_rows, :].astype(F32)
        for row_, out in ((4, one), (5, two), (6, three)):
            out[:, cut(d)] = line[row_ : row_ + 1]
        taps[:, cut(d)] = line[:4]
    width = gain_o.shape[1]
    if width % 128 == 0:
        f, _ = here()
        gain_o[...] = gain[:, pl.ds(pl.multiple_of(f * width, 128), width)]
    else:
        gain_o[...] = gain[:, :width]
    for cp in copies:
        cp.wait()


def last(nf, ns, rank, nstate, nsel, gates, inners, og, x, rout, small, gain, extras):
    shape = jax.ShapeDtypeStruct
    nq, ni = len(gates), len(inners)
    ch = og.shape[0]
    drow = gates[0].shape[3] * ns
    return pl.pallas_call(
        functools.partial(last_kernel, ns, nf, nq, ni, rank, nstate, nsel, len(extras)),
        out_shape=(
            shape(x.shape, BF16),
            shape(rout.shape, F32),
            shape((drow, 2 * nf * ch), F32),
            shape((4, ch), F32),
            shape((nsel, ch), F32),
            shape((rank, ch), F32),
            shape((nstate, ch), F32),
            shape(og.shape, F32),
            shape((1, ch), F32),
            shape((1, ch), F32),
            shape((1, ch), F32),
            shape((1, gain.shape[1] // nf), F32),
        ),
        in_specs=[VMEM] * (nq + ni + 5 + len(extras)),
        out_specs=[VMEM, VMEM, ANY] + [VMEM] * 9,
        scratch_shapes=[pltpu.VMEM((drow, 2 * nf * ch), F32), pltpu.SemaphoreType.DMA((ns,))],
        compiler_params=pltpu.CompilerParams(vmem_limit_bytes=56 << 20),
        name="last",
    )(*gates, *inners, og, x, rout, small, gain, *extras)


def rows_inner(left, right):
    return lax.dot_general(left, right, (((0,), (0,)), ((), ())), preferred_element_type=F32)


def times_transposed(left, right):
    return lax.dot_general(left, right, (((1,), (1,)), ((), ())), preferred_element_type=F32)


def silu_slope(value):
    sig = jax.nn.sigmoid(value)
    return sig * (1.0 + value * (1.0 - sig))


def shards(
    nf,
    ns,
    residual,
    out_cotangent,
    doc_lengths,
    norm_gain,
    input_proj,
    conv_kernel,
    conv_bias,
    select_proj,
    step_proj,
    step_bias,
    log_decay,
    skip_gain,
    output_proj,
):
    rd, stretch, width = residual.shape
    rows = nf * rd
    docs = doc_lengths.shape[1]
    ch = conv_bias.shape[0]
    rank = step_proj.shape[0]
    nstate = log_decay.shape[0]
    taps = conv_kernel.shape[0]
    edge = taps - 1
    tokens = rows * stretch
    half = stretch // 2
    blocks = rows // 4
    f, s = here()
    reach = -(-(stretch * ns // 2 - 1) // stretch)
    count = 4

    groups = ch // 128
    grows = norm_gain.shape[0]
    spot = lax.broadcasted_iota(jnp.int32, (width,), 0) // grows == f
    small = jnp.where(spot, jnp.tile(norm_gain.astype(F32), nf), 0.0).reshape(width // 128, 128)
    marks = jnp.pad(doc_lengths.astype(F32), ((0, 8 - rd), (0, 128 - docs)))
    small = jnp.concatenate([small, marks], axis=0)
    vecs = jnp.concatenate(
        [conv_kernel, conv_bias[None], step_bias[None], skip_gain[None], jnp.zeros((1, ch), BF16)], axis=0
    ).astype(F32)
    vecs = jnp.moveaxis(vecs.reshape(8, groups, 128), 1, 0)
    w_sel = jnp.pad(select_proj.T, ((0, 128 - select_proj.shape[1]), (0, 0)))
    normed, cot, ext, slope, mix, dy, ga, dgs, step, beg, proj, packed, w_inner, w_gate, gain = front(
        nf, ns, residual, out_cotangent, input_proj, small, vecs, w_sel, step_proj, output_proj, rank, nstate
    )
    rate = -jnp.exp(log_decay.astype(F32))
    rate2 = rate * LOG2E

    rates = jnp.moveaxis(rate2.reshape(nstate, groups, 128), 1, 0)
    gated, d_gate, states, coef_read, lin = middle(
        nf, ns, 2, reach, step, mix, dy, beg, packed, rates, vecs, ga, dgs, rank, count
    )
    nq = 2 if ch % 256 == 0 else 1
    cq = ch // nq
    piece_rows = width // nf // ns
    kind = BF16
    output_grad = rows_inner(gated, cot).astype(BF16)
    out_part = jnp.dot(gated, output_proj, preferred_element_type=F32).astype(BF16)
    gate_grads = [
        rows_inner(normed, d_gate[:, q * cq : (q + 1) * cq]).astype(kind).reshape(nf, 2, ns // 2, piece_rows, cq)
        for q in range(nq)
    ]
    output_grad, out_part, lin, *gate_grads = lax.optimization_barrier((output_grad, out_part, lin, *gate_grads))
    output_grad = lax.psum(output_grad, "seq")
    out_sum = lax.psum_scatter(out_part, "fsdp", scatter_dimension=0, tiled=True)

    pulled, slopes, coefs, decay = scan_backward(step, mix, dy, beg, packed, rate2, lin, states, coef_read, rank, count)
    big = (pulled, slopes, mix, step, dy, slope, ext, beg, normed, w_inner, w_gate, d_gate)
    little = (
        coefs,
        proj,
        vecs,
        w_sel,
        step_proj,
        gain,
        residual.reshape(rd * stretch, width),
        out_cotangent.reshape(rd * stretch, width),
        decay,
    )
    residual_grad, gain_sum, small_sum, *sums = post(nf, ns, nq, 3, rd, rank, nstate, big, little, gate_grads)
    (layer_output, residual_grad, input_grad, kernel_grad, select_grad, step_grad, decay_grad, output_grad, *vectors) = last(
        nf,
        ns,
        rank,
        nstate,
        select_proj.shape[1],
        sums[:nq],
        sums[nq:],
        output_grad,
        residual.reshape(rd * stretch, width),
        residual_grad,
        small_sum,
        gain_sum,
        [out_sum],
    )
    return (
        layer_output.reshape(rd, stretch, width),
        residual_grad.reshape(rd, stretch, width),
        vectors[3][0] if grows % 128 == 0 else lax.dynamic_slice(gain_sum[0], (f * grows,), (grows,)),
        input_grad,
        kernel_grad,
        vectors[0][0],
        select_grad.T,
        step_grad,
        vectors[1][0],
        decay_grad,
        vectors[2][0],
        output_grad,
    )


def solution(mesh):
    nf, ns = mesh.shape["fsdp"], mesh.shape["seq"]
    in_specs = (
        P("fsdp", "seq", None),
        P("fsdp", "seq", None),
        P("fsdp", None),
        P("fsdp"),
        P("fsdp", None),
        P(None, "fsdp"),
        P("fsdp"),
        P("fsdp", None),
        P(None, "fsdp"),
        P("fsdp"),
        P(None, "fsdp"),
        P("fsdp"),
        P("fsdp", None),
    )
    out_specs = (
        P("fsdp", "seq", None),
        P("fsdp", "seq", None),
        P("fsdp"),
        P("fsdp", None),
        P(None, "fsdp"),
        P("fsdp"),
        P("fsdp", None),
        P(None, "fsdp"),
        P("fsdp"),
        P(None, "fsdp"),
        P("fsdp"),
        P("fsdp", None),
    )
    return jax.shard_map(
        functools.partial(shards, nf, ns), mesh=mesh, in_specs=in_specs, out_specs=out_specs, check_vma=False
    )
```

```python
import functools
import math

import jax
import jax.numpy as jnp
from jax import lax
from jax.experimental import pallas as pl
from jax.experimental.pallas import tpu as pltpu
from jax.sharding import PartitionSpec as P

EPS = 1e-05
MESH = pl.DeviceIdType.MESH
LOG2E = math.log2(math.e)
LN2 = math.log(2.0)
BF16 = jnp.bfloat16
F32 = jnp.float32
ANY = pl.BlockSpec(memory_space=pl.ANY)
VMEM = pl.BlockSpec(memory_space=pltpu.VMEM)
RESET = 1e30
HALO = 16
DOCS = 8


def here():
    return lax.axis_index("fsdp"), lax.axis_index("seq")


def greet(peers):
    barrier = pltpu.get_barrier_semaphore()
    count = 0
    for ok, device in peers:
        if ok is None:
            pl.semaphore_signal(barrier, inc=1, device_id=device, device_id_type=MESH)
            count = count + 1
        else:

            @pl.when(ok)
            def _():
                pl.semaphore_signal(barrier, inc=1, device_id=device, device_id_type=MESH)

            count = count + ok.astype(jnp.int32)
    pl.semaphore_wait(barrier, count)


def remote(src, dst, send, recv, device):
    return pltpu.make_async_remote_copy(
        src_ref=src, dst_ref=dst, send_sem=send, recv_sem=recv, device_id=device, device_id_type=MESH
    )


def comm_params(cid, vmem=None):
    return pltpu.CompilerParams(collective_id=cid, has_side_effects=True, vmem_limit_bytes=vmem)


class Wire:
    def __init__(self, ssem, rsem):
        self.ssem, self.rsem, self.copies, self.done = ssem, rsem, [], []

    def send(self, src, dst, device):
        k = len(self.copies)
        cp = remote(src, dst, self.ssem.at[k], self.rsem.at[k], device)
        self.copies.append(cp)
        cp.start()
        return cp

    def sent(self, cp):
        cp.wait_send()
        self.done.append(cp)

    def drain(self):
        for cp in self.copies:
            if all(cp is not other for other in self.done):
                cp.wait_send()


LEAD = 24


def rows_at(base, size, unit=8):
    return pl.ds(pl.multiple_of(base, unit), size)


def split_at(i, n):
    return lax.div(i, n), lax.rem(i, n)


def front_kernel(nf, ns, rd, rank, nstate, sems, *refs):
    (x, ct, w, sm, vecs, w_sel, w_step, w_out) = refs[:8]
    (normed_o, cg_o, ext_o, slope_o, mix_o, dy_o, ga_o, dgs_o, step_o, beg_o, proj_o, packed_o, wi_o, wg_o, gain_o) = refs[8:23]
    (xg, cg, wi, wg, sg, hal, hres, vbuf, gbuf, ext, slope, mix, mixb, dy, ga, dgs, step, beg, part, got, mid, far, proj, packed) = refs[
        23:47
    ]
    ssem, rsem, hsem, hrem, lsem, osem = refs[47:]
    f, s = here()
    core, b = lax.rem(f, 2), lax.rem(s, 2)
    stretch = x.shape[1]
    half = stretch // 2
    dmodel = xg.shape[1]
    ch = wi.shape[1]
    groups = ch // 128
    rows = nf * rd
    blocks = rows // 4
    tokens = rows * stretch
    drow = w.shape[0]
    inner_all = w.shape[1] // 2
    chips = list(range(2, nf, 2))
    peer = (lax.bitwise_xor(f, 1), s)
    beside = (f, lax.bitwise_xor(s, 1))
    up, down = s + 1, s - 1
    has_up, has_down = up < ns, down >= 0

    def fdev(i):
        return (lax.bitwise_xor(f, i), s)

    greeted = [(None, fdev(i)) for i in range(1, nf)] + [(None, beside)]
    for i in range(nf):
        greeted.append((has_up, (lax.bitwise_xor(f, i), up)))
        greeted.append((has_down, (lax.bitwise_xor(f, i), down)))
    greet(greeted)
    wire = Wire(ssem, rsem)

    def act_rows(who):
        return rows_at(who * (rd * stretch), rd * stretch, 16)

    def wcols(who, base, start, size):
        return w.at[pl.ds(start, size), pl.ds(pl.multiple_of(base + who * ch, 128), ch)]

    def wrows(who, start, size):
        return pl.ds(pl.multiple_of(who * drow + start, 16), size)

    half_rows = drow // 2
    mine = pl.multiple_of(b * half_rows, 16)

    locals_ = []

    def local(src, dst):
        cp = pltpu.make_async_copy(src, dst, lsem.at[len(locals_)])
        locals_.append(cp)
        cp.start()
        return cp

    x2 = [x.at[q] for q in range(rd)]
    smalls = [wire.send(sm, sg.at[f], fdev(i)) for i in range(1, nf)]
    own_x = [local(x2[q], xg.at[rows_at((f * rd + q) * stretch, stretch, 16)]) for q in range(rd)]
    own_s = local(sm, sg.at[f])

    def send_rows(src, dst):
        if rd == 1:
            return [wire.send(src.at[0], dst.at[act_rows(f)], fdev(i)) for i in [1] + chips]
        return [wire.send(src, dst.at[act_rows(f)], fdev(i)) for i in [1] + chips]

    def send_weight(base, dst):
        out = [wire.send(wcols(peer[0], base, 0, drow), dst.at[wrows(f, 0, drow)], peer)]
        for i in range(2, nf):
            out.append(
                wire.send(wcols(lax.bitwise_xor(f, i), base, mine, half_rows), dst.at[wrows(f, mine, half_rows)], fdev(i))
            )
        return out

    xs = send_rows(x, xg)
    wis = send_weight(0, wi)
    halos = [
        remote(
            x.at[:, pl.ds(stretch - HALO, HALO), :],
            hal.at[pl.ds(f * rd, rd)],
            hsem.at[i],
            hrem.at[i],
            (lax.bitwise_xor(f, i), up),
        )
        for i in range(nf)
    ]

    @pl.when(has_up)
    def _():
        for cp in halos:
            cp.start()

    own_wi = local(wcols(f, 0, 0, drow), wi.at[wrows(f, 0, drow)])
    cs = send_rows(ct, cg)
    wgs = send_weight(inner_all, wg)
    own_c = [local(ct.at[q], cg.at[rows_at((f * rd + q) * stretch, stretch, 16)]) for q in range(rd)]
    own_wg = local(wcols(f, inner_all, 0, drow), wg.at[wrows(f, 0, drow)])

    own_s.wait()
    for cp in smalls:
        cp.wait_recv()
    table = sg[0]
    for k in range(1, nf):
        table = table + sg[k]
    gain = jnp.concatenate([table[q : q + 1, :] for q in range(dmodel // 128)], axis=1)
    gain_o[...] = table
    sub = lax.broadcasted_iota(jnp.int32, (8, 128), 0)
    for n in range(blocks):
        lens = jnp.zeros((8, 128), F32)
        for q in range(4):
            r = n * 4 + q
            line = sg[r // rd, 8 + r % rd : 9 + r % rd, :]
            lens = jnp.where(sub // 2 == q, jnp.broadcast_to(line, (8, 128)), lens)
        starts = [jnp.zeros((8, 128), F32)]
        for j in range(DOCS - 1):
            starts.append(starts[-1] + jnp.broadcast_to(lens[:, j : j + 1], (8, 128)))
        first = (s * stretch + (sub % 2) * half).astype(F32)

        def mark(t, carry, n=n, starts=starts, first=first):
            place = first + (t - 2).astype(F32)
            hit = starts[0] == place
            for j in range(1, DOCS):
                hit = jnp.logical_or(hit, starts[j] == place)
            beg[rows_at(n * (half + 2) * 8 + t * 8, 8), :] = jnp.where(hit, RESET, 0.0)
            return carry

        lax.fori_loop(0, half + 2, mark, 0)

    def norm_rows(ref, start, size):
        def one(i, carry):
            at_ = rows_at(start + i * 32, 32, 16)
            v = ref[at_, :].astype(F32)
            scale = lax.rsqrt(jnp.sum(v * v, axis=1, keepdims=True) * (1.0 / dmodel) + EPS)
            ref[at_, :] = (v * scale * gain).astype(BF16)
            return carry

        lax.fori_loop(0, size // 32, one, 0)

    span = rd * stretch
    for cp in own_x:
        cp.wait()
    norm_rows(xg, f * span, span)
    xs[0].wait_recv()
    norm_rows(xg, peer[0] * span, span)
    xf = []
    for n, i in enumerate(chips):
        xs[1 + n].wait_recv()
        block = act_rows(lax.bitwise_xor(f, i))
        xf.append(wire.send(xg.at[block], xg.at[block], peer))
    for n, i in enumerate(chips):
        xf[n].wait_recv()
        norm_rows(xg, lax.bitwise_xor(f, i + 1) * span, span)
        wire.sent(xf[n])
        norm_rows(xg, lax.bitwise_xor(f, i) * span, span)
    wif = []
    for n, i in enumerate(range(2, nf)):
        wis[1 + n].wait_recv()
        block = wrows(lax.bitwise_xor(f, i), mine, half_rows)
        wif.append(wire.send(wi.at[block], wi.at[block], beside))

    @pl.when(has_down)
    def _():
        for cp in halos:
            cp.wait_recv()

    hal_rows = rows * HALO
    hflat = vbuf
    for r in range(rows):
        v = hal[r].astype(F32)
        scale = lax.rsqrt(jnp.sum(v * v, axis=1, keepdims=True) * (1.0 / dmodel) + EPS)
        hflat[r * HALO : (r + 1) * HALO, :] = jnp.where(s > 0, v * scale * gain, 0.0).astype(BF16)
    own_wi.wait()
    wis[0].wait_recv()
    for cp in wif:
        cp.wait_recv()
    out_copies = []

    def put(src, dst):
        cp = pltpu.make_async_copy(src, dst, osem.at[len(out_copies)])
        out_copies.append(cp)
        cp.start()

    put(xg, normed_o)
    put(beg, beg_o)
    put(wi, wi_o)

    def inner_row(r, carry):
        v = jnp.dot(xg[rows_at(r * stretch, stretch, 16), :], wi[...], preferred_element_type=F32)
        v = v.astype(BF16).astype(F32)
        n, q = split_at(r, 4)
        base = n * (half * 8 + LEAD) + LEAD + q * 2
        for g in range(2):
            for d in range(groups):
                ext[d, pl.ds(base + g, half, stride=8), :] = v[g * half : (g + 1) * half, cut(d)]
        return carry

    lax.fori_loop(0, rows, inner_row, 0)
    hv = jnp.dot(hflat[...], wi[...], preferred_element_type=F32).astype(BF16).astype(F32)
    for d in range(groups):
        hres[d] = hv[:, cut(d)]
    for n in range(blocks):
        base = n * (half * 8 + LEAD)
        for d in range(groups):
            for j in range(3):
                before = hres[d, pl.ds(n * 4 * HALO + HALO - 3 + j, 4, stride=HALO), :]
                ext[d, pl.ds(base + j * 8, 4, stride=2), :] = before
                own = ext[d, pl.ds(base + LEAD + (half - 3 + j) * 8, 4, stride=2), :]
                ext[d, pl.ds(base + j * 8 + 1, 4, stride=2), :] = own
    put(ext, ext_o)

    span_t = half * 8
    chunk = 64
    per = span_t // chunk

    def conv_chunk(idx, carry):
        nd, c = split_at(idx, per)
        n, d = split_at(nd, groups)
        base = n * (span_t + LEAD) + c * chunk
        bb = n * (span_t + 16) + c * chunk
        same2 = jnp.where(beg[rows_at(bb + 16, chunk), :] > 0.0, 0.0, 1.0)
        same1 = jnp.where(beg[rows_at(bb + 8, chunk), :] > 0.0, 0.0, same2)
        same0 = jnp.where(beg[rows_at(bb, chunk), :] > 0.0, 0.0, same1)
        tap = [ext[d, rows_at(base + k * 8, chunk), :] for k in range(4)]
        v = vecs[d, 4:5, :] + vecs[d, 0:1, :] * (tap[0] * same0)
        v = v + vecs[d, 1:2, :] * (tap[1] * same1) + vecs[d, 2:3, :] * (tap[2] * same2) + vecs[d, 3:4, :] * tap[3]
        sig = jax.nn.sigmoid(v)
        m = (v * sig).astype(BF16)
        at_ = rows_at(n * span_t + c * chunk, chunk)
        slope[d, at_, :] = sig * (1.0 + v * (1.0 - sig))
        mixb[d, rows_at(n * span_t + c * chunk, chunk, 16), :] = m
        mix[d, at_, :] = m.astype(F32)
        return carry

    lax.fori_loop(0, blocks * groups * per, conv_chunk, 0)
    put(slope, slope_o)
    put(mix, mix_o)

    hs = tokens // 2
    other = (1 - core) * hs
    keep = core * hs

    def project(start):
        total = None
        for d in range(groups):
            term = times_transposed(mixb[d, rows_at(start, hs, 16), :], w_sel[:, cut(d)])
            total = term if total is None else total + term
        part[rows_at(start, hs), :] = total

    project(other)
    one = wire.send(part.at[rows_at(other, hs)], got, peer)
    project(keep)
    one.wait_recv()
    mid[...] = part[rows_at(keep, hs), :] + got[...]
    two = [wire.send(mid, far.at[n], fdev(i)) for n, i in enumerate(chips)]

    cf = []
    for n, i in enumerate(chips):
        cs[1 + n].wait_recv()
        block = act_rows(lax.bitwise_xor(f, i))
        cf.append(wire.send(cg.at[block], cg.at[block], peer))
    wgf = []
    for n, i in enumerate(range(2, nf)):
        wgs[1 + n].wait_recv()
        block = wrows(lax.bitwise_xor(f, i), mine, half_rows)
        wgf.append(wire.send(wg.at[block], wg.at[block], beside))
    for cp in own_c + [own_wg]:
        cp.wait()
    for cp in [cs[0], wgs[0]] + cf + wgf:
        cp.wait_recv()
    put(cg, cg_o)
    put(wg, wg_o)

    def gate_row(r, carry):
        at_ = rows_at(r * stretch, stretch, 16)
        gbuf[0] = jnp.dot(xg[at_, :], wg[...], preferred_element_type=F32).astype(BF16).astype(F32)
        gbuf[1] = times_transposed(cg[at_, :], w_out[...]).astype(BF16).astype(F32)
        n, q = split_at(r, 4)
        base = n * span_t + q * 2
        for g in range(2):
            for d in range(groups):
                def some(i, carry2, g=g, d=d):
                    src = rows_at(g * half + i * 32, 32)
                    v, dg = gbuf[0, src, cut(d)], gbuf[1, src, cut(d)]
                    sig = jax.nn.sigmoid(v)
                    act = v * sig
                    dst = rows_at(r * stretch + g * half + i * 32, 32)
                    ga[dst, cut(d)] = act
                    dgs[dst, cut(d)] = dg * (sig * (1.0 + v * (1.0 - sig)))
                    dy[d, pl.ds(base + g + i * 256, 32, stride=8), :] = dg * act
                    return carry2

                lax.fori_loop(0, half // 32, some, 0)
        return carry

    lax.fori_loop(0, rows, gate_row, 0)
    put(dy, dy_o)
    put(ga, ga_o)
    put(dgs, dgs_o)

    for cp in two:
        cp.wait_recv()
    acc = mid[...]
    for n in range(len(chips)):
        acc = acc + far[n]
    proj[rows_at(keep, hs), :] = acc
    three = wire.send(proj.at[rows_at(keep, hs)], proj.at[rows_at(keep, hs)], peer)

    lane = lax.broadcasted_iota(jnp.int32, (256, 128), 1)

    def step_rows(i, carry):
        at_ = rows_at(carry + i * 256, 256)
        p = proj[at_, :]
        pre = jnp.dot(p[:, :rank].astype(BF16), w_step[...], preferred_element_type=F32)
        for d in range(groups):
            v = pre[:, cut(d)] + vecs[d, 5:6, :]
            step[d, at_, :] = jnp.maximum(v, 0.0) + jnp.log1p(jnp.exp(-jnp.abs(v)))
        top = p.astype(BF16)
        rest = p - top.astype(F32)
        second = rest.astype(BF16)
        third = (rest - second.astype(F32)).astype(BF16).astype(F32)
        width = 2 * nstate
        out = pltpu.roll(top.astype(F32), 128 - rank, 1)
        out = jnp.where(lane < width, out, pltpu.roll(second.astype(F32), (128 - rank + width) % 128, 1))
        out = jnp.where(lane < 2 * width, out, pltpu.roll(third, (128 - rank + 2 * width) % 128, 1))
        packed[rows_at(carry + i * 256, 256, 16), :] = jnp.where(lane < 3 * width, out, 0.0).astype(BF16)
        return carry

    lax.fori_loop(0, hs // 256, step_rows, keep)
    three.wait_recv()
    lax.fori_loop(0, hs // 256, step_rows, other)
    put(step, step_o)
    put(proj, proj_o)
    put(packed, packed_o)
    for cp in out_copies:
        cp.wait()
    wire.drain()

    @pl.when(has_up)
    def _():
        for cp in halos:
            cp.wait_send()

    assert len(wire.copies) == sems


def front(nf, ns, x, ct, w, sm, vecs, w_sel, w_step, w_out, rank, nstate):
    rd, stretch, width = x.shape
    drow = w.shape[0]
    ch = w_step.shape[1]
    groups = ch // 128
    rows = nf * rd
    blocks = rows // 4
    tokens = rows * stretch
    half = stretch // 2
    chips = nf // 2 - 1
    ext_rows = blocks * (half * 8 + LEAD)
    beg_rows = blocks * (half + 2) * 8
    sems = 0
    sems += nf - 1
    sems += 2 * (1 + chips)
    sems += 2 * (nf - 1)
    sems += 2 * chips + 2 * (nf - 2)
    sems += 2 + chips
    shape = jax.ShapeDtypeStruct
    wide = (groups, tokens, 128)
    out_shape = (
        shape((tokens, width), BF16),
        shape((tokens, width), BF16),
        shape((groups, ext_rows, 128), F32),
        shape(wide, F32),
        shape(wide, F32),
        shape(wide, F32),
        shape((tokens, ch), F32),
        shape((tokens, ch), F32),
        shape(wide, F32),
        shape((beg_rows, 128), F32),
        shape((tokens, 128), F32),
        shape((tokens, 128), BF16),
        shape((width, ch), BF16),
        shape((width, ch), BF16),
        shape((16, 128), F32),
    )
    v = pltpu.VMEM
    scratch = [
        v((tokens, width), BF16),
        v((tokens, width), BF16),
        v((width, ch), BF16),
        v((width, ch), BF16),
        v((nf, 16, 128), F32),
        v((rows, HALO, width), BF16),
        v((groups, rows * HALO, 128), F32),
        v((rows * HALO, width), BF16),
        v((2, stretch, ch), F32),
        v((groups, ext_rows, 128), F32),
        v(wide, F32),
        v(wide, F32),
        v(wide, BF16),
        v(wide, F32),
        v((tokens, ch), F32),
        v((tokens, ch), F32),
        v(wide, F32),
        v((beg_rows, 128), F32),
        v((tokens, 128), F32),
        v((tokens // 2, 128), F32),
        v((tokens // 2, 128), F32),
        v((chips, tokens // 2, 128), F32),
        v((tokens, 128), F32),
        v((tokens, 128), BF16),
        pltpu.SemaphoreType.DMA((sems,)),
        pltpu.SemaphoreType.DMA((sems,)),
        pltpu.SemaphoreType.DMA((nf,)),
        pltpu.SemaphoreType.DMA((nf,)),
        pltpu.SemaphoreType.DMA((2 * rd + 3,)),
        pltpu.SemaphoreType.DMA((14,)),
    ]
    return pl.pallas_call(
        functools.partial(front_kernel, nf, ns, rd, rank, nstate, sems),
        out_shape=out_shape,
        in_specs=[ANY] * 4 + [VMEM] * 4,
        out_specs=[ANY] * 14 + [VMEM],
        scratch_shapes=scratch,
        compiler_params=comm_params(0, 62 << 20),
        name="front",
    )(x, ct, w, sm, vecs, w_sel, w_step, w_out)


BLOCK_TOKENS = 1024


def at(t):
    return pl.ds(pl.multiple_of(t * 8, 8), 8)


def cut(d):
    return slice(d * 128, (d + 1) * 128)


def pieces(v, count):
    out = []
    for _ in range(count):
        top = v.astype(BF16)
        out.append(top)
        v = v - top.astype(F32)
    return out


def spread_coefs(packed, cscr, first, count, nstate):
    wide = 2 * count * 128
    source = lax.broadcasted_iota(jnp.int32, (128, wide), 0)
    block = lax.broadcasted_iota(jnp.int32, (128, wide), 1) // 128
    want = jnp.where(block < count, block, nstate - count + block) + first
    pick = jnp.where(
        jnp.logical_and(source % (2 * nstate) == want, source < 6 * nstate), 1.0, 0.0
    ).astype(BF16)
    cscr[...] = jnp.dot(packed, pick, preferred_element_type=F32)


ENDS_UNROLL = 4
SCAN_UNROLL = 4
BACK_UNROLL = 8


def scan_specs(tokens, ch, nstate, count):
    blocks = tokens // BLOCK_TOKENS
    groups = ch // 128
    steps = BLOCK_TOKENS // 8
    tok = pl.BlockSpec((groups, BLOCK_TOKENS, 128), lambda n, j: (0, n, 0))
    narrow = pl.BlockSpec((BLOCK_TOKENS, 128), lambda n, j: (n, 0))
    marks = pl.BlockSpec((BLOCK_TOKENS + 16, 128), lambda n, j: (n, 0))
    rates = pl.BlockSpec((1, count, ch), lambda n, j: (j, 0, 0))
    state = pl.BlockSpec((1, count, 8, ch), lambda n, j: (n, j, 0, 0))
    flat = pl.BlockSpec((BLOCK_TOKENS, ch), lambda n, j: (n, 0))
    grid = (blocks, nstate // count)
    kept = pl.BlockSpec((1, steps, count * groups, 8, 128), lambda n, j: (n * grid[1] + j, 0, 0, 0, 0))
    kept_shape = jax.ShapeDtypeStruct((math.prod(grid), steps, count * groups, 8, 128), F32)
    return grid, groups, tok, narrow, marks, rates, state, flat, kept, kept_shape


def rates_of(rate, keys):
    return [jnp.broadcast_to(rate[0, i : i + 1, cut(d)], (8, 128)) for d, i in keys]


def lane_sums(seen, coef, count, first):
    wide = count * 128
    block = lax.broadcasted_iota(jnp.int32, (wide, 128), 0) // 128
    column = lax.broadcasted_iota(jnp.int32, (wide, 128), 1)
    ones = jnp.where(column == block + first, 1.0, 0.0).astype(BF16)
    for part in pieces(seen[...], 2):
        coef[...] += jnp.dot(part, ones, preferred_element_type=F32)


def mid_kernel(nf, ns, reach, count, rank, nstate, *refs):
    (step, mix, dy, beg, packed, rate, vecs, ga_i, dgs_i) = refs[:9]
    (gated, dgate, states_o, coef, lin_o) = refs[9:14]
    (cscr, seen, y, keep, bsc, psc, gsc, run, b_out, g_out, b_in, g_in, t_out, t_up, t_down, ga, dgs) = refs[14:31]
    ssem, rsem, tsem, tsem2, ksem, lsem = refs[31:]
    f, s = here()
    groups = step.shape[0]
    blocks = step.shape[1] // BLOCK_TOKENS
    steps = BLOCK_TOKENS // 8
    parts = nstate // count
    keys = [(d, i) for d in range(groups) for i in range(count)]
    size = len(keys)
    sub = lax.broadcasted_iota(jnp.int32, (8, 128), 0)
    odd = sub % 2 == 1
    zero = jnp.zeros((8, 128), F32)
    slots = parts if blocks == 1 else 1

    peers = []
    for q in range(1, reach + 1):
        peers.append((s + q < ns, (f, s + q)))
        peers.append((s - q >= 0, (f, s - q)))
    greet(peers)
    loads = [pltpu.make_async_copy(ga_i, ga, lsem.at[0]), pltpu.make_async_copy(dgs_i, dgs, lsem.at[1])]
    for cp in loads:
        cp.start()

    def each_way(q, up, down):
        @pl.when(s + q < ns)
        def _():
            up()

        @pl.when(s - q >= 0)
        def _():
            down()

    def starts(cps):
        for cp in cps:
            cp.start()

    def rates(j):
        return [jnp.broadcast_to(rate[d, j * count + i : j * count + i + 1, :], (8, 128)) for d, i in keys]

    def tokens_of(n):
        return slice(n * BLOCK_TOKENS, (n + 1) * BLOCK_TOKENS)

    def row(n, t):
        return rows_at(n * BLOCK_TOKENS + t * 8, 8)

    def marks(n, t):
        return beg[rows_at(n * (BLOCK_TOKENS + 16) + 16 + t * 8, 8), :]

    def pair_up(values, side):
        out = []
        for k in range(0, len(values), 2):
            one, two = values[k], values[k + 1]
            if side:
                out.append(jnp.where(odd, one, pltpu.roll(two, 7, 0)))
            else:
                out.append(jnp.where(odd, pltpu.roll(two, 1, 0), one))
        return out

    def both_rows(v, side):
        return jnp.where(odd, v, pltpu.roll(v, 7, 0)) if side else jnp.where(odd, pltpu.roll(v, 1, 0), v)

    carries = []
    for n in range(blocks):
        for j in range(parts):
            slot = j if blocks == 1 else 0
            spread_coefs(packed[tokens_of(n), :], cscr.at[slot], j * count, count, nstate)
            rt = rates(j)

            def one(t, carry, n=n, j=j, slot=slot, rt=rt):
                bs, ps, gs, rs = carry
                nb, np_, ng, nr = [], [], [], []
                reset = marks(n, t)
                enter = [cscr[slot, at(t), cut(i)] for i in range(count)]
                read = [cscr[slot, at(t), cut(count + i)] for i in range(count)]
                for d in range(groups):
                    st, dt = step[d, row(n, t), :], dy[d, row(n, t), :]
                    ut = st * mix[d, row(n, t), :]
                    st = st + reset
                    if j == 0:
                        nr.append(rs[d] + st)
                    for i in range(count):
                        k = d * count + i
                        a = jnp.exp2(st * rt[k])
                        prod = ps[k] * a
                        nb.append(bs[k] * a + enter[i] * ut)
                        np_.append(prod)
                        ng.append(gs[k] + prod * (read[i] * dt))
                return tuple(nb), tuple(np_), tuple(ng), tuple(nr)

            init = ((zero,) * size, (zero + 1.0,) * size, (zero,) * size, (zero,) * (groups if j == 0 else 0))
            bs, ps, gs, rs = lax.fori_loop(0, steps, one, init, unroll=ENDS_UNROLL)
            if j == 0:
                for d in range(groups):
                    both = rs[d] + jnp.where(odd, pltpu.roll(rs[d], 1, 0), pltpu.roll(rs[d], 7, 0))
                    t_out[n, d] = both
                cps = []
                for q in range(1, reach + 1):
                    cps.append(remote(t_out.at[n], t_up.at[n, q - 1], tsem.at[0, n, q - 1], tsem.at[1, n, q - 1], (f, s + q)))
                    cps.append(remote(t_out.at[n], t_down.at[n, q - 1], tsem2.at[0, n, q - 1], tsem2.at[1, n, q - 1], (f, s - q)))
                    each_way(q, cps[-2].start, cps[-1].start)
                carries.append(cps)
            bd, gd = [], []
            for k in range(size):
                bsc[n, j, k], psc[n, j, k], gsc[n, j, k] = bs[k], ps[k], gs[k]
                bd.append(ps[k] * pltpu.roll(bs[k], 1, 0) + bs[k])
                gd.append(gs[k] + ps[k] * pltpu.roll(gs[k], 7, 0))
            bp, gp = pair_up(bd, True), pair_up(gd, False)
            for k in range(0, size // 2, 2):
                b_out[n, j, k * 8 : k * 8 + 16, :] = jnp.concatenate([bp[k], bp[k + 1]], axis=0).astype(BF16)
                g_out[n, j, k * 8 : k * 8 + 16, :] = jnp.concatenate([gp[k], gp[k + 1]], axis=0).astype(BF16)
            cps = []
            for q in range(1, reach + 1):
                cps.append(
                    remote(b_out.at[n, j], b_in.at[n, j, q - 1], ssem.at[0, n, j, q - 1], rsem.at[0, n, j, q - 1], (f, s + q))
                )
                cps.append(
                    remote(g_out.at[n, j], g_in.at[n, j, q - 1], ssem.at[1, n, j, q - 1], rsem.at[1, n, j, q - 1], (f, s - q))
                )
                each_way(q, cps[-2].start, cps[-1].start)
            carries.append(cps)

    for cp in loads:
        cp.wait()
    coef[...] = jnp.zeros_like(coef)
    outs = []
    order = 0
    for n in range(blocks):
        for d in range(groups):
            y[d] = mix[d, tokens_of(n), :] * vecs[d, 6:7, :]
        for j in range(parts):
            slot = j if blocks == 1 else 0
            if blocks > 1:
                spread_coefs(packed[tokens_of(n), :], cscr.at[slot], j * count, count, nstate)
            mine = [carries[n * (parts + 1) + 1 + j]] + ([carries[n * (parts + 1)]] if j == 0 else [])
            for cps in mine:
                for q in range(1, reach + 1):
                    up, down = cps[2 * q - 2], cps[2 * q - 1]

                    def ahead(up=up, down=down):
                        up.wait_send()
                        down.wait_recv()

                    def behind(up=up, down=down):
                        down.wait_send()
                        up.wait_recv()

                    each_way(q, ahead, behind)
            rt = rates(j)
            hin = [None] * size
            for k in range(0, size, 2):
                h, l = [zero, zero], [zero, zero]
                for q in range(reach - 1, -1, -1):
                    at_ = slice(k * 4, k * 4 + 8)
                    bv, gv = b_in[n, j, q, at_, :].astype(F32), g_in[n, j, q, at_, :].astype(F32)
                    for m in range(2):
                        d = keys[k + m][0]
                        nh = jnp.exp2(rt[k + m] * t_up[n, q, d]) * h[m] + both_rows(bv, m == 0)
                        nl = jnp.exp2(rt[k + m] * t_down[n, q, d]) * l[m] + both_rows(gv, m == 1)
                        h[m] = jnp.where(s - (q + 1) >= 0, nh, 0.0)
                        l[m] = jnp.where(s + (q + 1) < ns, nl, 0.0)
                for m in range(2):
                    d, i = keys[k + m]
                    pv, bv, gv = psc[n, j, k + m], bsc[n, j, k + m], gsc[n, j, k + m]
                    hin[k + m] = jnp.where(odd, pltpu.roll(pv, 1, 0) * h[m] + pltpu.roll(bv, 1, 0), h[m])
                    lin = jnp.where(odd, l[m], pltpu.roll(gv, 7, 0) + pltpu.roll(pv, 7, 0) * l[m])
                    lin_o[n, j * count + i, :, cut(d)] = lin
            kslot = order % 2
            if order >= 2:
                outs[order - 2].wait()

            def forward(t, state, n=n, slot=slot, rt=rt, kslot=kslot):
                reset = marks(n, t)
                enter = [cscr[slot, at(t), cut(i)] for i in range(count)]
                read = [cscr[slot, at(t), cut(count + i)] for i in range(count)]
                new = []
                total = [None] * count
                for d in range(groups):
                    st, dt = step[d, row(n, t), :], dy[d, row(n, t), :]
                    ut = st * mix[d, row(n, t), :]
                    st = st + reset
                    out = None
                    for i in range(count):
                        k = d * count + i
                        a = jnp.exp2(st * rt[k])
                        keep[kslot, t, k] = state[k]
                        h = state[k] * a + enter[i] * ut
                        new.append(h)
                        out = read[i] * h if out is None else out + read[i] * h
                        term = h * dt
                        total[i] = term if total[i] is None else total[i] + term
                    y[d, at(t), :] += out
                for i in range(count):
                    seen[at(t), cut(i)] = total[i]
                return tuple(new)

            lax.fori_loop(0, steps, forward, tuple(hin), unroll=SCAN_UNROLL)
            cp = pltpu.make_async_copy(keep.at[kslot], states_o.at[n * parts + j], ksem.at[order])
            cp.start()
            outs.append(cp)
            order += 1
            lane_sums(seen, coef.at[tokens_of(n)], count, rank + nstate + j * count)

        def some(idx, carry, n=n):
            where, i = split_at(idx, steps // 32)
            q, g = split_at(where, 2)
            for d in range(groups):
                v = y[d, pl.ds(q * 2 + g + i * 256, 32, stride=8), :]
                at_ = rows_at(n * BLOCK_TOKENS + where * steps + i * 32, 32, 16)
                gated[at_, cut(d)] = (v * ga[at_, cut(d)]).astype(BF16)
                dgate[at_, cut(d)] = (v * dgs[at_, cut(d)]).astype(BF16)
            return carry

        lax.fori_loop(0, 8 * (steps // 32), some, 0)
    for cp in outs[-2:]:
        cp.wait()


def middle(nf, ns, cid, reach, step, mix, dy, beg, packed, rate, vecs, ga, dgs, rank, count):
    groups, tokens, _ = step.shape
    nstate, ch = rate.shape[1], groups * 128
    blocks = tokens // BLOCK_TOKENS
    steps = BLOCK_TOKENS // 8
    parts = nstate // count
    size = count * groups
    shape = jax.ShapeDtypeStruct
    v = pltpu.VMEM
    sem = pltpu.SemaphoreType.DMA
    rows_ = size // 2 * 8
    slots = parts if blocks == 1 else 1
    return pl.pallas_call(
        functools.partial(mid_kernel, nf, ns, reach, count, rank, nstate),
        out_shape=(
            shape((tokens, ch), BF16),
            shape((tokens, ch), BF16),
            shape((blocks * parts, steps, size, 8, 128), F32),
            shape((tokens, 128), F32),
            shape((blocks, nstate, 8, ch), F32),
        ),
        in_specs=[VMEM] * 7 + [ANY] * 2,
        out_specs=[VMEM, VMEM, ANY, VMEM, VMEM],
        scratch_shapes=[
            v((slots, BLOCK_TOKENS, 2 * count * 128), F32),
            v((BLOCK_TOKENS, count * 128), F32),
            v((groups, BLOCK_TOKENS, 128), F32),
            v((2, steps, size, 8, 128), F32),
            v((blocks, parts, size, 8, 128), F32),
            v((blocks, parts, size, 8, 128), F32),
            v((blocks, parts, size, 8, 128), F32),
            v((8, 128), F32),
            v((blocks, parts, rows_, 128), BF16),
            v((blocks, parts, rows_, 128), BF16),
            v((blocks, parts, reach, rows_, 128), BF16),
            v((blocks, parts, reach, rows_, 128), BF16),
            v((blocks, groups, 8, 128), F32),
            v((blocks, reach, groups, 8, 128), F32),
            v((blocks, reach, groups, 8, 128), F32),
            v((tokens, ch), F32),
            v((tokens, ch), F32),
            sem((2, blocks, parts, reach)),
            sem((2, blocks, parts, reach)),
            sem((2, blocks, reach)),
            sem((2, blocks, reach)),
            sem((blocks * parts,)),
            sem((2,)),
        ],
        compiler_params=comm_params(cid, 63 << 20),
        name="middle",
    )(step, mix, dy, beg, packed, rate, vecs, ga, dgs)


def backward_kernel(
    count, groups, rank, nstate, step, mix, dy, beg, packed, rate, lin, states, reads, pulled, gs, coef, tot, cscr, seen_scr
):
    j = pl.program_id(1)
    steps = step.shape[1] // 8
    size = count * groups
    keys = [(d, i) for d in range(groups) for i in range(count)]
    rates = rates_of(rate, keys)
    spread_coefs(packed[...], cscr, j * count, count, nstate)

    @pl.when(j == 0)
    def _():
        pulled[...] = jnp.zeros_like(pulled)
        gs[...] = jnp.zeros_like(gs)
        coef[...] = reads[...]

    def backward(k0, carry):
        t = steps - 1 - k0
        passed, sums = carry
        reset = beg[rows_at(16 + t * 8, 8), :]
        enter = [cscr[at(t), cut(i)] for i in range(count)]
        read = [cscr[at(t), cut(count + i)] for i in range(count)]
        new, news = [], []
        seen = [None] * count
        for d in range(groups):
            st, dt = step[d, at(t), :], dy[d, at(t), :]
            ut = st * mix[d, at(t), :]
            st = st + reset
            pull, slope_sum = None, None
            for i in range(count):
                k = d * count + i
                adj = passed[k] + read[i] * dt
                pull = adj * enter[i] if pull is None else pull + adj * enter[i]
                back = adj * jnp.exp2(st * rates[k])
                slope = back * states[0, t, k]
                slope_sum = slope * rates[k] if slope_sum is None else slope_sum + slope * rates[k]
                new.append(back)
                news.append(sums[k] + slope * st)
                term = adj * ut
                seen[i] = term if seen[i] is None else seen[i] + term
            pulled[d, at(t), :] += pull
            gs[d, at(t), :] += slope_sum
        for i in range(count):
            seen_scr[at(t), cut(i)] = seen[i]
        return tuple(new), tuple(news)

    zero = jnp.zeros((8, 128), F32)
    init = (tuple(lin[0, i, :, cut(d)] for d, i in keys), (zero,) * size)
    passed, sums = lax.fori_loop(0, steps, backward, init, unroll=BACK_UNROLL)
    for n, (d, i) in enumerate(keys):
        line = jnp.sum(sums[n] * rates[n], axis=0, keepdims=True) * LN2
        at_ = pl.ds(j * count + i, 1)

        @pl.when(pl.program_id(0) == 0)
        def _():
            tot[d, at_, :] = line

        @pl.when(pl.program_id(0) > 0)
        def _():
            tot[d, at_, :] += line

    lane_sums(seen_scr, coef, count, rank + j * count)


def scan_backward(step, mix, dy, beg, packed, rate, lin, states, reads, rank, count):
    groups, tokens, _ = step.shape
    nstate, ch = rate.shape
    grid, groups, tok, narrow, marks, rates, state, flat, kept, kept_shape = scan_specs(tokens, ch, nstate, count)
    shape = jax.ShapeDtypeStruct
    work = tokens * nstate * ch
    return pl.pallas_call(
        functools.partial(backward_kernel, count, groups, rank, nstate),
        out_shape=(
            shape(step.shape, F32),
            shape(step.shape, F32),
            shape((tokens, 128), F32),
            shape((groups, nstate, 128), F32),
        ),
        grid=grid,
        in_specs=[tok, tok, tok, marks, narrow, rates, state, kept, narrow],
        out_specs=[tok, tok, narrow, pl.BlockSpec((groups, nstate, 128), lambda n, j: (0, 0, 0))],
        scratch_shapes=[
            pltpu.VMEM((BLOCK_TOKENS, 2 * count * 128), F32),
            pltpu.VMEM((BLOCK_TOKENS, count * 128), F32),
        ],
        compiler_params=pltpu.CompilerParams(vmem_limit_bytes=60 << 20),
        cost_estimate=pl.CostEstimate(flops=12 * work, bytes_accessed=4 * work, transcendentals=work),
        name="scan_backward",
    )(step, mix, dy, beg, packed, rate.reshape(nstate // count, count, ch), lin, states, reads)


class Stream:
    def __init__(self, wire, place, src, got_y, mid, got_z, red, fin, out):
        self.wire, self.place = wire, place
        self.src, self.got_y, self.mid, self.got_z = src, got_y, mid, got_z
        self.red, self.fin, self.out = red, fin, out

    def start(self):
        p = self.place
        self.y = self.wire.send(self.src.at[:, 1 - p.b], self.got_y, p.beside)

    def across(self):
        p = self.place
        self.y.wait_recv()
        self.mid[...] = (self.src[:, p.b].astype(F32) + self.got_y[...].astype(F32)).astype(self.mid.dtype)
        self.z = [
            self.wire.send(self.mid.at[:, lax.bitwise_xor(p.a, i)], self.got_z.at[i - 1], p.zdev(i))
            for i in range(1, p.na)
        ]

    def swap(self):
        p = self.place
        for cp in self.z:
            cp.wait_recv()
        acc = self.mid[:, p.a].astype(F32)
        for i in range(1, p.na):
            acc = acc + self.got_z[i - 1].astype(F32)
        self.red[...] = acc.astype(self.red.dtype)
        self.w = [
            self.wire.send(self.red.at[lax.bitwise_xor(p.f, i)], self.fin.at[p.f], p.fdev(i)) for i in range(1, p.nf)
        ]
        self.fin[p.f] = self.red[p.f]

    def spread(self):
        p = self.place
        for cp in self.w:
            cp.wait_recv()
        self.out[p.b, p.a] = self.fin[...]
        self.g = [(self.wire.send(self.fin, self.out.at[p.b, p.a], p.zdev(i)), i) for i in range(1, p.na)]
        self.h = [self.wire.send(self.fin, self.out.at[p.b, p.a], p.beside)]

    def forward(self):
        p = self.place
        for cp, i in self.g:
            cp.wait_recv()
            block = self.out.at[p.b, lax.bitwise_xor(p.a, i)]
            self.h.append(self.wire.send(block, block, p.beside))

    def finish(self):
        for cp in self.h:
            cp.wait_recv()


class Place:
    def __init__(self, nf, ns):
        self.f, self.s = here()
        self.nf, self.ns, self.na = nf, ns, ns // 2
        self.a, self.b = lax.div(self.s, 2), lax.rem(self.s, 2)
        self.core = lax.rem(self.f, 2)
        self.peer = (lax.bitwise_xor(self.f, 1), self.s)
        self.beside = (self.f, lax.bitwise_xor(self.s, 1))

    def fdev(self, i):
        return (lax.bitwise_xor(self.f, i), self.s)

    def zdev(self, i):
        return (self.f, lax.bitwise_xor(self.a, i) * 2 + self.b)


def small_layout(groups, rank, nstate, ns):
    select, step, decay, vectors = 0, 128, 128 + rank, 128 + rank + nstate
    group = vectors + 8
    piece = -(-group * groups // (8 * ns)) * 8
    return select, step, decay, vectors, group, piece


def post_kernel(nf, ns, nq, rd, rank, nstate, sems, *refs):
    (pulled_i, slopes_i, mix_i, step_i, dy_i, slope_i, ext_i, beg_i, normed_i, wi_i, wg_i, dgate_i) = refs[:12]
    (ce, proj, vecs, w_sel, w_step, table, x, ct, decay) = refs[12:21]
    gates = refs[21 : 21 + nq]
    refs = refs[21 + nq :]
    rout, gain_out, small_out = refs[:3]
    outs = refs[3 : 3 + 2 * nq]
    refs = refs[3 + 2 * nq :]
    (pulled, slopes, mix, step, dy, slope, ext, beg, normed, wi, wg, dgate) = refs[:12]
    (mixb, dlin, dproj, dib, part, got, mid, far, sums) = refs[12:21]
    dconv, dp = mix, normed
    (near_d, mid_d, far_d, gain_l, gain_f, gain_m, gain_y, gain_n, gain_z, small, small_y, small_m, small_z) = refs[21:34]
    (edge_o, edge_i) = refs[34:36]
    refs = refs[36:]
    inners = refs[:nq]
    refs = refs[nq:]
    bufs = [refs[n * 2 * nq : (n + 1) * 2 * nq] for n in range(5)]
    ssem, rsem, lsem, esem = refs[10 * nq :]

    place = Place(nf, ns)
    f, s, a, b, core = place.f, place.s, place.a, place.b, place.core
    na = place.na
    chips = list(range(2, nf, 2))
    groups, tokens, _ = pulled.shape
    ch = groups * 128
    stretch = tokens // (nf * rd)
    half = stretch // 2
    span_t = half * 8
    blocks = tokens // span_t
    width = normed.shape[1]
    off_select, off_step, off_decay, off_vec, group_rows, piece = small_layout(groups, rank, nstate, ns)
    has_up, has_down = s + 1 < ns, s >= 1
    greet(
        [(None, place.fdev(i)) for i in range(1, nf)]
        + [(None, place.beside)]
        + [(None, place.zdev(i)) for i in range(1, na)]
        + [(has_up, (f, s + 1)), (has_down, (f, s - 1))]
    )
    wire = Wire(ssem, rsem)
    streams = []
    for n in range(2 * nq):
        src = gates[n] if n < nq else inners[n - nq]
        streams.append(Stream(wire, place, src, *[v[n] for v in bufs], outs[n]))
    for n in range(nq):
        streams[n].start()

    loads = []

    def load(src, dst):
        cp = pltpu.make_async_copy(src, dst, lsem.at[len(loads)])
        loads.append(cp)
        cp.start()
        return cp

    hs = tokens // 2
    other, keep = (1 - core) * hs, core * hs
    first = [(pulled_i, pulled), (slopes_i, slopes), (mix_i, mix), (step_i, step), (dy_i, dy)]
    by_half = []
    for start in (other, keep):
        rows_ = rows_at(start, hs)
        by_half.append([load(src.at[:, rows_], dst.at[:, rows_]) for src, dst in first])
    conv_in = [load(slope_i, slope), load(ext_i, ext), load(beg_i, beg.at[pl.ds(0, beg_i.shape[0])])]
    late = [load(normed_i, normed), load(wi_i, wi), load(wg_i, wg), load(dgate_i, dgate)]
    for d in range(groups):
        small[d * group_rows + off_decay : d * group_rows + off_vec, :] = decay[d]
        small[d * group_rows + off_vec : (d + 1) * group_rows, :] = jnp.zeros((8, 128), F32)
    rest = small.shape[0] - groups * group_rows
    if rest:
        small[groups * group_rows :, :] = jnp.zeros((rest, 128), F32)
    beg[beg_i.shape[0] :, :] = jnp.zeros((24, 128), F32)

    chunk = 64

    def fold(v):
        out = v[0:8]
        for q in range(1, v.shape[0] // 8):
            out = out + v[q * 8 : (q + 1) * 8]
        return out

    def add_row(d, k, v):
        at_ = slice(d * group_rows + off_vec + k, d * group_rows + off_vec + k + 1)
        small[at_, :] += jnp.sum(v, axis=0, keepdims=True)

    zero = jnp.zeros((8, 128), F32)

    def step_half(start, cps):
        for cp in cps:
            cp.wait()
        for d in range(groups):

            def one(c, carry, d=d):
                at_ = rows_at(start + c * chunk, chunk)
                pu, m, st, dv = pulled[d, at_, :], mix[d, at_, :], step[d, at_, :], dy[d, at_, :]
                tiny = st * (1.0 - st * (0.5 - st * (1.0 / 6.0 - st * (1.0 / 24.0))))
                sig = jnp.where(st < 0.03, tiny, 1.0 - jnp.exp(-st))
                dpre = (m * pu + slopes[d, at_, :] * LN2) * sig
                low_at = rows_at(start + c * chunk, chunk, 16)
                dlin[d, low_at, :] = dpre.astype(BF16)
                mixb[d, low_at, :] = m.astype(BF16)
                pulled[d, at_, :] = st * pu + dv * vecs[d, 6:7, :]
                return carry[0] + fold(dpre), carry[1] + fold(dv * m)

            bias, skip = lax.fori_loop(0, hs // chunk, one, (zero, zero))
            add_row(d, 5, bias)
            add_row(d, 6, skip)
        at_ = rows_at(start, hs)
        total = None
        for d in range(groups):
            term = times_transposed(dlin[d, rows_at(start, hs, 16), :], w_step[:, cut(d)])
            total = term if total is None else total + term
        part[at_, :] = ce[at_, :]
        part[at_, :rank] += total

    step_half(other, by_half[0])
    one = wire.send(part.at[rows_at(other, hs)], got, place.peer)
    step_half(keep, by_half[1])
    one.wait_recv()
    mid[...] = part[rows_at(keep, hs), :] + got[...]
    two = [wire.send(mid, far.at[n], place.fdev(i)) for n, i in enumerate(chips)]

    for d in range(groups):
        low = proj[...][:, :rank].astype(BF16)
        small[d * group_rows + off_step : d * group_rows + off_decay, :] = rows_inner(low, dlin[d])
    for n in range(nq):
        streams[n].across()

    for cp in two:
        cp.wait_recv()
    acc = mid[...]
    for n in range(len(chips)):
        acc = acc + far[n]
    sums[rows_at(keep, hs), :] = acc
    three = wire.send(sums.at[rows_at(keep, hs)], sums.at[rows_at(keep, hs)], place.peer)
    for cp in conv_in:
        cp.wait()

    def mask_at(base, k):
        out = jnp.where(beg[rows_at(base + 16, chunk), :] > 0.0, 0.0, 1.0)
        if k <= 1:
            out = jnp.where(beg[rows_at(base + 8, chunk), :] > 0.0, 0.0, out)
        if k == 0:
            out = jnp.where(beg[rows_at(base, chunk), :] > 0.0, 0.0, out)
        return out

    def conv_half(start):
        at_all = rows_at(start, hs)
        low_all = rows_at(start, hs, 16)
        dproj[low_all, :] = sums[at_all, :].astype(BF16)
        for d in range(groups):
            slopes[d, at_all, :] = jnp.dot(dproj[low_all, :], w_sel[:, cut(d)], preferred_element_type=F32)

            def one(c, carry, d=d):
                row = start + c * chunk
                n, inside = split_at(row, span_t)
                at_ = rows_at(row, chunk)
                v = (pulled[d, at_, :] + slopes[d, at_, :]) * slope[d, at_, :]
                base = n * (span_t + LEAD)
                dconv[d, rows_at(base + inside, chunk), :] = v
                bb = n * (span_t + 16) + inside
                out = [carry[0] + fold(v)]
                for k in range(4):
                    tap = ext[d, rows_at(base + inside + k * 8, chunk), :]
                    w = v * tap if k == 3 else v * tap * mask_at(bb, k)
                    out.append(carry[1 + k] + fold(w))
                return tuple(out)

            totals = lax.fori_loop(0, hs // chunk, one, (zero,) * 5)
            add_row(d, 4, totals[0])
            for k in range(4):
                add_row(d, k, totals[1 + k])

    for n in range(blocks):
        for d in range(groups):
            dconv[d, n * (span_t + LEAD) + span_t : (n + 1) * (span_t + LEAD), :] = jnp.zeros((LEAD, 128), F32)
    conv_half(keep)
    three.wait_recv()
    conv_half(other)

    sub = lax.broadcasted_iota(jnp.int32, (8, 128), 0)
    for n in range(blocks):
        base = n * (span_t + LEAD)
        bb = n * (span_t + 16)
        hit = [jnp.where(beg[bb + q * 8 : bb + q * 8 + 8, :] > 0.0, 0.0, 1.0) for q in range(5)]
        for d in range(groups):
            tail = [zero] * 3
            for q in range(3):
                v = dconv[d, base + q * 8 : base + q * 8 + 8, :]
                keepers = [hit[q + 2] * hit[q + 1] * hit[q], hit[q + 2] * hit[q + 1], hit[q + 2]]
                for k in range(3 - q):
                    tail[q + k] = tail[q + k] + vecs[d, k : k + 1, :] * (v * keepers[k])
            for q in range(3):
                edge_o[d, n * 24 + q * 8 : n * 24 + q * 8 + 8, :] = tail[q]
    edge = remote(edge_o, edge_i, esem.at[0], esem.at[1], (f, s - 1))

    @pl.when(has_down)
    def _():
        edge.start()

    for n in range(nq):
        streams[n].swap()

    per = span_t // chunk

    def inner_chunk(idx, carry):
        nd, c = split_at(idx, per)
        n, d = split_at(nd, groups)
        base = n * (span_t + LEAD) + c * chunk
        bb = n * (span_t + 16) + c * chunk
        acc = vecs[d, 3:4, :] * dconv[d, rows_at(base, chunk), :]
        for k in range(3):
            ahead = (3 - k) * 8
            acc = acc + vecs[d, k : k + 1, :] * (dconv[d, rows_at(base + ahead, chunk), :] * mask_at(bb + ahead, k))
        pulled[d, rows_at(n * span_t + c * chunk, chunk), :] = acc
        return carry

    lax.fori_loop(0, blocks * groups * per, inner_chunk, 0)

    for d in range(groups):
        small[d * group_rows + off_select : d * group_rows + off_step, :] = rows_inner(mixb[d], dproj[...])
    small_half = na * piece
    small_ys = wire.send(small.at[rows_at((1 - b) * small_half, small_half)], small_y, place.beside)
    for n in range(nq):
        streams[n].spread()

    @pl.when(has_up)
    def _():
        edge.wait_recv()

    for n in range(blocks):
        for d in range(groups):
            for q in range(3):
                at_ = slice(n * 24 + q * 8, n * 24 + q * 8 + 8)
                inward = pltpu.roll(edge_o[d, at_, :], 7, 0)
                outer = jnp.where(has_up, pltpu.roll(edge_i[d, at_, :], 1, 0), 0.0)
                row = n * span_t + (half - 3 + q) * 8
                pulled[d, row : row + 8, :] += jnp.where(sub % 2 == 0, inward, outer)

    def to_rows(idx, carry):
        r_g, i = split_at(idx, half // 32)
        r, g = split_at(r_g, 2)
        n, q = split_at(r, 4)
        at_ = rows_at(r_g * half + i * 32, 32, 16)
        for d in range(groups):
            v = pulled[d, pl.ds(n * span_t + q * 2 + g + i * 256, 32, stride=8), :]
            dib[at_, cut(d)] = v.astype(BF16)
        return carry

    lax.fori_loop(0, 2 * nf * rd * (half // 32), to_rows, 0)

    for cp in late:
        cp.wait()
    drow = width // nf
    prow = drow // ns
    lanes = max(drow, 128)
    cq = ch // nq
    for q in range(nq):

        def grad_block(k, carry, q=q):
            v = rows_inner(normed[:, pl.ds(pl.multiple_of(k * lanes, 128), lanes)], dib[:, q * cq : (q + 1) * cq])
            for m in range(lanes // drow):
                for p in range(ns):
                    r = m * drow + p * prow
                    piece_v = v[r : r + prow].astype(inners[q].dtype)
                    inners[q][k * (lanes // drow) + m, p // na, p % na] = piece_v
            return carry

        lax.fori_loop(0, width // lanes, grad_block, 0)
        streams[nq + q].start()

    span = rd * stretch

    def dn_rows(flip):
        def one(n, carry):
            who = lax.bitwise_xor(lax.bitwise_xor(f, flip), 2 * n)
            for q in range(rd):
                at_ = rows_at(who * span + q * stretch, stretch, 16)
                v = times_transposed(dib[at_, :], wi[...]) + times_transposed(dgate[at_, :], wg[...])
                dp[at_, :] = v.astype(BF16)
            return carry

        lax.fori_loop(0, nf // 2, one, 0)

    def dp_rows(who):
        return rows_at(who * span, span, 16)

    dn_rows(1)
    near = [
        wire.send(dp.at[dp_rows(lax.bitwise_xor(lax.bitwise_xor(f, 1), i))], near_d.at[n], place.peer)
        for n, i in enumerate([0] + chips)
    ]
    dn_rows(0)
    fars = []
    for n, i in reversed(list(enumerate([0] + chips))):
        near[n].wait_recv()
        if i:
            dest = lax.bitwise_xor(f, i)
            mid_d[n - 1] = (dp[dp_rows(dest), :].astype(F32) + near_d[n].astype(F32)).astype(BF16)
            fars.append(wire.send(mid_d.at[n - 1], far_d.at[n - 1], place.fdev(i)))
    for n in range(nq):
        streams[n].forward()
    small_ys.wait_recv()
    small_m[...] = small[rows_at(b * small_half, small_half), :] + small_y[...]

    def owned(who):
        return rows_at(who * piece, piece)

    small_zs = [
        wire.send(small_m.at[owned(lax.bitwise_xor(a, i))], small_z.at[i - 1], place.zdev(i)) for i in range(1, na)
    ]
    for n in range(nq, 2 * nq):
        streams[n].across()

    gain = jnp.concatenate([table[q : q + 1, :] for q in range(width // 128)], axis=1)
    for cp in fars:
        cp.wait_recv()

    def own_rows(i, total):
        at_ = rows_at(i * 16, 16, 16)
        v = x[at_, :].astype(F32)
        scale = lax.rsqrt(jnp.sum(v * v, axis=1, keepdims=True) * (1.0 / width) + EPS)
        hat = v * scale
        dn = dp[rows_at(f * span + i * 16, 16, 16), :].astype(F32) + near_d[0, at_, :].astype(F32)
        for n in range(len(chips)):
            dn = dn + far_d[n, at_, :].astype(F32)
        dh = dn * gain
        inner = jnp.sum(dh * hat, axis=1, keepdims=True) * (1.0 / width)
        rout[at_, :] = ct[at_, :].astype(F32) + scale * (dh - hat * inner)
        return total + jnp.sum(dn * hat, axis=0, keepdims=True)

    gain_l[...] = lax.fori_loop(0, x.shape[0] // 16, own_rows, jnp.zeros((1, width), F32))
    gain_a = [wire.send(gain_l, gain_f.at[i - 1], place.fdev(i)) for i in range(1, nf)]
    for cp in small_zs:
        cp.wait_recv()
    acc = small_m[owned(a), :]
    for i in range(1, na):
        acc = acc + small_z[i - 1]
    mine = rows_at(b * small_half + a * piece, piece)
    small_out[mine, :] = acc
    small_g = [(wire.send(small_out.at[mine], small_out.at[mine], place.zdev(i)), i) for i in range(1, na)]
    small_h = [wire.send(small_out.at[mine], small_out.at[mine], place.beside)]
    for n in range(nq, 2 * nq):
        streams[n].swap()
    for cp in gain_a:
        cp.wait_recv()
    acc = gain_l[...]
    for i in range(1, nf):
        acc = acc + gain_f[i - 1]
    gain_m[...] = acc
    gain_b = wire.send(gain_m, gain_y, place.beside)
    for n in range(nq, 2 * nq):
        streams[n].spread()
    for cp, i in small_g:
        cp.wait_recv()
        theirs = rows_at(b * small_half + lax.bitwise_xor(a, i) * piece, piece)
        small_h.append(wire.send(small_out.at[theirs], small_out.at[theirs], place.beside))
    gain_b.wait_recv()
    gain_n[...] = gain_m[...] + gain_y[...]
    gain_c = [wire.send(gain_n, gain_z.at[i - 1], place.zdev(i)) for i in range(1, na)]
    for n in range(nq, 2 * nq):
        streams[n].forward()
    for cp in gain_c:
        cp.wait_recv()
    acc = gain_n[...]
    for i in range(1, na):
        acc = acc + gain_z[i - 1]
    gain_out[...] = acc
    for cp in small_h:
        cp.wait_recv()
    for st in streams:
        st.finish()
    wire.drain()

    @pl.when(has_down)
    def _():
        edge.wait_send()

    assert len(wire.copies) == sems


def post(nf, ns, nq, cid, rd, rank, nstate, big, little, gates):
    shape = jax.ShapeDtypeStruct
    v = pltpu.VMEM
    pulled, ext, beg, normed, wi = big[0], big[6], big[7], big[8], big[9]
    x = little[6]
    groups, tokens, _ = pulled.shape
    ch = groups * 128
    width = normed.shape[1]
    na = ns // 2
    chips = nf // 2 - 1
    block = x.shape
    piece_shape = gates[0].shape[3:]
    piece = small_layout(groups, rank, nstate, ns)[-1]
    total = piece * ns
    hs = tokens // 2
    blocks = tokens // BLOCK_TOKENS
    stream = 1 + (na - 1) + (nf - 1) + (na - 1) + 1 + (na - 1)
    sems = 2 * nq * stream
    sems += 2 + chips
    sems += 1 + 2 * chips
    sems += 1 + (na - 1) + (na - 1) + 1 + (na - 1)
    sems += (nf - 1) + 1 + (na - 1)
    outs = [shape(block, F32), shape((1, width), F32), shape((total, 128), F32)]
    kind = gates[0].dtype
    outs += [shape((2, na, nf) + piece_shape, kind)] * (2 * nq)
    scratch = [v(m.shape, m.dtype) for m in big]
    scratch[2] = v(ext.shape, F32)
    scratch[7] = v((beg.shape[0] + 24, 128), F32)
    scratch += [
        v(pulled.shape, BF16),
        v(pulled.shape, BF16),
        v((tokens, 128), BF16),
        v((tokens, ch), BF16),
        v((tokens, 128), F32),
        v((hs, 128), F32),
        v((hs, 128), F32),
        v((chips, hs, 128), F32),
        v((tokens, 128), F32),
        v((chips + 1,) + block, BF16),
        v((chips,) + block, BF16),
        v((chips,) + block, BF16),
        v((1, width), F32),
        v((nf - 1, 1, width), F32),
        v((1, width), F32),
        v((1, width), F32),
        v((1, width), F32),
        v((na - 1, 1, width), F32),
        v((total, 128), F32),
        v((na * piece, 128), F32),
        v((na * piece, 128), F32),
        v((na - 1, piece, 128), F32),
        v((groups, blocks * 24, 128), F32),
        v((groups, blocks * 24, 128), F32),
    ]
    scratch += [v(gates[0].shape, kind)] * nq
    scratch += [v((nf, na) + piece_shape, kind)] * (2 * nq)
    scratch += [v((nf, na) + piece_shape, kind)] * (2 * nq)
    scratch += [v((na - 1, nf) + piece_shape, kind)] * (2 * nq)
    scratch += [v((nf,) + piece_shape, kind)] * (2 * nq)
    scratch += [v((nf,) + piece_shape, kind)] * (2 * nq)
    scratch += [
        pltpu.SemaphoreType.DMA((sems,)),
        pltpu.SemaphoreType.DMA((sems,)),
        pltpu.SemaphoreType.DMA((17,)),
        pltpu.SemaphoreType.DMA((2,)),
    ]
    return pl.pallas_call(
        functools.partial(post_kernel, nf, ns, nq, rd, rank, nstate, sems),
        out_shape=outs,
        in_specs=[ANY] * 12 + [VMEM] * (9 + nq),
        out_specs=[VMEM] * len(outs),
        scratch_shapes=scratch,
        compiler_params=comm_params(cid, 63 << 20),
        name="post",
    )(*big, *little, *gates)


def last_kernel(ns, nf, nq, ni, rank, nstate, nsel, nextra, *refs):
    gates, inners = refs[:nq], refs[nq : nq + ni]
    og, x, rout, small, gain = refs[nq + ni : nq + ni + 5]
    extras = refs[nq + ni + 5 : nq + ni + 5 + nextra]
    outs = refs[nq + ni + 5 + nextra :]
    layer, residual, grad_o, taps, select, step, decay, ogf, one, two, three, gain_o, grad, sem = outs
    groups = select.shape[1] // 128
    ch = groups * 128
    na = ns // 2
    prow = gates[0].shape[3]
    inner_all = nf * ch
    copies = []
    for p in range(ns):
        at_ = slice(p * prow, (p + 1) * prow)
        for parts, base in ((inners, 0), (gates, inner_all)):
            cq = ch // len(parts)
            for q, part in enumerate(parts):
                for k in range(nf):
                    start = base + k * ch + q * cq
                    grad[at_, start : start + cq] = part[p // na, p % na, k].astype(F32)
        if prow % 8 == 0:
            copies.append(pltpu.make_async_copy(grad.at[at_], grad_o.at[at_], sem.at[p]))
            copies[-1].start()
    if prow % 8:
        copies.append(pltpu.make_async_copy(grad, grad_o, sem.at[0]))
        copies[-1].start()
    ogf[...] = og[...].astype(F32)
    residual[...] = rout[...]
    total = x[...].astype(F32)
    for e in extras:
        total = total + e[...].astype(F32)
    layer[...] = total.astype(BF16)
    off_select, off_step, off_decay, off_vec, group_rows, _ = small_layout(groups, rank, nstate, ns)
    for d in range(groups):
        base = d * group_rows
        select[:, cut(d)] = jnp.transpose(small[base + off_select : base + off_step, :])[:nsel]
        step[:, cut(d)] = small[base + off_step : base + off_decay, :].astype(F32)
        decay[:, cut(d)] = small[base + off_decay : base + off_vec, :].astype(F32)
        line = small[base + off_vec : base + group_rows, :].astype(F32)
        for row_, out in ((4, one), (5, two), (6, three)):
            out[:, cut(d)] = line[row_ : row_ + 1]
        taps[:, cut(d)] = line[:4]
    width = gain_o.shape[1]
    if width % 128 == 0:
        f, _ = here()
        gain_o[...] = gain[:, pl.ds(pl.multiple_of(f * width, 128), width)]
    else:
        gain_o[...] = gain[:, :width]
    for cp in copies:
        cp.wait()


def last(nf, ns, rank, nstate, nsel, gates, inners, og, x, rout, small, gain, extras):
    shape = jax.ShapeDtypeStruct
    nq, ni = len(gates), len(inners)
    ch = og.shape[0]
    drow = gates[0].shape[3] * ns
    return pl.pallas_call(
        functools.partial(last_kernel, ns, nf, nq, ni, rank, nstate, nsel, len(extras)),
        out_shape=(
            shape(x.shape, BF16),
            shape(rout.shape, F32),
            shape((drow, 2 * nf * ch), F32),
            shape((4, ch), F32),
            shape((nsel, ch), F32),
            shape((rank, ch), F32),
            shape((nstate, ch), F32),
            shape(og.shape, F32),
            shape((1, ch), F32),
            shape((1, ch), F32),
            shape((1, ch), F32),
            shape((1, gain.shape[1] // nf), F32),
        ),
        in_specs=[VMEM] * (nq + ni + 5 + len(extras)),
        out_specs=[VMEM, VMEM, ANY] + [VMEM] * 9,
        scratch_shapes=[pltpu.VMEM((drow, 2 * nf * ch), F32), pltpu.SemaphoreType.DMA((ns,))],
        compiler_params=pltpu.CompilerParams(vmem_limit_bytes=56 << 20),
        name="last",
    )(*gates, *inners, og, x, rout, small, gain, *extras)


def rows_inner(left, right):
    return lax.dot_general(left, right, (((0,), (0,)), ((), ())), preferred_element_type=F32)


def times_transposed(left, right):
    return lax.dot_general(left, right, (((1,), (1,)), ((), ())), preferred_element_type=F32)


def silu_slope(value):
    sig = jax.nn.sigmoid(value)
    return sig * (1.0 + value * (1.0 - sig))


def shards(
    nf,
    ns,
    residual,
    out_cotangent,
    doc_lengths,
    norm_gain,
    input_proj,
    conv_kernel,
    conv_bias,
    select_proj,
    step_proj,
    step_bias,
    log_decay,
    skip_gain,
    output_proj,
):
    rd, stretch, width = residual.shape
    rows = nf * rd
    docs = doc_lengths.shape[1]
    ch = conv_bias.shape[0]
    rank = step_proj.shape[0]
    nstate = log_decay.shape[0]
    taps = conv_kernel.shape[0]
    edge = taps - 1
    tokens = rows * stretch
    half = stretch // 2
    blocks = rows // 4
    f, s = here()
    reach = -(-(stretch * ns // 2 - 1) // stretch)
    count = 4

    groups = ch // 128
    grows = norm_gain.shape[0]
    spot = lax.broadcasted_iota(jnp.int32, (width,), 0) // grows == f
    small = jnp.where(spot, jnp.tile(norm_gain.astype(F32), nf), 0.0).reshape(width // 128, 128)
    marks = jnp.pad(doc_lengths.astype(F32), ((0, 8 - rd), (0, 128 - docs)))
    small = jnp.concatenate([small, marks], axis=0)
    vecs = jnp.concatenate(
        [conv_kernel, conv_bias[None], step_bias[None], skip_gain[None], jnp.zeros((1, ch), BF16)], axis=0
    ).astype(F32)
    vecs = jnp.moveaxis(vecs.reshape(8, groups, 128), 1, 0)
    w_sel = jnp.pad(select_proj.T, ((0, 128 - select_proj.shape[1]), (0, 0)))
    normed, cot, ext, slope, mix, dy, ga, dgs, step, beg, proj, packed, w_inner, w_gate, gain = front(
        nf, ns, residual, out_cotangent, input_proj, small, vecs, w_sel, step_proj, output_proj, rank, nstate
    )
    rate = -jnp.exp(log_decay.astype(F32))
    rate2 = rate * LOG2E

    rates = jnp.moveaxis(rate2.reshape(nstate, groups, 128), 1, 0)
    gated, d_gate, states, coef_read, lin = middle(
        nf, ns, 2, reach, step, mix, dy, beg, packed, rates, vecs, ga, dgs, rank, count
    )
    nq = 2 if ch % 256 == 0 else 1
    cq = ch // nq
    piece_rows = width // nf // ns
    kind = BF16
    output_grad = rows_inner(gated, cot).astype(BF16)
    out_part = jnp.dot(gated, output_proj, preferred_element_type=F32).astype(BF16)
    gate_grads = [
        rows_inner(normed, d_gate[:, q * cq : (q + 1) * cq]).astype(kind).reshape(nf, 2, ns // 2, piece_rows, cq)
        for q in range(nq)
    ]
    output_grad, out_part, lin, *gate_grads = lax.optimization_barrier((output_grad, out_part, lin, *gate_grads))
    output_grad = lax.psum(output_grad, "seq")
    out_sum = lax.psum_scatter(out_part, "fsdp", scatter_dimension=0, tiled=True)

    pulled, slopes, coefs, decay = scan_backward(step, mix, dy, beg, packed, rate2, lin, states, coef_read, rank, count)
    big = (pulled, slopes, mix, step, dy, slope, ext, beg, normed, w_inner, w_gate, d_gate)
    little = (
        coefs,
        proj,
        vecs,
        w_sel,
        step_proj,
        gain,
        residual.reshape(rd * stretch, width),
        out_cotangent.reshape(rd * stretch, width),
        decay,
    )
    residual_grad, gain_sum, small_sum, *sums = post(nf, ns, nq, 3, rd, rank, nstate, big, little, gate_grads)
    (layer_output, residual_grad, input_grad, kernel_grad, select_grad, step_grad, decay_grad, output_grad, *vectors) = last(
        nf,
        ns,
        rank,
        nstate,
        select_proj.shape[1],
        sums[:nq],
        sums[nq:],
        output_grad,
        residual.reshape(rd * stretch, width),
        residual_grad,
        small_sum,
        gain_sum,
        [out_sum],
    )
    return (
        layer_output.reshape(rd, stretch, width),
        residual_grad.reshape(rd, stretch, width),
        vectors[3][0] if grows % 128 == 0 else lax.dynamic_slice(gain_sum[0], (f * grows,), (grows,)),
        input_grad,
        kernel_grad,
        vectors[0][0],
        select_grad.T,
        step_grad,
        vectors[1][0],
        decay_grad,
        vectors[2][0],
        output_grad,
    )


def solution(mesh):
    nf, ns = mesh.shape["fsdp"], mesh.shape["seq"]
    in_specs = (
        P("fsdp", "seq", None),
        P("fsdp", "seq", None),
        P("fsdp", None),
        P("fsdp"),
        P("fsdp", None),
        P(None, "fsdp"),
        P("fsdp"),
        P("fsdp", None),
        P(None, "fsdp"),
        P("fsdp"),
        P(None, "fsdp"),
        P("fsdp"),
        P("fsdp", None),
    )
    out_specs = (
        P("fsdp", "seq", None),
        P("fsdp", "seq", None),
        P("fsdp"),
        P("fsdp", None),
        P(None, "fsdp"),
        P("fsdp"),
        P("fsdp", None),
        P(None, "fsdp"),
        P("fsdp"),
        P(None, "fsdp"),
        P("fsdp"),
        P("fsdp", None),
    )
    return jax.shard_map(
        functools.partial(shards, nf, ns), mesh=mesh, in_specs=in_specs, out_specs=out_specs, check_vma=False
    )
```
